32 devices in a mesh: dp: 4 (over x, core), blk: 4 (over z), inner: 2 (over y).
Axes of the slice: x: 2, y: 2, z: 4, core: 2. Of those that a mesh axis runs over, the one named last changes fastest.
Arguments:
- queries: bfloat16 [4, 1024, 1536], P('dp', ('blk', 'inner')), may hold values from -6 to 6
- keys: bfloat16 [4, 1024, 1536], P('dp', ('blk', 'inner')), may hold values from -6 to 6
- values: bfloat16 [4, 1024, 1536], P('dp', ('blk', 'inner')), may hold values from -6 to 6
- v_scale: bfloat16 [4, 1024, 12], P('dp', ('blk', 'inner')), may hold values from 0.5 to 2
- d_out: bfloat16 [4, 1024, 1536], P('dp', ('blk', 'inner')), may hold values from -45 to 45
- q_gain: float32 [128], replicated, may hold values from 0.1 to 1.9
- k_gain: float32 [128], replicated, may hold values from 0.1 to 1.9
- segment_ids: int32 [4, 1024], P('dp'), may hold values from 0 to 63, never falling along the last dimension, each value on 1 to 32 neighbouring positions
Outputs:
- attended: bfloat16 [4, 1024, 1536], P('dp', ('blk', 'inner'))
- d_queries: bfloat16 [4, 1024, 1536], P('dp', ('blk', 'inner'))
- d_keys: bfloat16 [4, 1024, 1536], P('dp', ('blk', 'inner'))
- d_values: bfloat16 [4, 1024, 1536], P('dp', ('blk', 'inner'))
- d_q_gain: float32 [128], replicated
- d_k_gain: float32 [128], replicated
The draws below stay inside these ranges and needn't reach their ends.
Inputs may be any that keep to these rules, and one draw needn't show every extreme that they name: `segment_ids`: segment numbers never fall along a sequence; every segment has between 1 and 32 tokens and some segment has exactly 32.
All inputs are finite; a program needn't handle non-finite values.
Results may differ from the reference program's by a relative error of at most 0.0086.
Values may be sent and summed in bfloat16 or wider, within the bound.
A program may use at most 64 MiB of HBM per device.

```python
import math
import jax
import jax.numpy as jnp
import numpy as np
from jax import lax

HEADS = 12
HD = 128
SEQS = 4
BLOCK = 256
HALO = 32
S = 1024
N_BLK = 4


def draw_d_out(key, part):
    normal_part = jnp.clip(jax.random.normal(key, (SEQS, S, HEADS * HD), jnp.float32), -5.0, 5.0)
    rise_tokens = 1.0 + 2.0 * jnp.arange(S, dtype=jnp.float32) / (S - 1)
    rise_seqs = 1.0 + 2.0 * jnp.arange(SEQS, dtype=jnp.float32) / max(SEQS - 1, 1)
    return (normal_part * rise_tokens[None, :, None] * rise_seqs[:, None, None]).astype(jnp.bfloat16)


def level_of(key, extent, split, least, largest):
    factor_of = 1.0
    for dim, blocks in split:
        draws = jax.random.uniform(jax.random.fold_in(jax.random.fold_in(key, 6), dim), (blocks,), jnp.float32, least / len(split), largest / len(split))
        factor_of = factor_of * jnp.repeat(jnp.exp(draws), extent[dim] // blocks).reshape((-1,) + (1,) * (len(extent) - 1 - dim))
    return factor_of


def split_up(number_of, total, limit, lean):
    portions = [(1 << 20) // math.isqrt(standing ** lean) + 1 for standing in range(2, number_of + 1)]
    rest, holding = total - limit - (number_of - 1), [1] * (number_of - 1)
    while rest > 0:
        candidates = [i for i in range(number_of - 1) if holding[i] < limit]
        whole, budget = sum([portions[i] for i in candidates]), rest
        for i in candidates:
            extra = min(limit - holding[i], max(1, budget * portions[i] // whole), rest)
            holding[i] = holding[i] + extra
            rest = rest - extra
    return np.array([limit] + holding)


def ragged_sizes(stream_key, amount, total, most, skew):
    if amount == 2:
        one = jax.random.randint(stream_key, (), max(1, total - most), min(most, total - 1) + 1)
        return jnp.stack([one, total - one])
    tallies = jnp.asarray(split_up(amount, total, most, skew), jnp.int32)
    twos = (amount - 1) // 2
    donor, receiver = tallies[1:1 + 2 * twos:2], tallies[2:2 + 2 * twos:2]
    margin = jnp.minimum(donor - 1, most - receiver)
    shifted = jax.random.randint(jax.random.fold_in(stream_key, 1), (twos,), 0, 1 << 20) % (margin + 1)
    tallies = tallies.at[1:1 + 2 * twos:2].set(donor - shifted).at[2:2 + 2 * twos:2].set(receiver + shifted)
    return tallies[jax.random.permutation(jax.random.fold_in(stream_key, 2), amount)]


def noise(rng, dims, scale, bound, cuts=(), kind=jnp.bfloat16):
    entries = jax.random.normal(rng, dims, jnp.float32) * scale
    if len(cuts) > 0:
        entries = level_of(rng, dims, cuts, -0.22, 0.18) * entries
    return jnp.clip(entries, min=-bound, max=bound).astype(kind)


def setup_inputs(seed: int = 0) -> dict:
    splits = jax.random.split(jax.random.key(seed), 9)
    return {
        "queries": noise(splits[0], (SEQS, S, HEADS * HD), 1.0, 6.0, ((0, 4), (1, 8))),
        "keys": noise(splits[1], (SEQS, S, HEADS * HD), 1.0, 6.0, ((0, 4), (1, 8))),
        "values": noise(splits[2], (SEQS, S, HEADS * HD), 1.0, 6.0, ((0, 4), (1, 8))),
        "v_scale": jnp.clip(jnp.exp(math.log(2.0) - 1.3862944 * jax.random.uniform(splits[3], (SEQS, S, HEADS), jnp.float32) ** level_of(splits[3], (SEQS, S, HEADS), ((0, 4), (1, 8)), -0.2, 0.2)), 0.5, 2.0).astype(jnp.bfloat16),
        "d_out": draw_d_out(jax.random.fold_in(splits[8], 71), 0),
        "q_gain": jnp.clip(1.0 + 0.18 * jax.random.normal(splits[5], (HD,), jnp.float32), 0.1, 1.9),
        "k_gain": jnp.clip(1.0 + 0.18 * jax.random.normal(splits[6], (HD,), jnp.float32), 0.1, 1.9),
        "segment_ids": jax.vmap(lambda own: jnp.searchsorted(jnp.cumsum(ragged_sizes(own, 16 * N_BLK, S, HALO, 2)), jnp.arange(S), side="right"))(jax.random.split(splits[7], SEQS)).reshape((SEQS, S)).astype(jnp.int32),
    }


EPSILON = 1e-06

def normalize(raw_values, gain_vector):
    as_float = raw_values.astype(jnp.float32)
    inverse = lax.rsqrt(lax.optimization_barrier(jnp.mean(as_float * as_float, axis=-1, keepdims=True)) + EPSILON)
    unit_rows = as_float * inverse
    return ((unit_rows * gain_vector).astype(jnp.bfloat16), unit_rows, inverse)

def norm_back(d_norm, unit_rows, inverse, gain_vector):
    d_unit = d_norm * gain_vector
    d_raw = inverse * (d_unit - unit_rows * lax.optimization_barrier(jnp.mean(d_unit * unit_rows, axis=-1, keepdims=True)))
    return (d_raw, lax.optimization_barrier(jnp.sum(d_norm * unit_rows, axis=(0, 1))))

def reference(queries, keys, values, v_scale, d_out, q_gain, k_gain, segment_ids):
    head_shape = (S, HEADS, HD)
    score_scale = 1.0 / math.sqrt(HD)

    def scores_of(q_rows, k_rows, seg_query, seg_key):
        scores = jnp.einsum('qhd,khd->hqk', q_rows.astype(jnp.float32), k_rows.astype(jnp.float32)) * score_scale
        seg_match = (seg_query[:, None] == seg_key[None, :])[None]
        return (scores, seg_match)

    def one_sequence(operands):
        q_raw, k_raw, v_raw, v_scl, grad_raw, segments = operands
        q_norm, q_unit, q_inv = normalize(q_raw.reshape(head_shape), q_gain)
        k_norm, k_unit, k_inv = normalize(k_raw.reshape(head_shape), k_gain)
        scale_f = v_scl.astype(jnp.float32)[:, :, None]
        v_deq = (v_raw.reshape(head_shape).astype(jnp.float32) * scale_f).astype(jnp.bfloat16)
        grad_out = grad_raw.reshape(head_shape)
        pad_rows = ((BLOCK, BLOCK), (0, 0), (0, 0))
        q_pad = jnp.pad(q_norm, pad_rows)
        k_pad = jnp.pad(k_norm, pad_rows)
        v_pad = jnp.pad(v_deq, pad_rows)
        grad_pad = jnp.pad(grad_out, pad_rows)
        segment_pad = jnp.pad(segments, (BLOCK, BLOCK), constant_values=-1)
        block_ids = jnp.arange(N_BLK, dtype=jnp.int32)

        def forward_block(block_index):
            row_start = (block_index * BLOCK).astype(jnp.int32)
            q_rows = lax.dynamic_slice_in_dim(q_norm, row_start, BLOCK, 0)
            seg_query = lax.dynamic_slice_in_dim(segments, row_start, BLOCK, 0)
            k_rows = lax.dynamic_slice_in_dim(k_pad, row_start, 3 * BLOCK, 0)
            v_rows = lax.dynamic_slice_in_dim(v_pad, row_start, 3 * BLOCK, 0)
            seg_key = lax.dynamic_slice_in_dim(segment_pad, row_start, 3 * BLOCK, 0)
            scores, seg_match = scores_of(q_rows, k_rows, seg_query, seg_key)
            summed = lax.optimization_barrier(jnp.sum(jnp.where(seg_match, jnp.exp(scores), 0.0), axis=2))
            log_total = jnp.log(summed)
            weights = jnp.where(seg_match, jnp.exp(scores - log_total[:, :, None]), 0.0)
            out_rows = jnp.einsum('hqk,khd->qhd', weights.astype(jnp.bfloat16).astype(jnp.float32), v_rows.astype(jnp.float32))
            return (out_rows.astype(jnp.bfloat16), log_total)
        out_blocks, total_blocks = lax.map(forward_block, block_ids)
        attended = out_blocks.reshape(head_shape)
        log_total = jnp.transpose(total_blocks, (1, 0, 2)).reshape(HEADS, S)
        out_dot = lax.optimization_barrier(jnp.sum(grad_out.astype(jnp.float32) * attended.astype(jnp.float32), axis=-1)).T
        total_pad = jnp.pad(log_total, ((0, 0), (BLOCK, BLOCK)))
        dot_pad = jnp.pad(out_dot, ((0, 0), (BLOCK, BLOCK)))

        def query_block(block_index):
            row_start = (block_index * BLOCK).astype(jnp.int32)
            q_rows = lax.dynamic_slice_in_dim(q_norm, row_start, BLOCK, 0)
            grad_rows = lax.dynamic_slice_in_dim(grad_out, row_start, BLOCK, 0)
            seg_query = lax.dynamic_slice_in_dim(segments, row_start, BLOCK, 0)
            total_rows = lax.dynamic_slice_in_dim(log_total, row_start, BLOCK, 1)
            dot_rows = lax.dynamic_slice_in_dim(out_dot, row_start, BLOCK, 1)
            k_rows = lax.dynamic_slice_in_dim(k_pad, row_start, 3 * BLOCK, 0)
            v_rows = lax.dynamic_slice_in_dim(v_pad, row_start, 3 * BLOCK, 0)
            seg_key = lax.dynamic_slice_in_dim(segment_pad, row_start, 3 * BLOCK, 0)
            scores, seg_match = scores_of(q_rows, k_rows, seg_query, seg_key)
            weights = jnp.where(seg_match, jnp.exp(scores - total_rows[:, :, None]), 0.0)
            d_weights = jnp.einsum('qhd,khd->hqk', grad_rows.astype(jnp.float32), v_rows.astype(jnp.float32))
            d_scores = (weights * (d_weights - dot_rows[:, :, None])).astype(jnp.bfloat16)
            return score_scale * jnp.einsum('hqk,khd->qhd', d_scores.astype(jnp.float32), k_rows.astype(jnp.float32))

        def key_block(block_index):
            row_start = (block_index * BLOCK).astype(jnp.int32)
            k_rows = lax.dynamic_slice_in_dim(k_norm, row_start, BLOCK, 0)
            v_rows = lax.dynamic_slice_in_dim(v_deq, row_start, BLOCK, 0)
            seg_key = lax.dynamic_slice_in_dim(segments, row_start, BLOCK, 0)
            q_rows = lax.dynamic_slice_in_dim(q_pad, row_start, 3 * BLOCK, 0)
            grad_rows = lax.dynamic_slice_in_dim(grad_pad, row_start, 3 * BLOCK, 0)
            seg_query = lax.dynamic_slice_in_dim(segment_pad, row_start, 3 * BLOCK, 0)
            total_rows = lax.dynamic_slice_in_dim(total_pad, row_start, 3 * BLOCK, 1)
            dot_rows = lax.dynamic_slice_in_dim(dot_pad, row_start, 3 * BLOCK, 1)
            scores, seg_match = scores_of(q_rows, k_rows, seg_query, seg_key)
            weights = jnp.where(seg_match, jnp.exp(scores - total_rows[:, :, None]), 0.0)
            d_weights = jnp.einsum('qhd,khd->hqk', grad_rows.astype(jnp.float32), v_rows.astype(jnp.float32))
            d_scores = (weights * (d_weights - dot_rows[:, :, None])).astype(jnp.bfloat16)
            d_key = score_scale * jnp.einsum('hqk,qhd->khd', d_scores.astype(jnp.float32), q_rows.astype(jnp.float32))
            d_val = jnp.einsum('hqk,qhd->khd', weights.astype(jnp.bfloat16).astype(jnp.float32), grad_rows.astype(jnp.float32))
            return (d_key, d_val)
        dq_norm = lax.map(query_block, block_ids).reshape(head_shape)
        dk_blocks, dv_blocks = lax.map(key_block, block_ids)
        dk_norm = dk_blocks.reshape(head_shape)
        dv_deq = dv_blocks.reshape(head_shape)
        d_q_raw, gain_q = norm_back(dq_norm, q_unit, q_inv, q_gain)
        d_k_raw, gain_k = norm_back(dk_norm, k_unit, k_inv, k_gain)
        d_val_raw = (dv_deq * scale_f).astype(jnp.bfloat16)
        flat_shape = (S, HEADS * HD)
        return (attended.reshape(flat_shape), d_q_raw.astype(jnp.bfloat16).reshape(flat_shape), d_k_raw.astype(jnp.bfloat16).reshape(flat_shape), d_val_raw.reshape(flat_shape), gain_q, gain_k)
    results = lax.map(one_sequence, (queries, keys, values, v_scale, d_out, segment_ids))
    return (results[0], results[1], results[2], results[3], lax.optimization_barrier(jnp.sum(results[4], axis=0)), lax.optimization_barrier(jnp.sum(results[5], axis=0)))
```

```python
import functools
import math

import jax
import jax.numpy as jnp
from jax import lax
from jax.experimental import pallas as pl
from jax.experimental.pallas import tpu as pltpu
from jax.sharding import PartitionSpec as P

EPSILON = 1e-06
MESH = pl.DeviceIdType.MESH
AXES = ("dp", "blk", "inner")
F32 = jnp.float32
BF16 = jnp.bfloat16
NT = (((1,), (1,)), ((), ()))
NN = (((1,), (0,)), ((), ()))
TN = (((0,), (0,)), ((), ()))
OFF = -1e30
NO_SEGMENT = -9.0


def dot(a, b, dims):
    return lax.dot_general(a, b, dims, preferred_element_type=F32)


def unit(x):
    inverse = lax.rsqrt(jnp.mean(x * x, axis=-1, keepdims=True) + EPSILON)
    return x * inverse, inverse


def norm_back(d_norm, unit_rows, inverse, gain, scale):
    along = d_norm * unit_rows
    mean = jnp.mean(along * gain, axis=-1, keepdims=True)
    return (inverse * scale) * (d_norm * gain - unit_rows * mean), along


def attend(problems, scale):
    factor = scale * math.log2(math.e)
    scores = [dot(k_norm, q_norm, NT) for q_norm, k_norm, _, _, _ in problems]
    d_ws = [dot(v, g, NT) for _, _, v, g, _ in problems]
    es = [jnp.exp2(s * factor + p[4]) for s, p in zip(scores, problems)]
    totals = [jnp.sum(e, axis=0, keepdims=True) for e in es]
    ws = [e * (1.0 / jnp.where(t == 0.0, 1.0, t)) for e, t in zip(es, totals)]
    w_bs = [w.astype(BF16) for w in ws]
    outs = [dot(w_b, p[2], TN) for w_b, p in zip(w_bs, problems)]
    d_vs = [dot(w_b, p[3], NN) for w_b, p in zip(w_bs, problems)]
    dots = [jnp.sum(w * d_w, axis=0, keepdims=True) for w, d_w in zip(ws, d_ws)]
    d_ss = [(w * (d_w - o)).astype(BF16) for w, d_w, o in zip(ws, d_ws, dots)]
    d_qs = [dot(d_s, p[1], TN) for d_s, p in zip(d_ss, problems)]
    d_ks = [dot(d_s, p[0], NN) for d_s, p in zip(d_ss, problems)]
    return list(zip(outs, d_qs, d_ks, d_vs))


def to_column(row):
    n = row.shape[1]
    r = lax.broadcasted_iota(jnp.int32, (n, n), 0)
    c = lax.broadcasted_iota(jnp.int32, (n, n), 1)
    return jnp.sum(jnp.where(r == c, row, 0.0), axis=1, keepdims=True)


def transposed(x):
    n = x.shape[1]
    r = lax.broadcasted_iota(jnp.int32, (n, n), 0)
    c = lax.broadcasted_iota(jnp.int32, (n, n), 1)
    return dot((r == c).astype(F32).astype(BF16), x, NT)


def grouped(sizes):
    groups = []
    for axis in AXES:
        if groups and groups[-1][1] * sizes[axis] <= 32:
            groups[-1] = (groups[-1][0] + (axis,), groups[-1][1] * sizes[axis])
        else:
            groups.append(((axis,), sizes[axis]))
    return groups


def rounds(sizes):
    n, found, d = sizes["blk"] * sizes["inner"], [], 1
    while d < n:
        found.append(d)
        d *= 2
    return found


def kernel(cfg, q_hbm, k_hbm, v_hbm, s_hbm, g_hbm, qg_hbm, kg_hbm, seg_hbm,
           att_o, dq_o, dk_o, dv_o, gq_o, gk_o,
           qv, kv, vv, gv, s_ref, qg_ref, kg_ref, seg_ref, s_col, near, give, take, back,
           part_k, bias_own, bias_edge, gsrc, gslot,
           load_sem, send_sem, recv_sem, back_sem, take_sem, here_sem, gsend, grecv):
    sizes, rows, heads, hd, h, hpc = cfg
    n_dp, n_blk, n_inner = (sizes[a] for a in AXES)
    nc = heads // hpc
    hh = h // 2
    width = hpc * hd
    scale = 1.0 / math.sqrt(hd)
    dp, blk, inner = (lax.axis_index(a) for a in AXES)
    p = blk * n_inner + inner
    n_line = n_blk * n_inner
    last = n_line - 1
    has_left, has_right = p > 0, p < last
    left, right = p - 1, p + 1
    first, final = inner == 0, inner == n_inner - 1
    ids = ({"blk": jnp.where(first, blk - 1, blk), "inner": jnp.where(first, n_inner - 1, inner - 1)},
           {"blk": jnp.where(final, blk + 1, blk), "inner": jnp.where(final, 0, inner + 1)})
    sides = ((0, has_left), (1, has_right))
    lo, hi = slice(0, hh), slice(rows - hh, rows)
    lo_in, hi_in = slice(hh, h), slice(rows - h, rows - hh)

    loads = [
        pltpu.make_async_copy(src, dst, load_sem.at[i])
        for i, (src, dst) in enumerate(((s_hbm, s_ref), (seg_hbm, seg_ref), (v_hbm, vv), (k_hbm, kv),
                                        (q_hbm, qv), (g_hbm, gv), (qg_hbm, qg_ref), (kg_hbm, kg_ref)))
    ]
    for c in loads:
        c.start()

    barrier = pltpu.get_barrier_semaphore()
    others = [jnp.where(dp + d >= n_dp, dp + d - n_dp, dp + d) for d in range(1, n_dp)]
    for side, there in sides:
        @pl.when(there)
        def _():
            pl.semaphore_signal(barrier, inc=1, device_id=ids[side], device_id_type=MESH)
    for other in others:
        pl.semaphore_signal(barrier, inc=1, device_id={"dp": other}, device_id_type=MESH)

    dists = rounds(sizes)

    def say_here(i):
        if i > 0:
            d = dists[i - 1]
            pl.semaphore_wait(here_sem.at[i - 1], (p >= d).astype(jnp.int32) + (p + d <= last).astype(jnp.int32))
        if i < len(dists):
            for pos, there in ((p - dists[i], p >= dists[i]), (p + dists[i], p + dists[i] <= last)):
                @pl.when(there)
                def _():
                    pl.semaphore_signal(here_sem.at[i], inc=1, device_id_type=MESH,
                                        device_id={"blk": pos // n_inner, "inner": lax.rem(pos, n_inner)})
        else:
            for other in others:
                pl.semaphore_signal(here_sem.at[i], inc=1, device_id={"dp": other}, device_id_type=MESH)

    loads[0].wait()
    s_f = transposed(s_ref[...])
    s_col[...] = s_f.astype(BF16)

    def seg_at(pos):
        start = pl.multiple_of(pos * rows, 128)
        return seg_ref[:, pl.ds(start, rows)].astype(F32)

    loads[1].wait()
    own = seg_at(p)
    prev = jnp.where(has_left, seg_at(jnp.maximum(left, 0)), -1.0)
    nxt = jnp.where(has_right, seg_at(jnp.minimum(right, last)), -2.0)

    def pick(row, index):
        return jnp.sum(row[:, index:index + 1], axis=1, keepdims=True)

    before, after = pick(prev, rows - 1), pick(nxt, 0)
    own_first, own_last = pick(own, 0), pick(own, rows - 1)
    long_lo = jnp.where(pick(own, hh) == before, 1.0, 0.0)
    long_hi = jnp.where(pick(own, rows - hh - 1) == after, 1.0, 0.0)
    short_lo = jnp.where(pick(prev, rows - hh - 1) == own_first, 1.0, 0.0)
    short_hi = jnp.where(pick(nxt, hh) == own_last, 1.0, 0.0)

    def over(x):
        return jnp.broadcast_to(x, (hh, hd)) > 0.5

    lo_is_long, hi_is_long = over(long_lo), over(long_hi)
    lo_is_short, hi_is_short = over(short_lo), over(short_hi)

    def columns(c):
        return pl.ds(pl.multiple_of(c * width, 128), width)

    def near_copy(side, c):
        cols = slice(c * width, (c + 1) * width)
        return pltpu.make_async_remote_copy(
            src_ref=give.at[side, :, :, cols],
            dst_ref=near.at[1 - side, :, :, cols],
            send_sem=send_sem.at[side],
            recv_sem=recv_sem.at[1 - side, c],
            device_id=ids[side],
            device_id_type=MESH,
        )

    def back_copy(side):
        return pltpu.make_async_remote_copy(
            src_ref=back.at[side],
            dst_ref=take.at[1 - side],
            send_sem=back_sem.at[side],
            recv_sem=take_sem.at[1 - side],
            device_id=ids[side],
            device_id_type=MESH,
        )

    def arrival(ref, send, recv, side):
        return pltpu.make_async_remote_copy(
            src_ref=ref, dst_ref=ref, send_sem=send, recv_sem=recv, device_id=ids[side], device_id_type=MESH)

    for c in loads[2:6]:
        c.wait()
    pl.semaphore_wait(barrier, has_left.astype(jnp.int32) + has_right.astype(jnp.int32) + (n_dp - 1))
    for c in range(nc):
        for head in range(c * hpc, (c + 1) * hpc):
            cols = slice(head * hd, (head + 1) * hd)
            for side, edge, inward, is_long in ((0, lo, lo_in, lo_is_long), (1, hi, hi_in, hi_is_long)):
                s_edge, s_inward = s_f[edge, head:head + 1], s_f[inward, head:head + 1]
                give[side, 0, :, cols] = kv[edge, cols]
                give[side, 1, :, cols] = (vv[edge, cols].astype(F32) * s_edge).astype(BF16)
                give[side, 2, :, cols] = jnp.where(
                    is_long, kv[inward, cols].astype(F32), qv[edge, cols].astype(F32)).astype(BF16)
                give[side, 3, :, cols] = jnp.where(
                    is_long, vv[inward, cols].astype(F32) * s_inward, gv[edge, cols].astype(F32)).astype(BF16)
        for side, there in sides:
            @pl.when(there)
            def _():
                near_copy(side, c).start()

    for side, there in sides:
        @pl.when(jnp.logical_not(there))
        def _():
            near[side] = jnp.zeros((4, hh, heads * hd), BF16)
            take[side] = jnp.zeros((2, hh, heads * hd), BF16)

    own_col, prev_col, nxt_col = to_column(own), to_column(prev), to_column(nxt)

    later = jnp.where(own == before, short_lo, 0.0) + jnp.where(own == after, short_hi, 0.0)
    own_q = jnp.where(later > 0.5, NO_SEGMENT, own)
    wide_col = jnp.concatenate([prev_col[rows - hh:], own_col, nxt_col[:hh]], axis=0)
    bias_own[...] = jnp.where(wide_col == own_q, 0.0, OFF)

    q_lo = jnp.where(short_lo > 0.5, own[:, :hh], prev[:, rows - hh:])
    q_hi = jnp.where(short_hi > 0.5, own[:, rows - hh:], nxt[:, :hh])
    q_lo = jnp.where((q_lo == before) & (own_first == before), q_lo, NO_SEGMENT)
    q_hi = jnp.where((q_hi == after) & (own_last == after), q_hi, NO_SEGMENT)
    k_lo = jnp.where(short_lo > 0.5, prev_col[rows - h:rows - hh], own_col[hh:h])
    k_hi = jnp.where(short_hi > 0.5, nxt_col[hh:h], own_col[rows - h:rows - hh])
    edge_col = jnp.concatenate(
        [k_lo, prev_col[rows - hh:], own_col[:hh], own_col[rows - hh:], nxt_col[:hh], k_hi], axis=0)
    bias_edge[...] = jnp.where(edge_col == jnp.concatenate([q_lo, q_hi], axis=1), 0.0, OFF)
    lo_adds = over(jnp.where(own_col[:hh] == before, short_lo, 0.0))
    hi_adds = over(jnp.where(own_col[rows - hh:] == after, short_hi, 0.0))

    for c in loads[6:]:
        c.wait()
    q_gain, k_gain = qg_ref[...], kg_ref[...]
    which = lax.broadcasted_iota(jnp.int32, (heads, hd), 0)

    def scale_of(head, part):
        one = jnp.where(which == head, 1.0, 0.0).astype(BF16)
        return dot(s_col[part], one, NN)

    own_k = slice(hh, hh + rows)

    def both(for_lo, for_hi, x, y):
        return jnp.concatenate([jnp.where(for_lo, x[:hh], y[:hh]), jnp.where(for_hi, x[hh:], y[hh:])], axis=0)

    def ends(x, n):
        return jnp.concatenate([x[:n], x[x.shape[0] - n:]], axis=0)

    def prepare(head):
        cols = pl.ds(pl.multiple_of(head * hd, 128), hd)
        s_all = scale_of(head, slice(0, rows))
        g = gv[:, cols]
        v_own = (vv[:, cols].astype(F32) * s_all).astype(BF16)
        v = jnp.concatenate([near[0, 1, :, cols], v_own, near[1, 1, :, cols]], axis=0)
        k = jnp.concatenate([near[0, 0, :, cols], kv[:, cols], near[1, 0, :, cols]], axis=0)
        q_unit, q_inv = unit(qv[:, cols].astype(F32))
        k_unit, k_inv = unit(k.astype(F32))
        q_norm, k_norm = (q_unit * q_gain).astype(BF16), (k_unit * k_gain).astype(BF16)
        far_0 = jnp.concatenate([near[0, 2, :, cols], near[1, 2, :, cols]], axis=0).astype(F32)
        far_1 = jnp.concatenate([near[0, 3, :, cols], near[1, 3, :, cols]], axis=0).astype(F32)
        far_0, _ = unit(far_0)
        is_short = lo_is_short, hi_is_short
        q_e = (both(*is_short, ends(q_unit, hh), far_0) * q_gain).astype(BF16)
        g_e = both(*is_short, ends(g, hh).astype(F32), far_1).astype(BF16)
        own_in = slice(h, h + hh), slice(rows - hh, rows)
        k_x = jnp.concatenate([k_unit[i] for i in own_in], axis=0)
        v_x = jnp.concatenate([v[i] for i in own_in], axis=0).astype(F32)
        k_x = (both(*is_short, far_0, k_x) * k_gain).astype(BF16)
        v_x = both(*is_short, far_1, v_x).astype(BF16)
        k_e = jnp.concatenate([k_x[:hh], k_norm[:h], k_norm[rows:], k_x[hh:]], axis=0)
        v_e = jnp.concatenate([v_x[:hh], v[:h], v[rows:], v_x[hh:]], axis=0)
        own_problem = q_norm, k_norm, v, g, bias_own[...]
        edge_problem = q_e, k_e, v_e, g_e, bias_edge[...]
        return (cols, s_all, q_unit, q_inv, k_unit, k_inv), own_problem, edge_problem

    def conclude(ready, own_result, edge_result, acc):
        acc_q, acc_k = acc
        cols, s_all, q_unit, q_inv, k_unit, k_inv = ready
        out, d_q, d_k, d_v = own_result
        out_e, d_q_e, d_k_e, d_v_e = edge_result
        back[0, 0, :, cols], back[1, 0, :, cols] = d_k[:hh].astype(BF16), d_k[rows + hh:].astype(BF16)
        back[0, 1, :, cols], back[1, 1, :, cols] = d_v[:hh].astype(BF16), d_v[rows + hh:].astype(BF16)
        to_lo, to_hi = d_k[:hh] * k_unit[:hh], d_k[rows + hh:] * k_unit[rows + hh:]
        acc_k = acc_k + jnp.sum(
            jnp.where(lo_is_long, to_lo, 0.0) + jnp.where(hi_is_long, to_hi, 0.0), axis=0, keepdims=True)

        def to_queries(x, e):
            return jnp.concatenate(
                [x[lo] + jnp.where(lo_is_short, e[:hh], 0.0), x[hh:rows - hh],
                 x[hi] + jnp.where(hi_is_short, e[hh:], 0.0)], axis=0)

        def to_keys(x, e):
            x = x[own_k]
            middle = [x[h:rows - h]] if rows > 2 * h else []
            return jnp.concatenate(
                [x[lo] + e[2 * hh:3 * hh], x[lo_in] + jnp.where(lo_is_short, 0.0, e[:hh]), *middle,
                 x[hi_in] + jnp.where(hi_is_short, 0.0, e[5 * hh:]), x[hi] + e[3 * hh:4 * hh]], axis=0)

        att_o[:, cols] = to_queries(out, out_e).astype(BF16)
        d_x, along = norm_back(to_queries(d_q, d_q_e), q_unit, q_inv, q_gain, scale)
        dq_o[:, cols] = d_x.astype(BF16)
        acc_q = acc_q + jnp.sum(along, axis=0, keepdims=True)
        d_k, d_v = to_keys(d_k, d_k_e), to_keys(d_v, d_v_e)
        part_k[0, :, cols], part_k[1, :, cols] = ends(d_k, hh), ends(d_v, hh)
        d_x, along = norm_back(d_k, k_unit[own_k], k_inv[own_k], k_gain, scale)
        acc_k = acc_k + jnp.sum(along, axis=0, keepdims=True)
        mid = slice(hh, rows - hh)
        dk_o[mid, cols] = d_x[mid].astype(BF16)
        dv_o[mid, cols] = (d_v[mid] * s_all[mid]).astype(BF16)
        return acc_q, acc_k

    def step(c, acc):
        for side, there in sides:
            @pl.when(there)
            def _():
                arrival(near.at[side, :, :, columns(c)], send_sem.at[side], recv_sem.at[side, c], side).wait_recv()
        prepared = [prepare(c * hpc + j) for j in range(hpc)]
        results = attend([x for _, a, b in prepared for x in (a, b)], scale)
        for j, (ready, _, _) in enumerate(prepared):
            acc = conclude(ready, results[2 * j], results[2 * j + 1], acc)
        for i in range(min(nc, len(dists) + 1)):
            @pl.when(c == i)
            def _():
                say_here(i)
        return acc

    zero = jnp.zeros((1, hd), F32)
    acc_q, acc_k = lax.fori_loop(0, nc, step, (zero, zero))
    for i in range(nc, len(dists) + 1):
        say_here(i)
    pl.semaphore_wait(here_sem.at[len(dists)], n_dp - 1)

    stages = grouped(sizes)
    me = {a: i for a, i in zip(AXES, (dp, blk, inner))}
    total = jnp.concatenate([acc_q, acc_k], axis=0) * scale

    def spread(stage, offset, total):
        axes, n = stages[stage]
        index = 0
        for axis in axes:
            index = index * sizes[axis] + me[axis]
        gsrc[stage] = total
        gslot[offset + index] = total
        for to in range(n):
            device, rest = {}, to
            for axis in reversed(axes):
                device[axis], rest = rest % sizes[axis], rest // sizes[axis]

            @pl.when(index != to)
            def _():
                pltpu.make_async_remote_copy(
                    src_ref=gsrc.at[stage], dst_ref=gslot.at[offset + index],
                    send_sem=gsend.at[stage], recv_sem=grecv.at[stage],
                    device_id=device, device_id_type=MESH).start()

    def gathered(stage, offset):
        axes, n = stages[stage]
        everything = gslot.at[pl.ds(offset, n - 1)]
        pltpu.make_async_remote_copy(
            src_ref=everything, dst_ref=everything,
            send_sem=gsend.at[stage], recv_sem=grecv.at[stage],
            device_id={axis: 0 for axis in axes}, device_id_type=MESH).wait()
        total = gslot[offset]
        for i in range(1, n):
            total = total + gslot[offset + i]
        return total

    spread(0, 0, total)

    for side, there in sides:
        @pl.when(there)
        def _():
            back_copy(side).start()
    for side, there in sides:
        @pl.when(there)
        def _():
            arrival(take.at[side], back_sem.at[side], take_sem.at[side], side).wait_recv()

    def last_step(c, carry):
        for j in range(hpc):
            head = c * hpc + j
            cols = pl.ds(pl.multiple_of(head * hd, 128), hd)
            k_unit, k_inv = unit(ends(kv[:, cols], hh).astype(F32))
            s_ends = jnp.concatenate([scale_of(head, lo), scale_of(head, hi)], axis=0)
            none = jnp.zeros((2 * hh, hd), F32)
            d_k, d_v = (
                part_k[i, :, cols] + both(lo_adds, hi_adds, jnp.concatenate(
                    [take[0, i, :, cols], take[1, i, :, cols]], axis=0).astype(F32), none)
                for i in range(2))
            d_k, _ = norm_back(d_k, k_unit, k_inv, k_gain, scale)
            d_k, d_v = d_k.astype(BF16), (d_v * s_ends).astype(BF16)
            dk_o[lo, cols], dk_o[hi, cols] = d_k[:hh], d_k[hh:]
            dv_o[lo, cols], dv_o[hi, cols] = d_v[:hh], d_v[hh:]
        return carry

    lax.fori_loop(0, nc, last_step, 0)

    for side, there in sides:
        @pl.when(there)
        def _():
            arrival(near.at[side], send_sem.at[side], recv_sem.at[side, 0], side).wait_send()
            arrival(take.at[side], back_sem.at[side], take_sem.at[side], side).wait_send()

    offset = 0
    for stage, (_, n) in enumerate(stages):
        if stage > 0:
            spread(stage, offset, total)
        total = gathered(stage, offset)
        offset += n
    gq_o[...] = total[0:1]
    gk_o[...] = total[1:2]


def store(*refs):
    n = len(refs) // 2
    sem = refs[-1]
    copies = [pltpu.make_async_copy(refs[i], refs[n + i], sem.at[i]) for i in range(n)]
    for x in copies:
        x.start()
    for x in copies:
        x.wait()


def local(queries, keys, values, v_scale, d_out, q_gain, k_gain, segment_ids):
    _, rows, cols = queries.shape
    hd = q_gain.shape[0]
    heads = cols // hd
    sizes = {a: lax.axis_size(a) for a in AXES}
    h = rows * sizes["inner"] // 8
    hpc = 2 if heads % 2 == 0 else 1
    nc = heads // hpc
    flat = lambda x: x.reshape(rows, x.shape[2])
    vmem = pl.BlockSpec(memory_space=pltpu.VMEM)
    hbm = pl.BlockSpec(memory_space=pltpu.HBM)
    in_hbm = lambda x: pltpu.with_memory_space_constraint(x, pltpu.HBM)
    in_vmem = lambda x: pltpu.with_memory_space_constraint(x, pltpu.VMEM)
    big = jax.ShapeDtypeStruct((rows, cols), BF16)
    small = jax.ShapeDtypeStruct((1, hd), F32)
    stages = grouped(sizes)
    outs = pl.pallas_call(
        functools.partial(kernel, (sizes, rows, heads, hd, h, hpc)),
        out_shape=(big, big, big, big, small, small),
        in_specs=[hbm] * 8,
        out_specs=(vmem,) * 6,
        scratch_shapes=[
            pltpu.VMEM((rows, cols), BF16),
            pltpu.VMEM((rows, cols), BF16),
            pltpu.VMEM((rows, cols), BF16),
            pltpu.VMEM((rows, cols), BF16),
            pltpu.VMEM((heads, rows), BF16),
            pltpu.VMEM((1, hd), F32),
            pltpu.VMEM((1, hd), F32),
            pltpu.VMEM(segment_ids.shape, jnp.int32),
            pltpu.VMEM((rows, heads), BF16),
            pltpu.VMEM((2, 4, h // 2, cols), BF16),
            pltpu.VMEM((2, 4, h // 2, cols), BF16),
            pltpu.VMEM((2, 2, h // 2, cols), BF16),
            pltpu.VMEM((2, 2, h // 2, cols), BF16),
            pltpu.VMEM((2, h, cols), F32),
            pltpu.VMEM((rows + h, rows), F32),
            pltpu.VMEM((3 * h, h), F32),
            pltpu.VMEM((len(stages), 2, hd), F32),
            pltpu.VMEM((sum(n for _, n in stages), 2, hd), F32),
            pltpu.SemaphoreType.DMA((8,)),
            pltpu.SemaphoreType.DMA((2,)),
            pltpu.SemaphoreType.DMA((2, nc)),
            pltpu.SemaphoreType.DMA((2,)),
            pltpu.SemaphoreType.DMA((2,)),
            pltpu.SemaphoreType.REGULAR((len(rounds(sizes)) + 1,)),
            pltpu.SemaphoreType.DMA((len(stages),)),
            pltpu.SemaphoreType.DMA((len(stages),)),
        ],
        compiler_params=pltpu.CompilerParams(
            collective_id=0, has_side_effects=True, vmem_limit_bytes=32 << 20),
    )(*map(in_hbm, (flat(queries), flat(keys), flat(values), flat(v_scale).T, flat(d_out),
                    q_gain.reshape(1, hd), k_gain.reshape(1, hd), segment_ids)))
    outs = pl.pallas_call(
        store,
        out_shape=(big, big, big, big, small, small),
        in_specs=[vmem] * 6,
        out_specs=(hbm,) * 6,
        scratch_shapes=[pltpu.SemaphoreType.DMA((6,))],
    )(*map(in_vmem, outs))
    wide = tuple(x.reshape(1, rows, cols) for x in outs[:4])
    return wide + (outs[4].reshape(hd), outs[5].reshape(hd))


def solution(mesh):
    tokens = P("dp", ("blk", "inner"), None)
    return jax.shard_map(
        local,
        mesh=mesh,
        in_specs=(tokens,) * 5 + (P(), P(), P("dp", None)),
        out_specs=(tokens,) * 4 + (P(), P()),
        check_vma=False,
    )
```

```python
import functools
import math

import jax
import jax.numpy as jnp
from jax import lax
from jax.experimental import pallas as pl
from jax.experimental.pallas import tpu as pltpu
from jax.sharding import PartitionSpec as P

EPSILON = 1e-06
MESH = pl.DeviceIdType.MESH
AXES = ("dp", "blk", "inner")
F32 = jnp.float32
BF16 = jnp.bfloat16
NT = (((1,), (1,)), ((), ()))
NN = (((1,), (0,)), ((), ()))
TN = (((0,), (0,)), ((), ()))
OFF = -1e30
NO_SEGMENT = -9.0


def dot(a, b, dims):
    return lax.dot_general(a, b, dims, preferred_element_type=F32)


def unit(x):
    inverse = lax.rsqrt(jnp.mean(x * x, axis=-1, keepdims=True) + EPSILON)
    return x * inverse, inverse


def norm_back(d_norm, unit_rows, inverse, gain, scale):
    along = d_norm * unit_rows
    mean = jnp.mean(along * gain, axis=-1, keepdims=True)
    return (inverse * scale) * (d_norm * gain - unit_rows * mean), along


def attend(problems, scale):
    factor = scale * math.log2(math.e)
    scores = [dot(k_norm, q_norm, NT) for q_norm, k_norm, _, _, _ in problems]
    d_ws = [dot(v, g, NT) for _, _, v, g, _ in problems]
    es = [jnp.exp2(s * factor + p[4]) for s, p in zip(scores, problems)]
    totals = [jnp.sum(e, axis=0, keepdims=True) for e in es]
    ws = [e * (1.0 / jnp.where(t == 0.0, 1.0, t)) for e, t in zip(es, totals)]
    w_bs = [w.astype(BF16) for w in ws]
    outs = [dot(w_b, p[2], TN) for w_b, p in zip(w_bs, problems)]
    d_vs = [dot(w_b, p[3], NN) for w_b, p in zip(w_bs, problems)]
    dots = [jnp.sum(w * d_w, axis=0, keepdims=True) for w, d_w in zip(ws, d_ws)]
    d_ss = [(w * (d_w - o)).astype(BF16) for w, d_w, o in zip(ws, d_ws, dots)]
    d_qs = [dot(d_s, p[1], TN) for d_s, p in zip(d_ss, problems)]
    d_ks = [dot(d_s, p[0], NN) for d_s, p in zip(d_ss, problems)]
    return list(zip(outs, d_qs, d_ks, d_vs))


def to_column(row):
    n = row.shape[1]
    r = lax.broadcasted_iota(jnp.int32, (n, n), 0)
    c = lax.broadcasted_iota(jnp.int32, (n, n), 1)
    return jnp.sum(jnp.where(r == c, row, 0.0), axis=1, keepdims=True)


def transposed(x):
    n = x.shape[1]
    r = lax.broadcasted_iota(jnp.int32, (n, n), 0)
    c = lax.broadcasted_iota(jnp.int32, (n, n), 1)
    return dot((r == c).astype(F32).astype(BF16), x, NT)


def grouped(sizes):
    groups = []
    for axis in AXES:
        if groups and groups[-1][1] * sizes[axis] <= 32:
            groups[-1] = (groups[-1][0] + (axis,), groups[-1][1] * sizes[axis])
        else:
            groups.append(((axis,), sizes[axis]))
    return groups


def rounds(sizes):
    n, found, d = sizes["blk"] * sizes["inner"], [], 1
    while d < n:
        found.append(d)
        d *= 2
    return found


def kernel(cfg, q_hbm, k_hbm, v_hbm, s_hbm, g_hbm, qg_hbm, kg_hbm, seg_hbm,
           att_o, dq_o, dk_o, dv_o, gq_o, gk_o,
           qv, kv, vv, gv, s_ref, qg_ref, kg_ref, seg_ref, s_col, near, give, take, back,
           part_k, bias_own, bias_edge, gsrc, gslot,
           load_sem, send_sem, recv_sem, back_sem, take_sem, here_sem, gsend, grecv):
    sizes, rows, heads, hd, h, hpc = cfg
    n_dp, n_blk, n_inner = (sizes[a] for a in AXES)
    nc = heads // hpc
    hh = h // 2
    width = hpc * hd
    scale = 1.0 / math.sqrt(hd)
    dp, blk, inner = (lax.axis_index(a) for a in AXES)
    p = blk * n_inner + inner
    n_line = n_blk * n_inner
    last = n_line - 1
    has_left, has_right = p > 0, p < last
    left, right = p - 1, p + 1
    first, final = inner == 0, inner == n_inner - 1
    ids = ({"blk": jnp.where(first, blk - 1, blk), "inner": jnp.where(first, n_inner - 1, inner - 1)},
           {"blk": jnp.where(final, blk + 1, blk), "inner": jnp.where(final, 0, inner + 1)})
    sides = ((0, has_left), (1, has_right))
    lo, hi = slice(0, hh), slice(rows - hh, rows)
    lo_in, hi_in = slice(hh, h), slice(rows - h, rows - hh)

    loads = [
        pltpu.make_async_copy(src, dst, load_sem.at[i])
        for i, (src, dst) in enumerate(((s_hbm, s_ref), (seg_hbm, seg_ref), (v_hbm, vv), (k_hbm, kv),
                                        (q_hbm, qv), (g_hbm, gv), (qg_hbm, qg_ref), (kg_hbm, kg_ref)))
    ]
    for c in loads:
        c.start()

    barrier = pltpu.get_barrier_semaphore()
    others = [jnp.where(dp + d >= n_dp, dp + d - n_dp, dp + d) for d in range(1, n_dp)]
    for side, there in sides:
        @pl.when(there)
        def _():
            pl.semaphore_signal(barrier, inc=1, device_id=ids[side], device_id_type=MESH)
    for other in others:
        pl.semaphore_signal(barrier, inc=1, device_id={"dp": other}, device_id_type=MESH)

    dists = rounds(sizes)

    def say_here(i):
        if i > 0:
            d = dists[i - 1]
            pl.semaphore_wait(here_sem.at[i - 1], (p >= d).astype(jnp.int32) + (p + d <= last).astype(jnp.int32))
        if i < len(dists):
            for pos, there in ((p - dists[i], p >= dists[i]), (p + dists[i], p + dists[i] <= last)):
                @pl.when(there)
                def _():
                    pl.semaphore_signal(here_sem.at[i], inc=1, device_id_type=MESH,
                                        device_id={"blk": pos // n_inner, "inner": lax.rem(pos, n_inner)})
        else:
            for other in others:
                pl.semaphore_signal(here_sem.at[i], inc=1, device_id={"dp": other}, device_id_type=MESH)

    loads[0].wait()
    s_f = transposed(s_ref[...])
    s_col[...] = s_f.astype(BF16)

    def seg_at(pos):
        start = pl.multiple_of(pos * rows, 128)
        return seg_ref[:, pl.ds(start, rows)].astype(F32)

    loads[1].wait()
    own = seg_at(p)
    prev = jnp.where(has_left, seg_at(jnp.maximum(left, 0)), -1.0)
    nxt = jnp.where(has_right, seg_at(jnp.minimum(right, last)), -2.0)

    def pick(row, index):
        return jnp.sum(row[:, index:index + 1], axis=1, keepdims=True)

    before, after = pick(prev, rows - 1), pick(nxt, 0)
    own_first, own_last = pick(own, 0), pick(own, rows - 1)
    long_lo = jnp.where(pick(own, hh) == before, 1.0, 0.0)
    long_hi = jnp.where(pick(own, rows - hh - 1) == after, 1.0, 0.0)
    short_lo = jnp.where(pick(prev, rows - hh - 1) == own_first, 1.0, 0.0)
    short_hi = jnp.where(pick(nxt, hh) == own_last, 1.0, 0.0)

    def over(x):
        return jnp.broadcast_to(x, (hh, hd)) > 0.5

    lo_is_long, hi_is_long = over(long_lo), over(long_hi)
    lo_is_short, hi_is_short = over(short_lo), over(short_hi)

    def columns(c):
        return pl.ds(pl.multiple_of(c * width, 128), width)

    def near_copy(side, c):
        cols = slice(c * width, (c + 1) * width)
        return pltpu.make_async_remote_copy(
            src_ref=give.at[side, :, :, cols],
            dst_ref=near.at[1 - side, :, :, cols],
            send_sem=send_sem.at[side],
            recv_sem=recv_sem.at[1 - side, c],
            device_id=ids[side],
            device_id_type=MESH,
        )

    def back_copy(side):
        return pltpu.make_async_remote_copy(
            src_ref=back.at[side],
            dst_ref=take.at[1 - side],
            send_sem=back_sem.at[side],
            recv_sem=take_sem.at[1 - side],
            device_id=ids[side],
            device_id_type=MESH,
        )

    def arrival(ref, send, recv, side):
        return pltpu.make_async_remote_copy(
            src_ref=ref, dst_ref=ref, send_sem=send, recv_sem=recv, device_id=ids[side], device_id_type=MESH)

    for c in loads[2:6]:
        c.wait()
    pl.semaphore_wait(barrier, has_left.astype(jnp.int32) + has_right.astype(jnp.int32) + (n_dp - 1))
    say_here(0)
    for c in range(nc):
        for head in range(c * hpc, (c + 1) * hpc):
            cols = slice(head * hd, (head + 1) * hd)
            for side, edge, inward, is_long in ((0, lo, lo_in, lo_is_long), (1, hi, hi_in, hi_is_long)):
                s_edge, s_inward = s_f[edge, head:head + 1], s_f[inward, head:head + 1]
                give[side, 0, :, cols] = kv[edge, cols]
                give[side, 1, :, cols] = (vv[edge, cols].astype(F32) * s_edge).astype(BF16)
                give[side, 2, :, cols] = jnp.where(
                    is_long, kv[inward, cols].astype(F32), qv[edge, cols].astype(F32)).astype(BF16)
                give[side, 3, :, cols] = jnp.where(
                    is_long, vv[inward, cols].astype(F32) * s_inward, gv[edge, cols].astype(F32)).astype(BF16)
        for side, there in sides:
            @pl.when(there)
            def _():
                near_copy(side, c).start()

    for side, there in sides:
        @pl.when(jnp.logical_not(there))
        def _():
            near[side] = jnp.zeros((4, hh, heads * hd), BF16)
            take[side] = jnp.zeros((2, hh, heads * hd), BF16)

    own_col, prev_col, nxt_col = to_column(own), to_column(prev), to_column(nxt)

    later = jnp.where(own == before, short_lo, 0.0) + jnp.where(own == after, short_hi, 0.0)
    own_q = jnp.where(later > 0.5, NO_SEGMENT, own)
    wide_col = jnp.concatenate([prev_col[rows - hh:], own_col, nxt_col[:hh]], axis=0)
    bias_own[...] = jnp.where(wide_col == own_q, 0.0, OFF)

    q_lo = jnp.where(short_lo > 0.5, own[:, :hh], prev[:, rows - hh:])
    q_hi = jnp.where(short_hi > 0.5, own[:, rows - hh:], nxt[:, :hh])
    q_lo = jnp.where((q_lo == before) & (own_first == before), q_lo, NO_SEGMENT)
    q_hi = jnp.where((q_hi == after) & (own_last == after), q_hi, NO_SEGMENT)
    k_lo = jnp.where(short_lo > 0.5, prev_col[rows - h:rows - hh], own_col[hh:h])
    k_hi = jnp.where(short_hi > 0.5, nxt_col[hh:h], own_col[rows - h:rows - hh])
    edge_col = jnp.concatenate(
        [k_lo, prev_col[rows - hh:], own_col[:hh], own_col[rows - hh:], nxt_col[:hh], k_hi], axis=0)
    bias_edge[...] = jnp.where(edge_col == jnp.concatenate([q_lo, q_hi], axis=1), 0.0, OFF)
    lo_adds = over(jnp.where(own_col[:hh] == before, short_lo, 0.0))
    hi_adds = over(jnp.where(own_col[rows - hh:] == after, short_hi, 0.0))

    for c in loads[6:]:
        c.wait()
    q_gain, k_gain = qg_ref[...], kg_ref[...]
    which = lax.broadcasted_iota(jnp.int32, (heads, hd), 0)

    def scale_of(head, part):
        one = jnp.where(which == head, 1.0, 0.0).astype(BF16)
        return dot(s_col[part], one, NN)

    own_k = slice(hh, hh + rows)

    def both(for_lo, for_hi, x, y):
        return jnp.concatenate([jnp.where(for_lo, x[:hh], y[:hh]), jnp.where(for_hi, x[hh:], y[hh:])], axis=0)

    def ends(x, n):
        return jnp.concatenate([x[:n], x[x.shape[0] - n:]], axis=0)

    def prepare(head):
        cols = pl.ds(pl.multiple_of(head * hd, 128), hd)
        s_all = scale_of(head, slice(0, rows))
        g = gv[:, cols]
        v_own = (vv[:, cols].astype(F32) * s_all).astype(BF16)
        v = jnp.concatenate([near[0, 1, :, cols], v_own, near[1, 1, :, cols]], axis=0)
        k = jnp.concatenate([near[0, 0, :, cols], kv[:, cols], near[1, 0, :, cols]], axis=0)
        q_unit, q_inv = unit(qv[:, cols].astype(F32))
        k_unit, k_inv = unit(k.astype(F32))
        q_norm, k_norm = (q_unit * q_gain).astype(BF16), (k_unit * k_gain).astype(BF16)
        far_0 = jnp.concatenate([near[0, 2, :, cols], near[1, 2, :, cols]], axis=0).astype(F32)
        far_1 = jnp.concatenate([near[0, 3, :, cols], near[1, 3, :, cols]], axis=0).astype(F32)
        far_0, _ = unit(far_0)
        is_short = lo_is_short, hi_is_short
        q_e = (both(*is_short, ends(q_unit, hh), far_0) * q_gain).astype(BF16)
        g_e = both(*is_short, ends(g, hh).astype(F32), far_1).astype(BF16)
        own_in = slice(h, h + hh), slice(rows - hh, rows)
        k_x = jnp.concatenate([k_unit[i] for i in own_in], axis=0)
        v_x = jnp.concatenate([v[i] for i in own_in], axis=0).astype(F32)
        k_x = (both(*is_short, far_0, k_x) * k_gain).astype(BF16)
        v_x = both(*is_short, far_1, v_x).astype(BF16)
        k_e = jnp.concatenate([k_x[:hh], k_norm[:h], k_norm[rows:], k_x[hh:]], axis=0)
        v_e = jnp.concatenate([v_x[:hh], v[:h], v[rows:], v_x[hh:]], axis=0)
        own_problem = q_norm, k_norm, v, g, bias_own[...]
        edge_problem = q_e, k_e, v_e, g_e, bias_edge[...]
        return (cols, s_all, q_unit, q_inv, k_unit, k_inv), own_problem, edge_problem

    def conclude(ready, own_result, edge_result, acc):
        acc_q, acc_k = acc
        cols, s_all, q_unit, q_inv, k_unit, k_inv = ready
        out, d_q, d_k, d_v = own_result
        out_e, d_q_e, d_k_e, d_v_e = edge_result
        back[0, 0, :, cols], back[1, 0, :, cols] = d_k[:hh].astype(BF16), d_k[rows + hh:].astype(BF16)
        back[0, 1, :, cols], back[1, 1, :, cols] = d_v[:hh].astype(BF16), d_v[rows + hh:].astype(BF16)
        to_lo, to_hi = d_k[:hh] * k_unit[:hh], d_k[rows + hh:] * k_unit[rows + hh:]
        acc_k = acc_k + jnp.sum(
            jnp.where(lo_is_long, to_lo, 0.0) + jnp.where(hi_is_long, to_hi, 0.0), axis=0, keepdims=True)

        def to_queries(x, e):
            return jnp.concatenate(
                [x[lo] + jnp.where(lo_is_short, e[:hh], 0.0), x[hh:rows - hh],
                 x[hi] + jnp.where(hi_is_short, e[hh:], 0.0)], axis=0)

        def to_keys(x, e):
            x = x[own_k]
            middle = [x[h:rows - h]] if rows > 2 * h else []
            return jnp.concatenate(
                [x[lo] + e[2 * hh:3 * hh], x[lo_in] + jnp.where(lo_is_short, 0.0, e[:hh]), *middle,
                 x[hi_in] + jnp.where(hi_is_short, 0.0, e[5 * hh:]), x[hi] + e[3 * hh:4 * hh]], axis=0)

        att_o[:, cols] = to_queries(out, out_e).astype(BF16)
        d_x, along = norm_back(to_queries(d_q, d_q_e), q_unit, q_inv, q_gain, scale)
        dq_o[:, cols] = d_x.astype(BF16)
        acc_q = acc_q + jnp.sum(along, axis=0, keepdims=True)
        d_k, d_v = to_keys(d_k, d_k_e), to_keys(d_v, d_v_e)
        part_k[0, :, cols], part_k[1, :, cols] = ends(d_k, hh), ends(d_v, hh)
        d_x, along = norm_back(d_k, k_unit[own_k], k_inv[own_k], k_gain, scale)
        acc_k = acc_k + jnp.sum(along, axis=0, keepdims=True)
        mid = slice(hh, rows - hh)
        dk_o[mid, cols] = d_x[mid].astype(BF16)
        dv_o[mid, cols] = (d_v[mid] * s_all[mid]).astype(BF16)
        return acc_q, acc_k

    rounds_at = [0, 1, 2]

    def step(c, acc):
        for side, there in sides:
            @pl.when(there)
            def _():
                arrival(near.at[side, :, :, columns(c)], send_sem.at[side], recv_sem.at[side, c], side).wait_recv()
        prepared = [prepare(c * hpc + j) for j in range(hpc)]
        results = attend([x for _, a, b in prepared for x in (a, b)], scale)
        for j, (ready, _, _) in enumerate(prepared):
            acc = conclude(ready, results[2 * j], results[2 * j + 1], acc)
        for i, at in enumerate(rounds_at):
            @pl.when(c == at)
            def _():
                say_here(i + 1)
        return acc

    zero = jnp.zeros((1, hd), F32)
    acc_q, acc_k = lax.fori_loop(0, nc, step, (zero, zero))
    for side, there in sides:
        @pl.when(there)
        def _():
            back_copy(side).start()
    for i in range(len(rounds_at), len(dists)):
        say_here(i + 1)
    pl.semaphore_wait(here_sem.at[len(dists)], n_dp - 1)

    stages = grouped(sizes)
    me = {a: i for a, i in zip(AXES, (dp, blk, inner))}
    total = jnp.concatenate([acc_q, acc_k], axis=0) * scale

    def spread(stage, offset, total):
        axes, n = stages[stage]
        index = 0
        for axis in axes:
            index = index * sizes[axis] + me[axis]
        gsrc[stage] = total
        gslot[offset + index] = total
        for to in range(n):
            device, rest = {}, to
            for axis in reversed(axes):
                device[axis], rest = rest % sizes[axis], rest // sizes[axis]

            @pl.when(index != to)
            def _():
                pltpu.make_async_remote_copy(
                    src_ref=gsrc.at[stage], dst_ref=gslot.at[offset + index],
                    send_sem=gsend.at[stage], recv_sem=grecv.at[stage],
                    device_id=device, device_id_type=MESH).start()

    def gathered(stage, offset):
        axes, n = stages[stage]
        everything = gslot.at[pl.ds(offset, n - 1)]
        pltpu.make_async_remote_copy(
            src_ref=everything, dst_ref=everything,
            send_sem=gsend.at[stage], recv_sem=grecv.at[stage],
            device_id={axis: 0 for axis in axes}, device_id_type=MESH).wait()
        total = gslot[offset]
        for i in range(1, n):
            total = total + gslot[offset + i]
        return total

    spread(0, 0, total)

    for side, there in sides:
        @pl.when(there)
        def _():
            arrival(take.at[side], back_sem.at[side], take_sem.at[side], side).wait_recv()

    def last_step(c, carry):
        for j in range(hpc):
            head = c * hpc + j
            cols = pl.ds(pl.multiple_of(head * hd, 128), hd)
            k_unit, k_inv = unit(ends(kv[:, cols], hh).astype(F32))
            s_ends = jnp.concatenate([scale_of(head, lo), scale_of(head, hi)], axis=0)
            none = jnp.zeros((2 * hh, hd), F32)
            d_k, d_v = (
                part_k[i, :, cols] + both(lo_adds, hi_adds, jnp.concatenate(
                    [take[0, i, :, cols], take[1, i, :, cols]], axis=0).astype(F32), none)
                for i in range(2))
            d_k, _ = norm_back(d_k, k_unit, k_inv, k_gain, scale)
            d_k, d_v = d_k.astype(BF16), (d_v * s_ends).astype(BF16)
            dk_o[lo, cols], dk_o[hi, cols] = d_k[:hh], d_k[hh:]
            dv_o[lo, cols], dv_o[hi, cols] = d_v[:hh], d_v[hh:]
        return carry

    lax.fori_loop(0, nc, last_step, 0)

    for side, there in sides:
        @pl.when(there)
        def _():
            arrival(near.at[side], send_sem.at[side], recv_sem.at[side, 0], side).wait_send()
            arrival(take.at[side], back_sem.at[side], take_sem.at[side], side).wait_send()

    offset = 0
    for stage, (_, n) in enumerate(stages):
        if stage > 0:
            spread(stage, offset, total)
        total = gathered(stage, offset)
        offset += n
    gq_o[...] = total[0:1]
    gk_o[...] = total[1:2]


def store(*refs):
    n = len(refs) // 2
    sem = refs[-1]
    copies = [pltpu.make_async_copy(refs[i], refs[n + i], sem.at[i]) for i in range(n)]
    for x in copies:
        x.start()
    for x in copies:
        x.wait()


def local(queries, keys, values, v_scale, d_out, q_gain, k_gain, segment_ids):
    _, rows, cols = queries.shape
    hd = q_gain.shape[0]
    heads = cols // hd
    sizes = {a: lax.axis_size(a) for a in AXES}
    h = rows * sizes["inner"] // 8
    hpc = 3 if heads % 3 == 0 else 1
    nc = heads // hpc
    flat = lambda x: x.reshape(rows, x.shape[2])
    vmem = pl.BlockSpec(memory_space=pltpu.VMEM)
    hbm = pl.BlockSpec(memory_space=pltpu.HBM)
    in_hbm = lambda x: pltpu.with_memory_space_constraint(x, pltpu.HBM)
    in_vmem = lambda x: pltpu.with_memory_space_constraint(x, pltpu.VMEM)
    big = jax.ShapeDtypeStruct((rows, cols), BF16)
    small = jax.ShapeDtypeStruct((1, hd), F32)
    stages = grouped(sizes)
    outs = pl.pallas_call(
        functools.partial(kernel, (sizes, rows, heads, hd, h, hpc)),
        out_shape=(big, big, big, big, small, small),
        in_specs=[hbm] * 8,
        out_specs=(vmem,) * 6,
        scratch_shapes=[
            pltpu.VMEM((rows, cols), BF16),
            pltpu.VMEM((rows, cols), BF16),
            pltpu.VMEM((rows, cols), BF16),
            pltpu.VMEM((rows, cols), BF16),
            pltpu.VMEM((heads, rows), BF16),
            pltpu.VMEM((1, hd), F32),
            pltpu.VMEM((1, hd), F32),
            pltpu.VMEM(segment_ids.shape, jnp.int32),
            pltpu.VMEM((rows, heads), BF16),
            pltpu.VMEM((2, 4, h // 2, cols), BF16),
            pltpu.VMEM((2, 4, h // 2, cols), BF16),
            pltpu.VMEM((2, 2, h // 2, cols), BF16),
            pltpu.VMEM((2, 2, h // 2, cols), BF16),
            pltpu.VMEM((2, h, cols), F32),
            pltpu.VMEM((rows + h, rows), F32),
            pltpu.VMEM((3 * h, h), F32),
            pltpu.VMEM((len(stages), 2, hd), F32),
            pltpu.VMEM((sum(n for _, n in stages), 2, hd), F32),
            pltpu.SemaphoreType.DMA((8,)),
            pltpu.SemaphoreType.DMA((2,)),
            pltpu.SemaphoreType.DMA((2, nc)),
            pltpu.SemaphoreType.DMA((2,)),
            pltpu.SemaphoreType.DMA((2,)),
            pltpu.SemaphoreType.REGULAR((len(rounds(sizes)) + 1,)),
            pltpu.SemaphoreType.DMA((len(stages),)),
            pltpu.SemaphoreType.DMA((len(stages),)),
        ],
        compiler_params=pltpu.CompilerParams(
            collective_id=0, has_side_effects=True, vmem_limit_bytes=32 << 20),
    )(*map(in_hbm, (flat(queries), flat(keys), flat(values), flat(v_scale).T, flat(d_out),
                    q_gain.reshape(1, hd), k_gain.reshape(1, hd), segment_ids)))
    outs = pl.pallas_call(
        store,
        out_shape=(big, big, big, big, small, small),
        in_specs=[vmem] * 6,
        out_specs=(hbm,) * 6,
        scratch_shapes=[pltpu.SemaphoreType.DMA((6,))],
    )(*map(in_vmem, outs))
    wide = tuple(x.reshape(1, rows, cols) for x in outs[:4])
    return wide + (outs[4].reshape(hd), outs[5].reshape(hd))


def solution(mesh):
    tokens = P("dp", ("blk", "inner"), None)
    return jax.shard_map(
        local,
        mesh=mesh,
        in_specs=(tokens,) * 5 + (P(), P(), P("dp", None)),
        out_specs=(tokens,) * 4 + (P(), P()),
        check_vma=False,
    )
```

```python
import functools
import math

import jax
import jax.numpy as jnp
from jax import lax
from jax.experimental import pallas as pl
from jax.experimental.pallas import tpu as pltpu
from jax.sharding import PartitionSpec as P

EPSILON = 1e-06
MESH = pl.DeviceIdType.MESH
AXES = ("dp", "blk", "inner")
F32 = jnp.float32
BF16 = jnp.bfloat16
NT = (((1,), (1,)), ((), ()))
NN = (((1,), (0,)), ((), ()))
TN = (((0,), (0,)), ((), ()))
OFF = -1e30
NO_SEGMENT = -9.0


def dot(a, b, dims):
    return lax.dot_general(a, b, dims, preferred_element_type=F32)


def unit(x):
    inverse = lax.rsqrt(jnp.mean(x * x, axis=-1, keepdims=True) + EPSILON)
    return x * inverse, inverse


def norm_back(d_norm, unit_rows, inverse, gain, scale):
    along = d_norm * unit_rows
    mean = jnp.mean(along * gain, axis=-1, keepdims=True)
    return (inverse * scale) * (d_norm * gain - unit_rows * mean), along


def attend(problems, scale):
    factor = scale * math.log2(math.e)
    scores = [dot(k_norm, q_norm, NT) for q_norm, k_norm, _, _, _ in problems]
    d_ws = [dot(v, g, NT) for _, _, v, g, _ in problems]
    es = [jnp.exp2(s * factor + p[4]) for s, p in zip(scores, problems)]
    totals = [jnp.sum(e, axis=0, keepdims=True) for e in es]
    ws = [e * (1.0 / jnp.where(t == 0.0, 1.0, t)) for e, t in zip(es, totals)]
    w_bs = [w.astype(BF16) for w in ws]
    outs = [dot(w_b, p[2], TN) for w_b, p in zip(w_bs, problems)]
    d_vs = [dot(w_b, p[3], NN) for w_b, p in zip(w_bs, problems)]
    dots = [jnp.sum(w * d_w, axis=0, keepdims=True) for w, d_w in zip(ws, d_ws)]
    d_ss = [(w * (d_w - o)).astype(BF16) for w, d_w, o in zip(ws, d_ws, dots)]
    d_qs = [dot(d_s, p[1], TN) for d_s, p in zip(d_ss, problems)]
    d_ks = [dot(d_s, p[0], NN) for d_s, p in zip(d_ss, problems)]
    return list(zip(outs, d_qs, d_ks, d_vs))


def to_column(row):
    n = row.shape[1]
    r = lax.broadcasted_iota(jnp.int32, (n, n), 0)
    c = lax.broadcasted_iota(jnp.int32, (n, n), 1)
    return jnp.sum(jnp.where(r == c, row, 0.0), axis=1, keepdims=True)


def transposed(x):
    n = x.shape[1]
    r = lax.broadcasted_iota(jnp.int32, (n, n), 0)
    c = lax.broadcasted_iota(jnp.int32, (n, n), 1)
    return dot((r == c).astype(F32).astype(BF16), x, NT)


def grouped(sizes):
    groups = []
    for axis in AXES:
        if groups and groups[-1][1] * sizes[axis] <= 32:
            groups[-1] = (groups[-1][0] + (axis,), groups[-1][1] * sizes[axis])
        else:
            groups.append(((axis,), sizes[axis]))
    return groups


def rounds(sizes):
    n, found, d = sizes["blk"] * sizes["inner"], [], 1
    while d < n:
        found.append(d)
        d *= 2
    return found


def kernel(cfg, q_hbm, k_hbm, v_hbm, s_hbm, g_hbm, qg_hbm, kg_hbm, seg_hbm,
           att_o, dq_o, dk_o, dv_o, gq_o, gk_o,
           qv, kv, vv, gv, s_ref, qg_ref, kg_ref, seg_ref, s_col, near, give, take, back,
           part_q, part_k, bias_own, bias_lo, bias_hi, gsrc, gslot,
           load_sem, send_sem, recv_sem, back_sem, take_sem, here_sem, gsend, grecv):
    sizes, rows, heads, hd, h, hpc, late_hpc = cfg
    n_dp, n_blk, n_inner = (sizes[a] for a in AXES)
    nc = heads // hpc
    hh = h // 2
    width = hpc * hd
    scale = 1.0 / math.sqrt(hd)
    dp, blk, inner = (lax.axis_index(a) for a in AXES)
    p = blk * n_inner + inner
    n_line = n_blk * n_inner
    last = n_line - 1
    has_left, has_right = p > 0, p < last
    left, right = p - 1, p + 1
    first, final = inner == 0, inner == n_inner - 1
    ids = ({"blk": jnp.where(first, blk - 1, blk), "inner": jnp.where(first, n_inner - 1, inner - 1)},
           {"blk": jnp.where(final, blk + 1, blk), "inner": jnp.where(final, 0, inner + 1)})
    sides = ((0, has_left), (1, has_right))
    lo, hi = slice(0, hh), slice(rows - hh, rows)
    lo_in, hi_in = slice(hh, h), slice(rows - h, rows - hh)

    loads = [
        pltpu.make_async_copy(src, dst, load_sem.at[i])
        for i, (src, dst) in enumerate(((s_hbm, s_ref), (seg_hbm, seg_ref), (v_hbm, vv), (k_hbm, kv),
                                        (q_hbm, qv), (g_hbm, gv), (qg_hbm, qg_ref), (kg_hbm, kg_ref)))
    ]
    for c in loads:
        c.start()

    barrier = pltpu.get_barrier_semaphore()
    others = [jnp.where(dp + d >= n_dp, dp + d - n_dp, dp + d) for d in range(1, n_dp)]
    for side, there in sides:
        @pl.when(there)
        def _():
            pl.semaphore_signal(barrier, inc=1, device_id=ids[side], device_id_type=MESH)
    for other in others:
        pl.semaphore_signal(barrier, inc=1, device_id={"dp": other}, device_id_type=MESH)

    dists = rounds(sizes)

    def say_here(i):
        if i > 0:
            d = dists[i - 1]
            pl.semaphore_wait(here_sem.at[i - 1], (p >= d).astype(jnp.int32) + (p + d <= last).astype(jnp.int32))
        if i < len(dists):
            for pos, there in ((p - dists[i], p >= dists[i]), (p + dists[i], p + dists[i] <= last)):
                @pl.when(there)
                def _():
                    pl.semaphore_signal(here_sem.at[i], inc=1, device_id_type=MESH,
                                        device_id={"blk": pos // n_inner, "inner": lax.rem(pos, n_inner)})
        else:
            for other in others:
                pl.semaphore_signal(here_sem.at[i], inc=1, device_id={"dp": other}, device_id_type=MESH)

    loads[0].wait()
    s_f = transposed(s_ref[...])
    s_col[...] = s_f.astype(BF16)

    def seg_at(pos):
        start = pl.multiple_of(pos * rows, 128)
        return seg_ref[:, pl.ds(start, rows)].astype(F32)

    loads[1].wait()
    own = seg_at(p)
    prev = jnp.where(has_left, seg_at(jnp.maximum(left, 0)), -1.0)
    nxt = jnp.where(has_right, seg_at(jnp.minimum(right, last)), -2.0)

    def pick(row, index):
        return jnp.sum(row[:, index:index + 1], axis=1, keepdims=True)

    before, after = pick(prev, rows - 1), pick(nxt, 0)
    own_first, own_last = pick(own, 0), pick(own, rows - 1)
    long_lo = jnp.where(pick(own, hh) == before, 1.0, 0.0)
    long_hi = jnp.where(pick(own, rows - hh - 1) == after, 1.0, 0.0)
    short_lo = jnp.where(pick(prev, rows - hh - 1) == own_first, 1.0, 0.0)
    short_hi = jnp.where(pick(nxt, hh) == own_last, 1.0, 0.0)

    def over(x):
        return jnp.broadcast_to(x, (hh, hd)) > 0.5

    lo_is_long, hi_is_long = over(long_lo), over(long_hi)
    lo_is_short, hi_is_short = over(short_lo), over(short_hi)

    def columns(c):
        return pl.ds(pl.multiple_of(c * width, 128), width)

    def near_copy(side, c):
        cols = slice(c * width, (c + 1) * width)
        parts = slice(0, 2 + 2 * side)
        return pltpu.make_async_remote_copy(
            src_ref=give.at[side, parts, :, cols],
            dst_ref=near.at[1 - side, parts, :, cols],
            send_sem=send_sem.at[side],
            recv_sem=recv_sem.at[1 - side, c],
            device_id=ids[side],
            device_id_type=MESH,
        )

    def back_copy(side, c):
        return pltpu.make_async_remote_copy(
            src_ref=back.at[side, :, :, columns(c)],
            dst_ref=take.at[1 - side, :, :, columns(c)],
            send_sem=back_sem.at[side],
            recv_sem=take_sem.at[1 - side, c],
            device_id=ids[side],
            device_id_type=MESH,
        )

    def arrival(ref, send, recv, side):
        return pltpu.make_async_remote_copy(
            src_ref=ref, dst_ref=ref, send_sem=send, recv_sem=recv, device_id=ids[side], device_id_type=MESH)

    for c in loads[2:6]:
        c.wait()
    pl.semaphore_wait(barrier, has_left.astype(jnp.int32) + has_right.astype(jnp.int32) + (n_dp - 1))
    say_here(0)
    for c in range(nc):
        for head in range(c * hpc, (c + 1) * hpc):
            cols = slice(head * hd, (head + 1) * hd)
            for side, edge in ((0, lo), (1, hi)):
                give[side, 0, :, cols] = kv[edge, cols]
                give[side, 1, :, cols] = (vv[edge, cols].astype(F32) * s_f[edge, head:head + 1]).astype(BF16)
            give[1, 2, :, cols] = jnp.where(
                hi_is_long, kv[hi_in, cols].astype(F32), qv[hi, cols].astype(F32)).astype(BF16)
            give[1, 3, :, cols] = jnp.where(
                hi_is_long, vv[hi_in, cols].astype(F32) * s_f[hi_in, head:head + 1],
                gv[hi, cols].astype(F32)).astype(BF16)
        for side, there in sides:
            @pl.when(there)
            def _():
                near_copy(side, c).start()
    for side, there in sides:
        @pl.when(jnp.logical_not(there))
        def _():
            near[side] = jnp.zeros((4, hh, heads * hd), BF16)
            take[side] = jnp.zeros((2, hh, heads * hd), BF16)

    own_col, prev_col, nxt_col = to_column(own), to_column(prev), to_column(nxt)

    later = jnp.where(own == before, short_lo, 0.0) + jnp.where(own == after, short_hi, 0.0)
    own_q = jnp.where(later > 0.5, NO_SEGMENT, own)
    wide_col = jnp.concatenate([prev_col[rows - hh:], own_col, nxt_col[:hh]], axis=0)
    bias_own[...] = jnp.where(wide_col == own_q, 0.0, OFF)

    q_lo = jnp.where(short_lo > 0.5, own[:, :hh], prev[:, rows - hh:])
    q_hi = jnp.where(short_hi > 0.5, own[:, rows - hh:], nxt[:, :hh])
    q_lo = jnp.where((q_lo == before) & (own_first == before), q_lo, NO_SEGMENT)
    q_hi = jnp.where((q_hi == after) & (own_last == after), q_hi, NO_SEGMENT)
    k_lo = jnp.where(short_lo > 0.5, prev_col[rows - h:rows - hh], own_col[hh:h])
    k_hi = jnp.where(short_hi > 0.5, nxt_col[hh:h], own_col[rows - h:rows - hh])
    lo_col = jnp.concatenate([k_lo, prev_col[rows - hh:], own_col[:hh]], axis=0)
    hi_col = jnp.concatenate([own_col[rows - hh:], nxt_col[:hh], k_hi], axis=0)
    bias_lo[...] = jnp.where(lo_col == q_lo, 0.0, OFF)
    bias_hi[...] = jnp.where(hi_col == q_hi, 0.0, OFF)
    lo_far = jnp.broadcast_to(own_col[lo_in], (hh, hd)) == before
    lo_adds = over(jnp.where(own_col[:hh] == before, short_lo, 0.0))
    hi_adds = over(jnp.where(own_col[rows - hh:] == after, short_hi, 0.0))

    for c in loads[6:]:
        c.wait()
    q_gain, k_gain = qg_ref[...], kg_ref[...]
    which = lax.broadcasted_iota(jnp.int32, (heads, hd), 0)

    def scale_of(head, part):
        one = jnp.where(which == head, 1.0, 0.0).astype(BF16)
        return dot(s_col[part], one, NN)

    own_k = slice(hh, hh + rows)
    q_done, k_done = slice(0, rows - hh), slice(hh, rows - h)
    hi_all = slice(rows - h, rows)
    is_counted = jnp.broadcast_to(long_lo + short_lo, (1, hd)) > 0.5
    is_foreign = jnp.broadcast_to(long_lo, (1, hd)) > 0.5

    def column_sum(x):
        return jnp.sum(x, axis=0, keepdims=True)

    def prepare(head):
        cols = pl.ds(pl.multiple_of(head * hd, 128), hd)
        s_all = scale_of(head, slice(0, rows))
        g = gv[:, cols]
        v_own = (vv[:, cols].astype(F32) * s_all).astype(BF16)
        v = jnp.concatenate([near[0, 1, :, cols], v_own, near[1, 1, :, cols]], axis=0)
        k = jnp.concatenate([near[0, 0, :, cols], kv[:, cols], near[1, 0, :, cols]], axis=0)
        q_unit, q_inv = unit(qv[:, cols].astype(F32))
        k_unit, k_inv = unit(k.astype(F32))
        q_norm, k_norm = (q_unit * q_gain).astype(BF16), (k_unit * k_gain).astype(BF16)
        far_0, far_1 = near[0, 2, :, cols].astype(F32), near[0, 3, :, cols].astype(F32)
        far_0, _ = unit(far_0)
        q_e = (jnp.where(lo_is_short, q_unit[lo], far_0) * q_gain).astype(BF16)
        g_e = jnp.where(lo_is_short, g[lo].astype(F32), far_1).astype(BF16)
        k_x = jnp.where(lo_is_short, far_0, k_unit[h:h + hh])
        v_x = jnp.where(lo_is_short, far_1, v[h:h + hh].astype(F32)).astype(BF16)
        k_e = jnp.concatenate([(k_x * k_gain).astype(BF16), k_norm[:h]], axis=0)
        v_e = jnp.concatenate([v_x, v[:h]], axis=0)
        own_problem = q_norm, k_norm, v, g, bias_own[...]
        edge_problem = q_e, k_e, v_e, g_e, bias_lo[...]
        k_in, v_in = k[h:h + hh].astype(F32), v[h:h + hh].astype(F32)
        q_lo, g_lo = qv[lo, cols].astype(F32), g[lo].astype(F32)
        to_left = (k_in, q_lo), (v_in, g_lo)
        return (cols, s_all, q_unit, q_inv, k_unit, k_inv, far_0, k_x, to_left), own_problem, edge_problem

    def conclude(ready, own_result, edge_result, acc):
        acc_q, acc_k = acc
        cols, s_all, q_unit, q_inv, k_unit, k_inv, far_0, k_x, to_left = ready
        out, d_q, d_k, d_v = own_result
        out_e, d_q_e, d_k_e, d_v_e = edge_result
        for i, x in enumerate((d_k, d_v)):
            inward, edge = to_left[i]
            back[0, i, :, cols] = jnp.where(lo_is_long, jnp.where(lo_far, inward, x[:hh]), edge).astype(BF16)
            back[1, i, :, cols] = x[rows + hh:].astype(BF16)
        edge_k = column_sum(d_k_e[:hh] * k_x) + column_sum(d_k_e[hh:] * k_unit[:h])
        acc_k = acc_k + column_sum(d_k * k_unit) + jnp.where(is_counted, edge_k, 0.0)
        acc_q = acc_q + jnp.where(is_foreign, column_sum(d_q_e * far_0), 0.0)

        def to_queries(x, e):
            return jnp.concatenate([x[lo] + jnp.where(lo_is_short, e, 0.0), x[hh:]], axis=0)

        def to_keys(x, e):
            x = x[own_k]
            return jnp.concatenate(
                [x[lo] + e[2 * hh:], x[lo_in] + jnp.where(lo_is_short, 0.0, e[:hh]), x[h:]], axis=0)

        out, d_q = to_queries(out, out_e), to_queries(d_q, d_q_e)
        att_o[q_done, cols] = out[q_done].astype(BF16)
        part_q[0, :, cols], part_q[1, :, cols] = out[hi], d_q[hi]
        d_x, along = norm_back(d_q, q_unit, q_inv, q_gain, scale)
        dq_o[q_done, cols] = d_x[q_done].astype(BF16)
        acc_q = acc_q + column_sum(along)
        d_k, d_v = to_keys(d_k, d_k_e), to_keys(d_v, d_v_e)
        for i, x in enumerate((d_k, d_v)):
            part_k[i, lo, cols], part_k[i, hh:, cols] = x[lo], x[hi_all]
        d_x, _ = norm_back(d_k[k_done], k_unit[own_k][k_done], k_inv[own_k][k_done], k_gain, scale)
        dk_o[k_done, cols] = d_x.astype(BF16)
        dv_o[k_done, cols] = (d_v[k_done] * s_all[k_done]).astype(BF16)
        return acc_q, acc_k

    rounds_at = [c for c in range(nc)][:len(dists)]

    def step(c, acc):
        for side, there in sides:
            @pl.when(there)
            def _():
                arrival(near.at[side, 0:4 - 2 * side, :, columns(c)], send_sem.at[side], recv_sem.at[side, c],
                        side).wait_recv()

        prepared = [prepare(c * hpc + j) for j in range(hpc)]
        results = attend([x for _, a, b in prepared for x in (a, b)], scale)
        for j, (ready, _, _) in enumerate(prepared):
            acc = conclude(ready, results[2 * j], results[2 * j + 1], acc)
        for side, there in sides:
            @pl.when(there)
            def _():
                back_copy(side, c).start()
        for i, at in enumerate(rounds_at):
            @pl.when(c == at)
            def _():
                say_here(i + 1)
        return acc

    zero = jnp.zeros((1, hd), F32)
    acc_q, acc_k = lax.fori_loop(0, nc, step, (zero, zero))
    for i in range(len(rounds_at), len(dists)):
        say_here(i + 1)
    pl.semaphore_wait(here_sem.at[len(dists)], n_dp - 1)

    stages = grouped(sizes)
    me = {a: i for a, i in zip(AXES, (dp, blk, inner))}
    total = jnp.concatenate([acc_q, acc_k], axis=0) * scale

    def spread(stage, offset, total):
        axes, n = stages[stage]
        index = 0
        for axis in axes:
            index = index * sizes[axis] + me[axis]
        gsrc[stage] = total
        gslot[offset + index] = total
        for to in range(n):
            device, rest = {}, to
            for axis in reversed(axes):
                device[axis], rest = rest % sizes[axis], rest // sizes[axis]

            @pl.when(index != to)
            def _():
                pltpu.make_async_remote_copy(
                    src_ref=gsrc.at[stage], dst_ref=gslot.at[offset + index],
                    send_sem=gsend.at[stage], recv_sem=grecv.at[stage],
                    device_id=device, device_id_type=MESH).start()

    def gathered(stage, offset):
        axes, n = stages[stage]
        everything = gslot.at[pl.ds(offset, n - 1)]
        pltpu.make_async_remote_copy(
            src_ref=everything, dst_ref=everything,
            send_sem=gsend.at[stage], recv_sem=grecv.at[stage],
            device_id={axis: 0 for axis in axes}, device_id_type=MESH).wait()
        total = gslot[offset]
        for i in range(1, n):
            total = total + gslot[offset + i]
        return total

    spread(0, 0, total)

    def late_prepare(head):
        cols = pl.ds(pl.multiple_of(head * hd, 128), hd)
        s_ends = jnp.concatenate([scale_of(head, lo), scale_of(head, hi_all)], axis=0)
        k_unit, k_inv = unit(jnp.concatenate([kv[lo, cols], kv[hi_all, cols]], axis=0).astype(F32))
        q_unit, q_inv = unit(qv[hi, cols].astype(F32))
        near_k, _ = unit(near[1, 0, :, cols].astype(F32))
        far_0, _ = unit(take[1, 0, :, cols].astype(F32))
        far_1 = take[1, 1, :, cols].astype(F32)
        v_f = vv[hi_all, cols].astype(F32) * s_ends[hh:]
        q_e = (jnp.where(hi_is_short, q_unit, far_0) * q_gain).astype(BF16)
        g_e = jnp.where(hi_is_short, gv[hi, cols].astype(F32), far_1).astype(BF16)
        k_x = jnp.where(hi_is_short, far_0, k_unit[hh:h])
        k_e = (jnp.concatenate([k_unit[h:], near_k, k_x], axis=0) * k_gain).astype(BF16)
        v_x = jnp.where(hi_is_short, far_1, v_f[:hh]).astype(BF16)
        v_e = jnp.concatenate([v_f[hh:].astype(BF16), near[1, 1, :, cols], v_x], axis=0)
        return (cols, s_ends, q_unit, q_inv, k_unit, k_inv), (q_e, k_e, v_e, g_e, bias_hi[...])

    def late_conclude(ready, result):
        cols, s_ends, q_unit, q_inv, k_unit, k_inv = ready
        out, d_q, d_k, d_v = result

        def to_keys(i, e):
            x = part_k[i, :, cols]
            from_lo, from_hi = take[0, i, :, cols].astype(F32), take[1, i, :, cols].astype(F32)
            return jnp.concatenate(
                [x[lo] + jnp.where(lo_adds, from_lo, 0.0), x[hh:h] + jnp.where(hi_is_short, 0.0, e[h:]),
                 x[h:] + e[:hh] + jnp.where(hi_adds, from_hi, 0.0)], axis=0)

        att_o[hi, cols] = (part_q[0, :, cols] + jnp.where(hi_is_short, out, 0.0)).astype(BF16)
        d_q = part_q[1, :, cols] + jnp.where(hi_is_short, d_q, 0.0)
        dq_o[hi, cols] = norm_back(d_q, q_unit, q_inv, q_gain, scale)[0].astype(BF16)
        d_x = norm_back(to_keys(0, d_k), k_unit, k_inv, k_gain, scale)[0].astype(BF16)
        dk_o[lo, cols], dk_o[hi_all, cols] = d_x[lo], d_x[hh:]
        d_v = (to_keys(1, d_v) * s_ends).astype(BF16)
        dv_o[lo, cols], dv_o[hi_all, cols] = d_v[lo], d_v[hh:]

    def late_step(c, carry):
        for i in range(late_hpc // hpc):
            chunk = c * (late_hpc // hpc) + i
            for side, there in sides:
                @pl.when(there)
                def _():
                    arrival(take.at[side, :, :, columns(chunk)], back_sem.at[side], take_sem.at[side, chunk],
                            side).wait_recv()
        prepared = [late_prepare(c * late_hpc + j) for j in range(late_hpc)]
        results = attend([x for _, x in prepared], scale)
        for (ready, _), result in zip(prepared, results):
            late_conclude(ready, result)
        return carry

    lax.fori_loop(0, heads // late_hpc, late_step, 0)

    @pl.when(has_left)
    def _():
        arrival(near.at[1, 0:2], send_sem.at[0], recv_sem.at[1, 0], 0).wait_send()

    @pl.when(has_right)
    def _():
        arrival(near.at[0], send_sem.at[1], recv_sem.at[0, 0], 1).wait_send()
    for side, there in sides:
        @pl.when(there)
        def _():
            arrival(take.at[side], back_sem.at[side], take_sem.at[side, 0], side).wait_send()

    offset = 0
    for stage, (_, n) in enumerate(stages):
        if stage > 0:
            spread(stage, offset, total)
        total = gathered(stage, offset)
        offset += n
    gq_o[...] = total[0:1]
    gk_o[...] = total[1:2]


def store(*refs):
    n = len(refs) // 2
    sem = refs[-1]
    copies = [pltpu.make_async_copy(refs[i], refs[n + i], sem.at[i]) for i in range(n)]
    for x in copies:
        x.start()
    for x in copies:
        x.wait()


def local(queries, keys, values, v_scale, d_out, q_gain, k_gain, segment_ids):
    _, rows, cols = queries.shape
    hd = q_gain.shape[0]
    heads = cols // hd
    sizes = {a: lax.axis_size(a) for a in AXES}
    h = rows * sizes["inner"] // 8
    hpc = 3 if heads % 3 == 0 else 1
    nc = heads // hpc
    late_hpc = 2 * hpc if heads % (2 * hpc) == 0 else hpc
    flat = lambda x: x.reshape(rows, x.shape[2])
    vmem = pl.BlockSpec(memory_space=pltpu.VMEM)
    hbm = pl.BlockSpec(memory_space=pltpu.HBM)
    in_hbm = lambda x: pltpu.with_memory_space_constraint(x, pltpu.HBM)
    in_vmem = lambda x: pltpu.with_memory_space_constraint(x, pltpu.VMEM)
    big = jax.ShapeDtypeStruct((rows, cols), BF16)
    small = jax.ShapeDtypeStruct((1, hd), F32)
    stages = grouped(sizes)
    outs = pl.pallas_call(
        functools.partial(kernel, (sizes, rows, heads, hd, h, hpc, late_hpc)),
        out_shape=(big, big, big, big, small, small),
        in_specs=[hbm] * 8,
        out_specs=(vmem,) * 6,
        scratch_shapes=[
            pltpu.VMEM((rows, cols), BF16),
            pltpu.VMEM((rows, cols), BF16),
            pltpu.VMEM((rows, cols), BF16),
            pltpu.VMEM((rows, cols), BF16),
            pltpu.VMEM((heads, rows), BF16),
            pltpu.VMEM((1, hd), F32),
            pltpu.VMEM((1, hd), F32),
            pltpu.VMEM(segment_ids.shape, jnp.int32),
            pltpu.VMEM((rows, heads), BF16),
            pltpu.VMEM((2, 4, h // 2, cols), BF16),
            pltpu.VMEM((2, 4, h // 2, cols), BF16),
            pltpu.VMEM((2, 2, h // 2, cols), BF16),
            pltpu.VMEM((2, 2, h // 2, cols), BF16),
            pltpu.VMEM((2, h // 2, cols), F32),
            pltpu.VMEM((2, h + h // 2, cols), F32),
            pltpu.VMEM((rows + h, rows), F32),
            pltpu.VMEM((3 * h // 2, h // 2), F32),
            pltpu.VMEM((3 * h // 2, h // 2), F32),
            pltpu.VMEM((len(stages), 2, hd), F32),
            pltpu.VMEM((sum(n for _, n in stages), 2, hd), F32),
            pltpu.SemaphoreType.DMA((8,)),
            pltpu.SemaphoreType.DMA((2,)),
            pltpu.SemaphoreType.DMA((2, nc)),
            pltpu.SemaphoreType.DMA((2,)),
            pltpu.SemaphoreType.DMA((2, nc)),
            pltpu.SemaphoreType.REGULAR((len(rounds(sizes)) + 1,)),
            pltpu.SemaphoreType.DMA((len(stages),)),
            pltpu.SemaphoreType.DMA((len(stages),)),
        ],
        compiler_params=pltpu.CompilerParams(
            collective_id=0, has_side_effects=True, vmem_limit_bytes=32 << 20),
    )(*map(in_hbm, (flat(queries), flat(keys), flat(values), flat(v_scale).T, flat(d_out),
                    q_gain.reshape(1, hd), k_gain.reshape(1, hd), segment_ids)))
    outs = pl.pallas_call(
        store,
        out_shape=(big, big, big, big, small, small),
        in_specs=[vmem] * 6,
        out_specs=(hbm,) * 6,
        scratch_shapes=[pltpu.SemaphoreType.DMA((6,))],
    )(*map(in_vmem, outs))
    wide = tuple(x.reshape(1, rows, cols) for x in outs[:4])
    return wide + (outs[4].reshape(hd), outs[5].reshape(hd))


def solution(mesh):
    tokens = P("dp", ("blk", "inner"), None)
    return jax.shard_map(
        local,
        mesh=mesh,
        in_specs=(tokens,) * 5 + (P(), P(), P("dp", None)),
        out_specs=(tokens,) * 4 + (P(), P()),
        check_vma=False,
    )
```

```python
import functools
import math

import jax
import jax.numpy as jnp
from jax import lax
from jax.experimental import pallas as pl
from jax.experimental.pallas import tpu as pltpu
from jax.sharding import PartitionSpec as P

EPSILON = 1e-06
MESH = pl.DeviceIdType.MESH
AXES = ("dp", "blk", "inner")
F32 = jnp.float32
BF16 = jnp.bfloat16
NT = (((1,), (1,)), ((), ()))
NN = (((1,), (0,)), ((), ()))
TN = (((0,), (0,)), ((), ()))
OFF = -1e30
NO_QUERY = -9.0
NO_KEY = -7.0


def dot(a, b, dims):
    return lax.dot_general(a, b, dims, preferred_element_type=F32)


def unit(x):
    inverse = lax.rsqrt(jnp.mean(x * x, axis=-1, keepdims=True) + EPSILON)
    return x * inverse, inverse


def norm_back(d_norm, unit_rows, inverse, gain, scale):
    along = d_norm * unit_rows
    mean = jnp.mean(along * gain, axis=-1, keepdims=True)
    return (inverse * scale) * (d_norm * gain - unit_rows * mean), along


def attend(problems, scale):
    factor = scale * math.log2(math.e)
    scores = [dot(k_norm, q_norm, NT) for q_norm, k_norm, _, _, _ in problems]
    d_ws = [dot(v, g, NT) for _, _, v, g, _ in problems]
    es = [jnp.exp2(s * factor + p[4]) for s, p in zip(scores, problems)]
    totals = [jnp.sum(e, axis=0, keepdims=True) for e in es]
    ws = [e * (1.0 / jnp.where(t == 0.0, 1.0, t)) for e, t in zip(es, totals)]
    w_bs = [w.astype(BF16) for w in ws]
    outs = [dot(w_b, p[2], TN) for w_b, p in zip(w_bs, problems)]
    d_vs = [dot(w_b, p[3], NN) for w_b, p in zip(w_bs, problems)]
    dots = [jnp.sum(w * d_w, axis=0, keepdims=True) for w, d_w in zip(ws, d_ws)]
    d_ss = [(w * (d_w - o)).astype(BF16) for w, d_w, o in zip(ws, d_ws, dots)]
    d_qs = [dot(d_s, p[1], TN) for d_s, p in zip(d_ss, problems)]
    d_ks = [dot(d_s, p[0], NN) for d_s, p in zip(d_ss, problems)]
    return list(zip(outs, d_qs, d_ks, d_vs))


def to_column(row):
    n = row.shape[1]
    r = lax.broadcasted_iota(jnp.int32, (n, n), 0)
    c = lax.broadcasted_iota(jnp.int32, (n, n), 1)
    return jnp.sum(jnp.where(r == c, row, 0.0), axis=1, keepdims=True)


def transposed(x):
    n = x.shape[1]
    r = lax.broadcasted_iota(jnp.int32, (n, n), 0)
    c = lax.broadcasted_iota(jnp.int32, (n, n), 1)
    return dot((r == c).astype(F32).astype(BF16), x, NT)


def grouped(sizes):
    groups = []
    for axis in AXES:
        if groups and groups[-1][1] * sizes[axis] <= 32:
            groups[-1] = (groups[-1][0] + (axis,), groups[-1][1] * sizes[axis])
        else:
            groups.append(((axis,), sizes[axis]))
    return groups


def rounds(sizes):
    n, found, d = sizes["blk"] * sizes["inner"], [], 1
    while d < n:
        found.append(d)
        d *= 2
    return found


def kernel(cfg, q_hbm, k_hbm, v_hbm, s_hbm, g_hbm, qg_hbm, kg_hbm, seg_hbm,
           att_o, dq_o, dk_o, dv_o, gq_o, gk_o,
           qv, kv, vv, gv, s_ref, qg_ref, kg_ref, seg_ref, s_col, near, give, take, back,
           part_q, part_k, unit_q, unit_k, inv_q, inv_k, qn, kn, vd, kn_hi,
           bias_own, bias_edge, bias_hi, gsrc, gslot,
           load_sem, send_sem, recv_sem, back_sem, take_sem, here_sem, gsend, grecv):
    sizes, rows, heads, hd, h, hpc, own_hpc, late_hpc = cfg
    n_dp, n_blk, n_inner = (sizes[a] for a in AXES)
    nc = heads // hpc
    hh = h // 2
    width = hpc * hd
    scale = 1.0 / math.sqrt(hd)
    dp, blk, inner = (lax.axis_index(a) for a in AXES)
    p = blk * n_inner + inner
    n_line = n_blk * n_inner
    last = n_line - 1
    has_left, has_right = p > 0, p < last
    left, right = p - 1, p + 1
    first, final = inner == 0, inner == n_inner - 1
    ids = ({"blk": jnp.where(first, blk - 1, blk), "inner": jnp.where(first, n_inner - 1, inner - 1)},
           {"blk": jnp.where(final, blk + 1, blk), "inner": jnp.where(final, 0, inner + 1)})
    sides = ((0, has_left), (1, has_right))
    lo, hi = slice(0, hh), slice(rows - hh, rows)
    lo_in, hi_in = slice(hh, h), slice(rows - h, rows - hh)

    loads = [
        pltpu.make_async_copy(src, dst, load_sem.at[i])
        for i, (src, dst) in enumerate(((s_hbm, s_ref), (seg_hbm, seg_ref), (v_hbm, vv), (k_hbm, kv),
                                        (q_hbm, qv), (g_hbm, gv), (qg_hbm, qg_ref), (kg_hbm, kg_ref)))
    ]
    for c in loads:
        c.start()

    barrier = pltpu.get_barrier_semaphore()
    others = [jnp.where(dp + d >= n_dp, dp + d - n_dp, dp + d) for d in range(1, n_dp)]
    for side, there in sides:
        @pl.when(there)
        def _():
            pl.semaphore_signal(barrier, inc=1, device_id=ids[side], device_id_type=MESH)
    for other in others:
        pl.semaphore_signal(barrier, inc=1, device_id={"dp": other}, device_id_type=MESH)

    dists = rounds(sizes)

    def say_here(i):
        if i > 0:
            d = dists[i - 1]
            pl.semaphore_wait(here_sem.at[i - 1], (p >= d).astype(jnp.int32) + (p + d <= last).astype(jnp.int32))
        if i < len(dists):
            for pos, there in ((p - dists[i], p >= dists[i]), (p + dists[i], p + dists[i] <= last)):
                @pl.when(there)
                def _():
                    pl.semaphore_signal(here_sem.at[i], inc=1, device_id_type=MESH,
                                        device_id={"blk": pos // n_inner, "inner": lax.rem(pos, n_inner)})
        else:
            for other in others:
                pl.semaphore_signal(here_sem.at[i], inc=1, device_id={"dp": other}, device_id_type=MESH)

    loads[0].wait()
    s_f = transposed(s_ref[...])
    s_col[...] = s_f.astype(BF16)

    def seg_at(pos):
        start = pl.multiple_of(pos * rows, 128)
        return seg_ref[:, pl.ds(start, rows)].astype(F32)

    loads[1].wait()
    own = seg_at(p)
    prev = jnp.where(has_left, seg_at(jnp.maximum(left, 0)), -1.0)
    nxt = jnp.where(has_right, seg_at(jnp.minimum(right, last)), -2.0)

    def pick(row, index):
        return jnp.sum(row[:, index:index + 1], axis=1, keepdims=True)

    before, after = pick(prev, rows - 1), pick(nxt, 0)
    own_first, own_last = pick(own, 0), pick(own, rows - 1)
    long_lo = jnp.where(pick(own, hh) == before, 1.0, 0.0)
    long_hi = jnp.where(pick(own, rows - hh - 1) == after, 1.0, 0.0)
    short_lo = jnp.where(pick(prev, rows - hh - 1) == own_first, 1.0, 0.0)
    short_hi = jnp.where(pick(nxt, hh) == own_last, 1.0, 0.0)

    def over(x):
        return jnp.broadcast_to(x, (hh, hd)) > 0.5

    lo_is_long, hi_is_long = over(long_lo), over(long_hi)
    lo_is_short, hi_is_short = over(short_lo), over(short_hi)

    def columns(c):
        return pl.ds(pl.multiple_of(c * width, 128), width)

    def near_copy(side, c):
        cols = slice(c * width, (c + 1) * width)
        parts = slice(0, 2 + 2 * side)
        return pltpu.make_async_remote_copy(
            src_ref=give.at[side, parts, :, cols],
            dst_ref=near.at[1 - side, parts, :, cols],
            send_sem=send_sem.at[side],
            recv_sem=recv_sem.at[1 - side, c],
            device_id=ids[side],
            device_id_type=MESH,
        )

    def back_copy(side, c):
        return pltpu.make_async_remote_copy(
            src_ref=back.at[side, :, :, columns(c)],
            dst_ref=take.at[1 - side, :, :, columns(c)],
            send_sem=back_sem.at[side],
            recv_sem=take_sem.at[1 - side, c],
            device_id=ids[side],
            device_id_type=MESH,
        )

    def arrival(ref, send, recv, side):
        return pltpu.make_async_remote_copy(
            src_ref=ref, dst_ref=ref, send_sem=send, recv_sem=recv, device_id=ids[side], device_id_type=MESH)

    for c in loads[2:6]:
        c.wait()
    pl.semaphore_wait(barrier, has_left.astype(jnp.int32) + has_right.astype(jnp.int32) + (n_dp - 1))
    say_here(0)
    for c in range(nc):
        for head in range(c * hpc, (c + 1) * hpc):
            cols = slice(head * hd, (head + 1) * hd)
            for side, edge in ((0, lo), (1, hi)):
                give[side, 0, :, cols] = kv[edge, cols]
                give[side, 1, :, cols] = (vv[edge, cols].astype(F32) * s_f[edge, head:head + 1]).astype(BF16)
            give[1, 2, :, cols] = jnp.where(
                hi_is_long, kv[hi_in, cols].astype(F32), qv[hi, cols].astype(F32)).astype(BF16)
            give[1, 3, :, cols] = jnp.where(
                hi_is_long, vv[hi_in, cols].astype(F32) * s_f[hi_in, head:head + 1],
                gv[hi, cols].astype(F32)).astype(BF16)
        for side, there in sides:
            @pl.when(there)
            def _():
                near_copy(side, c).start()
    for side, there in sides:
        @pl.when(jnp.logical_not(there))
        def _():
            near[side] = jnp.zeros((4, hh, heads * hd), BF16)
            take[side] = jnp.zeros((2, hh, heads * hd), BF16)

    own_col, prev_col, nxt_col = to_column(own), to_column(prev), to_column(nxt)

    own_q = jnp.where((own == before) | (own == after), NO_QUERY, own)
    bias_own[...] = jnp.where(own_col == own_q, 0.0, OFF)

    split_lo, split_hi = own_first == before, own_last == after
    q_recv = jnp.where((prev[:, rows - hh:] == before) & split_lo & (short_lo < 0.5), prev[:, rows - hh:], NO_QUERY)
    q_lo = jnp.where(own[:, :h] == before, own[:, :h], NO_QUERY)
    q_hi = jnp.where((own[:, rows - h:] == after) & (short_hi < 0.5), own[:, rows - h:], NO_QUERY)
    k_far = jnp.where(short_lo > 0.5, prev_col[rows - h:rows - hh], NO_KEY)
    edge_q = jnp.concatenate([q_recv, q_lo, q_hi], axis=1)
    edge_k = jnp.concatenate(
        [k_far, prev_col[rows - hh:], own_col[:h], own_col[rows - h:], nxt_col[:hh]], axis=0)
    bias_edge[...] = jnp.where(edge_k == edge_q, 0.0, OFF)

    q_late = jnp.where(short_hi > 0.5, own[:, rows - hh:], nxt[:, :hh])
    q_late = jnp.where((q_late == after) & split_hi, q_late, NO_QUERY)
    k_late = jnp.where(short_hi > 0.5, nxt_col[hh:h], own_col[rows - h:rows - hh])
    hi_col = jnp.concatenate([own_col[rows - hh:], nxt_col[:hh], k_late], axis=0)
    bias_hi[...] = jnp.where(hi_col == q_late, 0.0, OFF)
    lo_far = jnp.broadcast_to(own_col[lo_in], (hh, hd)) == before
    lo_adds = over(jnp.where(own_col[:hh] == before, short_lo, 0.0))
    hi_adds = over(jnp.where(own_col[rows - hh:] == after, short_hi, 0.0))

    for c in loads[6:]:
        c.wait()
    q_gain, k_gain = qg_ref[...], kg_ref[...]
    which = lax.broadcasted_iota(jnp.int32, (heads, hd), 0)

    def scale_of(head, part):
        one = jnp.where(which == head, 1.0, 0.0).astype(BF16)
        return dot(s_col[part], one, NN)

    mid, hi_all = slice(h, rows - h), slice(rows - h, rows)
    hi_is_counted = jnp.broadcast_to(long_hi, (1, hd)) > 0.5

    def column_sum(x):
        return jnp.sum(x, axis=0, keepdims=True)

    def ends(x):
        return jnp.concatenate([x[:h], x[rows - h:]], axis=0)

    def columns_of(head):
        return pl.ds(pl.multiple_of(head * hd, 128), hd)

    def own_prepare(head):
        cols = columns_of(head)
        s_all = scale_of(head, slice(0, rows))
        v = (vv[:, cols].astype(F32) * s_all).astype(BF16)
        q_unit, q_inv = unit(qv[:, cols].astype(F32))
        k_unit, k_inv = unit(kv[:, cols].astype(F32))
        q_norm, k_norm = (q_unit * q_gain).astype(BF16), (k_unit * k_gain).astype(BF16)
        for ref, x in ((unit_q, q_unit), (unit_k, k_unit), (qn, q_norm), (kn, k_norm), (vd, v)):
            ref[:, cols] = ends(x)
        for ref, x in ((inv_q, q_inv), (inv_k, k_inv)):
            ref[:, cols] = jnp.broadcast_to(ends(x), (2 * h, hd))
        return (cols, s_all, q_unit, q_inv, k_unit, k_inv), (q_norm, k_norm, v, gv[:, cols], bias_own[...])

    def own_conclude(ready, result, acc):
        acc_q, acc_k = acc
        cols, s_all, q_unit, q_inv, k_unit, k_inv = ready
        out, d_q, d_k, d_v = result
        for ref, xs in ((part_q, (out, d_q)), (part_k, (d_k, d_v))):
            for i, x in enumerate(xs):
                ref[i, :, cols] = ends(x)
        if rows > 2 * h:
            att_o[mid, cols] = out[mid].astype(BF16)
            d_x, _ = norm_back(d_q[mid], q_unit[mid], q_inv[mid], q_gain, scale)
            dq_o[mid, cols] = d_x.astype(BF16)
            d_x, _ = norm_back(d_k[mid], k_unit[mid], k_inv[mid], k_gain, scale)
            dk_o[mid, cols] = d_x.astype(BF16)
            dv_o[mid, cols] = (d_v[mid] * s_all[mid]).astype(BF16)
        return acc_q + column_sum(d_q * q_unit), acc_k + column_sum(d_k * k_unit)

    n_own = heads // own_hpc

    def own_step(c, acc):
        prepared = [own_prepare(c * own_hpc + j) for j in range(own_hpc)]
        results = attend([x for _, x in prepared], scale)
        for (ready, _), result in zip(prepared, results):
            acc = own_conclude(ready, result, acc)
        for i in range(min(n_own, len(dists))):
            @pl.when(c == i)
            def _():
                say_here(i + 1)
        return acc

    zero = jnp.zeros((1, hd), F32)
    acc = lax.fori_loop(0, n_own, own_step, (zero, zero))

    def edge_prepare(head):
        cols = columns_of(head)
        near_u, _ = unit(jnp.concatenate([near[0, 0, :, cols], near[1, 0, :, cols]], axis=0).astype(F32))
        near_k = (near_u * k_gain).astype(BF16)
        far_u, _ = unit(near[0, 2, :, cols].astype(F32))
        kn_hi[:, cols] = near_k[hh:]
        k = jnp.concatenate([(far_u * k_gain).astype(BF16), near_k[:hh], kn[:, cols], near_k[hh:]], axis=0)
        v = jnp.concatenate([near[0, 3, :, cols], near[0, 1, :, cols], vd[:, cols], near[1, 1, :, cols]], axis=0)
        q = jnp.concatenate([(far_u * q_gain).astype(BF16), qn[:, cols]], axis=0)
        g = jnp.concatenate([near[0, 3, :, cols], gv[:h, cols], gv[hi_all, cols]], axis=0)
        return (cols, near_u, far_u), (q, k, v, g, bias_edge[...])

    def edge_conclude(ready, result, acc):
        acc_q, acc_k = acc
        cols, near_u, far_u = ready
        own_rows = slice(h, h + 2 * h)
        for i, (x, inward, edge) in enumerate(((result[2], kv[lo_in, cols], qv[lo, cols]),
                                               (result[3], vd[lo_in, cols], gv[lo, cols]))):
            back[0, i, :, cols] = jnp.where(
                lo_is_long, jnp.where(lo_far, inward.astype(F32), x[hh:h]), edge.astype(F32)).astype(BF16)
            back[1, i, :, cols] = x[3 * h:].astype(BF16)
            part_k[i, :, cols] += x[own_rows]
            part_q[i, :, cols] += result[i][hh:]
        d_q, d_k = result[1], result[2]
        along_q, along_k = d_q[hh:] * unit_q[:, cols], d_k[own_rows] * unit_k[:, cols]
        for_lo = (column_sum(d_q[:hh] * far_u) + column_sum(along_q[:h]),
                  column_sum(d_k[:hh] * far_u) + column_sum(d_k[hh:h] * near_u[:hh]) + column_sum(along_k[:h]))
        for_hi = (column_sum(along_q[h:]), column_sum(along_k[h:]) + column_sum(d_k[3 * h:] * near_u[hh:]))
        return tuple(a + x + jnp.where(hi_is_counted, y, 0.0) for a, x, y in zip(acc, for_lo, for_hi))

    rounds_at = list(range(nc))[:max(len(dists) - n_own, 0)]

    def edge_step(c, acc):
        for side, there in sides:
            @pl.when(there)
            def _():
                arrival(near.at[side, 0:4 - 2 * side, :, columns(c)], send_sem.at[side], recv_sem.at[side, c],
                        side).wait_recv()
        prepared = [edge_prepare(c * hpc + j) for j in range(hpc)]
        results = attend([x for _, x in prepared], scale)
        for (ready, _), result in zip(prepared, results):
            acc = edge_conclude(ready, result, acc)
        for side, there in sides:
            @pl.when(there)
            def _():
                back_copy(side, c).start()
        for i, at in enumerate(rounds_at):
            @pl.when(c == at)
            def _():
                say_here(n_own + i + 1)
        return acc

    acc_q, acc_k = lax.fori_loop(0, nc, edge_step, acc)
    for i in range(min(n_own, len(dists)) + len(rounds_at), len(dists)):
        say_here(i + 1)
    pl.semaphore_wait(here_sem.at[len(dists)], n_dp - 1)

    stages = grouped(sizes)
    me = {a: i for a, i in zip(AXES, (dp, blk, inner))}
    total = jnp.concatenate([acc_q, acc_k], axis=0) * scale

    def spread(stage, offset, total):
        axes, n = stages[stage]
        index = 0
        for axis in axes:
            index = index * sizes[axis] + me[axis]
        gsrc[stage] = total
        gslot[offset + index] = total
        for to in range(n):
            device, rest = {}, to
            for axis in reversed(axes):
                device[axis], rest = rest % sizes[axis], rest // sizes[axis]

            @pl.when(index != to)
            def _():
                pltpu.make_async_remote_copy(
                    src_ref=gsrc.at[stage], dst_ref=gslot.at[offset + index],
                    send_sem=gsend.at[stage], recv_sem=grecv.at[stage],
                    device_id=device, device_id_type=MESH).start()

    def gathered(stage, offset):
        axes, n = stages[stage]
        everything = gslot.at[pl.ds(offset, n - 1)]
        pltpu.make_async_remote_copy(
            src_ref=everything, dst_ref=everything,
            send_sem=gsend.at[stage], recv_sem=grecv.at[stage],
            device_id={axis: 0 for axis in axes}, device_id_type=MESH).wait()
        total = gslot[offset]
        for i in range(1, n):
            total = total + gslot[offset + i]
        return total

    spread(0, 0, total)

    q_done, k_done = slice(0, h + hh), slice(hh, h)

    def finish_step(c, carry):
        for j in range(late_hpc):
            head = c * late_hpc + j
            cols = columns_of(head)
            out = part_q[0, q_done, cols].astype(BF16)
            d_q = norm_back(part_q[1, q_done, cols], unit_q[q_done, cols], inv_q[q_done, cols], q_gain, scale)[0]
            d_q = d_q.astype(BF16)
            att_o[:h, cols], att_o[hi_in, cols] = out[:h], out[h:]
            dq_o[:h, cols], dq_o[hi_in, cols] = d_q[:h], d_q[h:]
            d_k = norm_back(part_k[0, k_done, cols], unit_k[k_done, cols], inv_k[k_done, cols], k_gain, scale)[0]
            dk_o[lo_in, cols] = d_k.astype(BF16)
            dv_o[lo_in, cols] = (part_k[1, k_done, cols] * scale_of(head, lo_in)).astype(BF16)
        return carry

    lax.fori_loop(0, heads // late_hpc, finish_step, 0)

    q_late, k_lo, k_hi = slice(h + hh, 2 * h), slice(0, hh), slice(h, 2 * h)

    def late_prepare(head):
        cols = columns_of(head)
        s_ends = jnp.concatenate([scale_of(head, lo), scale_of(head, hi_all)], axis=0)
        far_u, _ = unit(take[1, 0, :, cols].astype(F32))
        far_1 = take[1, 1, :, cols].astype(F32)
        q_e = (jnp.where(hi_is_short, unit_q[q_late, cols], far_u) * q_gain).astype(BF16)
        g_e = jnp.where(hi_is_short, gv[hi, cols].astype(F32), far_1).astype(BF16)
        k_x = (jnp.where(hi_is_short, far_u, unit_k[h:h + hh, cols]) * k_gain).astype(BF16)
        v_x = jnp.where(hi_is_short, far_1, vd[h:h + hh, cols].astype(F32)).astype(BF16)
        k_e = jnp.concatenate([kn[q_late, cols], kn_hi[:, cols], k_x], axis=0)
        v_e = jnp.concatenate([vd[q_late, cols], near[1, 1, :, cols], v_x], axis=0)
        return (cols, s_ends), (q_e, k_e, v_e, g_e, bias_hi[...])

    def late_conclude(ready, result):
        cols, s_ends = ready
        out, d_q, d_k, d_v = result

        def to_keys(i, e):
            from_lo, from_hi = take[0, i, :, cols].astype(F32), take[1, i, :, cols].astype(F32)
            return jnp.concatenate(
                [part_k[i, lo, cols] + jnp.where(lo_adds, from_lo, 0.0),
                 part_k[i, h:h + hh, cols] + jnp.where(hi_is_short, 0.0, e[h:]),
                 part_k[i, q_late, cols] + jnp.where(hi_is_short, jnp.where(hi_adds, from_hi, 0.0), e[:hh])], axis=0)

        def both(ref):
            return jnp.concatenate([ref[k_lo, cols], ref[k_hi, cols]], axis=0)

        att_o[hi, cols] = (part_q[0, q_late, cols] + jnp.where(hi_is_short, out, 0.0)).astype(BF16)
        d_q = part_q[1, q_late, cols] + jnp.where(hi_is_short, d_q, 0.0)
        dq_o[hi, cols] = norm_back(d_q, unit_q[q_late, cols], inv_q[q_late, cols], q_gain, scale)[0].astype(BF16)
        d_x = norm_back(to_keys(0, d_k), both(unit_k), both(inv_k), k_gain, scale)[0].astype(BF16)
        dk_o[lo, cols], dk_o[hi_all, cols] = d_x[lo], d_x[hh:]
        d_v = (to_keys(1, d_v) * s_ends).astype(BF16)
        dv_o[lo, cols], dv_o[hi_all, cols] = d_v[lo], d_v[hh:]

    def late_step(c, carry):
        for i in range(late_hpc // hpc):
            chunk = c * (late_hpc // hpc) + i
            for side, there in sides:
                @pl.when(there)
                def _():
                    arrival(take.at[side, :, :, columns(chunk)], back_sem.at[side], take_sem.at[side, chunk],
                            side).wait_recv()
        prepared = [late_prepare(c * late_hpc + j) for j in range(late_hpc)]
        results = attend([x for _, x in prepared], scale)
        for (ready, _), result in zip(prepared, results):
            late_conclude(ready, result)
        return carry

    lax.fori_loop(0, heads // late_hpc, late_step, 0)

    @pl.when(has_left)
    def _():
        arrival(near.at[1, 0:2], send_sem.at[0], recv_sem.at[1, 0], 0).wait_send()

    @pl.when(has_right)
    def _():
        arrival(near.at[0], send_sem.at[1], recv_sem.at[0, 0], 1).wait_send()
    for side, there in sides:
        @pl.when(there)
        def _():
            arrival(take.at[side], back_sem.at[side], take_sem.at[side, 0], side).wait_send()

    offset = 0
    for stage, (_, n) in enumerate(stages):
        if stage > 0:
            spread(stage, offset, total)
        total = gathered(stage, offset)
        offset += n
    gq_o[...] = total[0:1]
    gk_o[...] = total[1:2]


def store(*refs):
    n = len(refs) // 2
    sem = refs[-1]
    copies = [pltpu.make_async_copy(refs[i], refs[n + i], sem.at[i]) for i in range(n)]
    for x in copies:
        x.start()
    for x in copies:
        x.wait()


def local(queries, keys, values, v_scale, d_out, q_gain, k_gain, segment_ids):
    _, rows, cols = queries.shape
    hd = q_gain.shape[0]
    heads = cols // hd
    sizes = {a: lax.axis_size(a) for a in AXES}
    h = rows * sizes["inner"] // 8
    hpc = 4 if heads % 4 == 0 else 1
    nc = heads // hpc
    late_hpc = hpc
    own_hpc = 6 if heads % 6 == 0 else 1
    flat = lambda x: x.reshape(rows, x.shape[2])
    vmem = pl.BlockSpec(memory_space=pltpu.VMEM)
    hbm = pl.BlockSpec(memory_space=pltpu.HBM)
    in_hbm = lambda x: pltpu.with_memory_space_constraint(x, pltpu.HBM)
    in_vmem = lambda x: pltpu.with_memory_space_constraint(x, pltpu.VMEM)
    big = jax.ShapeDtypeStruct((rows, cols), BF16)
    small = jax.ShapeDtypeStruct((1, hd), F32)
    stages = grouped(sizes)
    outs = pl.pallas_call(
        functools.partial(kernel, (sizes, rows, heads, hd, h, hpc, own_hpc, late_hpc)),
        out_shape=(big, big, big, big, small, small),
        in_specs=[hbm] * 8,
        out_specs=(vmem,) * 6,
        scratch_shapes=[
            pltpu.VMEM((rows, cols), BF16),
            pltpu.VMEM((rows, cols), BF16),
            pltpu.VMEM((rows, cols), BF16),
            pltpu.VMEM((rows, cols), BF16),
            pltpu.VMEM((heads, rows), BF16),
            pltpu.VMEM((1, hd), F32),
            pltpu.VMEM((1, hd), F32),
            pltpu.VMEM(segment_ids.shape, jnp.int32),
            pltpu.VMEM((rows, heads), BF16),
            pltpu.VMEM((2, 4, h // 2, cols), BF16),
            pltpu.VMEM((2, 4, h // 2, cols), BF16),
            pltpu.VMEM((2, 2, h // 2, cols), BF16),
            pltpu.VMEM((2, 2, h // 2, cols), BF16),
            pltpu.VMEM((2, 2 * h, cols), F32),
            pltpu.VMEM((2, 2 * h, cols), F32),
            pltpu.VMEM((2 * h, cols), F32),
            pltpu.VMEM((2 * h, cols), F32),
            pltpu.VMEM((2 * h, cols), F32),
            pltpu.VMEM((2 * h, cols), F32),
            pltpu.VMEM((2 * h, cols), BF16),
            pltpu.VMEM((2 * h, cols), BF16),
            pltpu.VMEM((2 * h, cols), BF16),
            pltpu.VMEM((h // 2, cols), BF16),
            pltpu.VMEM((rows, rows), F32),
            pltpu.VMEM((7 * h // 2, 5 * h // 2), F32),
            pltpu.VMEM((3 * h // 2, h // 2), F32),
            pltpu.VMEM((len(stages), 2, hd), F32),
            pltpu.VMEM((sum(n for _, n in stages), 2, hd), F32),
            pltpu.SemaphoreType.DMA((8,)),
            pltpu.SemaphoreType.DMA((2,)),
            pltpu.SemaphoreType.DMA((2, nc)),
            pltpu.SemaphoreType.DMA((2,)),
            pltpu.SemaphoreType.DMA((2, nc)),
            pltpu.SemaphoreType.REGULAR((len(rounds(sizes)) + 1,)),
            pltpu.SemaphoreType.DMA((len(stages),)),
            pltpu.SemaphoreType.DMA((len(stages),)),
        ],
        compiler_params=pltpu.CompilerParams(
            collective_id=0, has_side_effects=True, vmem_limit_bytes=32 << 20),
    )(*map(in_hbm, (flat(queries), flat(keys), flat(values), flat(v_scale).T, flat(d_out),
                    q_gain.reshape(1, hd), k_gain.reshape(1, hd), segment_ids)))
    outs = pl.pallas_call(
        store,
        out_shape=(big, big, big, big, small, small),
        in_specs=[vmem] * 6,
        out_specs=(hbm,) * 6,
        scratch_shapes=[pltpu.SemaphoreType.DMA((6,))],
    )(*map(in_vmem, outs))
    wide = tuple(x.reshape(1, rows, cols) for x in outs[:4])
    return wide + (outs[4].reshape(hd), outs[5].reshape(hd))


def solution(mesh):
    tokens = P("dp", ("blk", "inner"), None)
    return jax.shard_map(
        local,
        mesh=mesh,
        in_specs=(tokens,) * 5 + (P(), P(), P("dp", None)),
        out_specs=(tokens,) * 4 + (P(), P()),
        check_vma=False,
    )
```

```python
import functools
import math

import jax
import jax.numpy as jnp
from jax import lax
from jax.experimental import pallas as pl
from jax.experimental.pallas import tpu as pltpu
from jax.sharding import PartitionSpec as P

EPSILON = 1e-06
MESH = pl.DeviceIdType.MESH
AXES = ("dp", "blk", "inner")
F32 = jnp.float32
BF16 = jnp.bfloat16
NT = (((1,), (1,)), ((), ()))
NN = (((1,), (0,)), ((), ()))
TN = (((0,), (0,)), ((), ()))
OFF = -1e30
NO_QUERY = -9.0
NO_KEY = -7.0


def dot(a, b, dims):
    return lax.dot_general(a, b, dims, preferred_element_type=F32)


def unit(x):
    inverse = lax.rsqrt(jnp.mean(x * x, axis=-1, keepdims=True) + EPSILON)
    return x * inverse, inverse


def norm_back(d_norm, unit_rows, inverse, gain, scale):
    along = d_norm * unit_rows
    mean = jnp.mean(along * gain, axis=-1, keepdims=True)
    return (inverse * scale) * (d_norm * gain - unit_rows * mean), along


def attend(problems, scale):
    factor = scale * math.log2(math.e)
    scores = [dot(k_norm, q_norm, NT) for q_norm, k_norm, _, _, _ in problems]
    d_ws = [dot(v, g, NT) for _, _, v, g, _ in problems]
    es = [jnp.exp2(s * factor + p[4]) for s, p in zip(scores, problems)]
    totals = [jnp.sum(e, axis=0, keepdims=True) for e in es]
    ws = [e * (1.0 / jnp.where(t == 0.0, 1.0, t)) for e, t in zip(es, totals)]
    w_bs = [w.astype(BF16) for w in ws]
    outs = [dot(w_b, p[2], TN) for w_b, p in zip(w_bs, problems)]
    d_vs = [dot(w_b, p[3], NN) for w_b, p in zip(w_bs, problems)]
    dots = [jnp.sum(w * d_w, axis=0, keepdims=True) for w, d_w in zip(ws, d_ws)]
    d_ss = [(w * (d_w - o)).astype(BF16) for w, d_w, o in zip(ws, d_ws, dots)]
    d_qs = [dot(d_s, p[1], TN) for d_s, p in zip(d_ss, problems)]
    d_ks = [dot(d_s, p[0], NN) for d_s, p in zip(d_ss, problems)]
    return list(zip(outs, d_qs, d_ks, d_vs))


def to_column(row):
    n = row.shape[1]
    r = lax.broadcasted_iota(jnp.int32, (n, n), 0)
    c = lax.broadcasted_iota(jnp.int32, (n, n), 1)
    return jnp.sum(jnp.where(r == c, row, 0.0), axis=1, keepdims=True)


def transposed(x):
    n = x.shape[1]
    r = lax.broadcasted_iota(jnp.int32, (n, n), 0)
    c = lax.broadcasted_iota(jnp.int32, (n, n), 1)
    return dot((r == c).astype(F32).astype(BF16), x, NT)


def grouped(sizes):
    groups = []
    for axis in AXES:
        if groups and groups[-1][1] * sizes[axis] <= 32:
            groups[-1] = (groups[-1][0] + (axis,), groups[-1][1] * sizes[axis])
        else:
            groups.append(((axis,), sizes[axis]))
    return groups


def rounds(sizes):
    n, found, d = sizes["blk"] * sizes["inner"], [], 1
    while d < n:
        found.append(d)
        d *= 2
    return found


def kernel(cfg, q_hbm, k_hbm, v_hbm, s_hbm, g_hbm, qg_hbm, kg_hbm, seg_hbm,
           att_o, dq_o, dk_o, dv_o, gq_o, gk_o,
           qv, kv, vv, gv, s_ref, qg_ref, kg_ref, seg_ref, s_col, near, give, take, back,
           part_q, part_k, unit_q, unit_k, inv_q, inv_k, qn, kn, vd, kn_hi,
           bias_own, bias_edge, bias_hi, gsrc, gslot,
           load_sem, send_sem, recv_sem, back_sem, take_sem, here_sem, gsend, grecv):
    sizes, rows, heads, hd, h, hpc, own_hpc, late_hpc = cfg
    n_dp, n_blk, n_inner = (sizes[a] for a in AXES)
    nc = heads // hpc
    hh = h // 2
    width = hpc * hd
    scale = 1.0 / math.sqrt(hd)
    dp, blk, inner = (lax.axis_index(a) for a in AXES)
    p = blk * n_inner + inner
    n_line = n_blk * n_inner
    last = n_line - 1
    has_left, has_right = p > 0, p < last
    left, right = p - 1, p + 1
    first, final = inner == 0, inner == n_inner - 1
    ids = ({"blk": jnp.where(first, blk - 1, blk), "inner": jnp.where(first, n_inner - 1, inner - 1)},
           {"blk": jnp.where(final, blk + 1, blk), "inner": jnp.where(final, 0, inner + 1)})
    sides = ((0, has_left), (1, has_right))
    lo, hi = slice(0, hh), slice(rows - hh, rows)
    lo_in, hi_in = slice(hh, h), slice(rows - h, rows - hh)

    loads = [
        pltpu.make_async_copy(src, dst, load_sem.at[i])
        for i, (src, dst) in enumerate(((s_hbm, s_ref), (seg_hbm, seg_ref), (v_hbm, vv), (k_hbm, kv),
                                        (q_hbm, qv), (g_hbm, gv), (qg_hbm, qg_ref), (kg_hbm, kg_ref)))
    ]
    for c in loads:
        c.start()

    barrier = pltpu.get_barrier_semaphore()
    others = [jnp.where(dp + d >= n_dp, dp + d - n_dp, dp + d) for d in range(1, n_dp)]
    for side, there in sides:
        @pl.when(there)
        def _():
            pl.semaphore_signal(barrier, inc=1, device_id=ids[side], device_id_type=MESH)
    for other in others:
        pl.semaphore_signal(barrier, inc=1, device_id={"dp": other}, device_id_type=MESH)

    dists = rounds(sizes)

    def say_here(i):
        if i > 0:
            d = dists[i - 1]
            pl.semaphore_wait(here_sem.at[i - 1], (p >= d).astype(jnp.int32) + (p + d <= last).astype(jnp.int32))
        if i < len(dists):
            for pos, there in ((p - dists[i], p >= dists[i]), (p + dists[i], p + dists[i] <= last)):
                @pl.when(there)
                def _():
                    pl.semaphore_signal(here_sem.at[i], inc=1, device_id_type=MESH,
                                        device_id={"blk": pos // n_inner, "inner": lax.rem(pos, n_inner)})
        else:
            for other in others:
                pl.semaphore_signal(here_sem.at[i], inc=1, device_id={"dp": other}, device_id_type=MESH)

    loads[0].wait()
    s_f = transposed(s_ref[...])
    s_col[...] = s_f.astype(BF16)

    def seg_at(pos):
        start = pl.multiple_of(pos * rows, 128)
        return seg_ref[:, pl.ds(start, rows)].astype(F32)

    loads[1].wait()
    own = seg_at(p)
    prev = jnp.where(has_left, seg_at(jnp.maximum(left, 0)), -1.0)
    nxt = jnp.where(has_right, seg_at(jnp.minimum(right, last)), -2.0)

    def pick(row, index):
        return jnp.sum(row[:, index:index + 1], axis=1, keepdims=True)

    before, after = pick(prev, rows - 1), pick(nxt, 0)
    own_first, own_last = pick(own, 0), pick(own, rows - 1)
    long_lo = jnp.where(pick(own, hh) == before, 1.0, 0.0)
    long_hi = jnp.where(pick(own, rows - hh - 1) == after, 1.0, 0.0)
    short_lo = jnp.where(pick(prev, rows - hh - 1) == own_first, 1.0, 0.0)
    short_hi = jnp.where(pick(nxt, hh) == own_last, 1.0, 0.0)

    def over(x):
        return jnp.broadcast_to(x, (hh, hd)) > 0.5

    lo_is_long, hi_is_long = over(long_lo), over(long_hi)
    lo_is_short, hi_is_short = over(short_lo), over(short_hi)

    def columns(c):
        return pl.ds(pl.multiple_of(c * width, 128), width)

    def near_copy(side, c):
        cols = slice(c * width, (c + 1) * width)
        parts = slice(0, 2 + 2 * side)
        return pltpu.make_async_remote_copy(
            src_ref=give.at[side, parts, :, cols],
            dst_ref=near.at[1 - side, parts, :, cols],
            send_sem=send_sem.at[side],
            recv_sem=recv_sem.at[1 - side, c],
            device_id=ids[side],
            device_id_type=MESH,
        )

    def back_copy(side, c):
        return pltpu.make_async_remote_copy(
            src_ref=back.at[side, :, :, columns(c)],
            dst_ref=take.at[1 - side, :, :, columns(c)],
            send_sem=back_sem.at[side],
            recv_sem=take_sem.at[1 - side, c],
            device_id=ids[side],
            device_id_type=MESH,
        )

    def arrival(ref, send, recv, side):
        return pltpu.make_async_remote_copy(
            src_ref=ref, dst_ref=ref, send_sem=send, recv_sem=recv, device_id=ids[side], device_id_type=MESH)

    for c in loads[2:6]:
        c.wait()
    pl.semaphore_wait(barrier, has_left.astype(jnp.int32) + has_right.astype(jnp.int32) + (n_dp - 1))
    say_here(0)
    for c in range(nc):
        for head in range(c * hpc, (c + 1) * hpc):
            cols = slice(head * hd, (head + 1) * hd)
            for side, edge in ((0, lo), (1, hi)):
                give[side, 0, :, cols] = kv[edge, cols]
                give[side, 1, :, cols] = (vv[edge, cols].astype(F32) * s_f[edge, head:head + 1]).astype(BF16)
            give[1, 2, :, cols] = jnp.where(
                hi_is_long, kv[hi_in, cols].astype(F32), qv[hi, cols].astype(F32)).astype(BF16)
            give[1, 3, :, cols] = jnp.where(
                hi_is_long, vv[hi_in, cols].astype(F32) * s_f[hi_in, head:head + 1],
                gv[hi, cols].astype(F32)).astype(BF16)
        for side, there in sides:
            @pl.when(there)
            def _():
                near_copy(side, c).start()
    for side, there in sides:
        @pl.when(jnp.logical_not(there))
        def _():
            near[side] = jnp.zeros((4, hh, heads * hd), BF16)
            take[side] = jnp.zeros((2, hh, heads * hd), BF16)

    own_col, prev_col, nxt_col = to_column(own), to_column(prev), to_column(nxt)

    own_q = jnp.where((own == before) | (own == after), NO_QUERY, own)
    bias_own[...] = jnp.where(own_col == own_q, 0.0, OFF)

    split_lo, split_hi = own_first == before, own_last == after
    q_recv = jnp.where((prev[:, rows - hh:] == before) & split_lo & (short_lo < 0.5), prev[:, rows - hh:], NO_QUERY)
    q_lo = jnp.where(own[:, :h] == before, own[:, :h], NO_QUERY)
    q_hi = jnp.where((own[:, rows - h:] == after) & (short_hi < 0.5), own[:, rows - h:], NO_QUERY)
    k_far = jnp.where(short_lo > 0.5, prev_col[rows - h:rows - hh], NO_KEY)
    edge_q = jnp.concatenate([q_recv, q_lo, q_hi], axis=1)
    edge_k = jnp.concatenate(
        [k_far, prev_col[rows - hh:], own_col[:h], own_col[rows - h:], nxt_col[:hh]], axis=0)
    bias_edge[...] = jnp.where(edge_k == edge_q, 0.0, OFF)

    q_late = jnp.where(short_hi > 0.5, own[:, rows - hh:], nxt[:, :hh])
    q_late = jnp.where((q_late == after) & split_hi, q_late, NO_QUERY)
    k_late = jnp.where(short_hi > 0.5, nxt_col[hh:h], own_col[rows - h:rows - hh])
    hi_col = jnp.concatenate([own_col[rows - hh:], nxt_col[:hh], k_late], axis=0)
    bias_hi[...] = jnp.where(hi_col == q_late, 0.0, OFF)
    lo_far = jnp.broadcast_to(own_col[lo_in], (hh, hd)) == before
    lo_adds = over(jnp.where(own_col[:hh] == before, short_lo, 0.0))
    hi_adds = over(jnp.where(own_col[rows - hh:] == after, short_hi, 0.0))

    for c in loads[6:]:
        c.wait()
    q_gain, k_gain = qg_ref[...], kg_ref[...]
    which = lax.broadcasted_iota(jnp.int32, (heads, hd), 0)

    def scale_of(head, part):
        one = jnp.where(which == head, 1.0, 0.0).astype(BF16)
        return dot(s_col[part], one, NN)

    mid, hi_all = slice(h, rows - h), slice(rows - h, rows)
    hi_is_counted = jnp.broadcast_to(long_hi, (1, hd)) > 0.5

    def column_sum(x):
        return jnp.sum(x, axis=0, keepdims=True)

    def ends(x):
        return jnp.concatenate([x[:h], x[rows - h:]], axis=0)

    def columns_of(head):
        return pl.ds(pl.multiple_of(head * hd, 128), hd)

    def own_prepare(head):
        cols = columns_of(head)
        s_all = scale_of(head, slice(0, rows))
        v = (vv[:, cols].astype(F32) * s_all).astype(BF16)
        q_unit, q_inv = unit(qv[:, cols].astype(F32))
        k_unit, k_inv = unit(kv[:, cols].astype(F32))
        q_norm, k_norm = (q_unit * q_gain).astype(BF16), (k_unit * k_gain).astype(BF16)
        for ref, x in ((unit_q, q_unit), (unit_k, k_unit), (qn, q_norm), (kn, k_norm), (vd, v)):
            ref[:, cols] = ends(x)
        for ref, x in ((inv_q, q_inv), (inv_k, k_inv)):
            ref[:, cols] = jnp.broadcast_to(ends(x), (2 * h, hd))
        return (cols, s_all, q_unit, q_inv, k_unit, k_inv), (q_norm, k_norm, v, gv[:, cols], bias_own[...])

    def own_conclude(ready, result, acc):
        acc_q, acc_k = acc
        cols, s_all, q_unit, q_inv, k_unit, k_inv = ready
        out, d_q, d_k, d_v = result
        for ref, xs in ((part_q, (out, d_q)), (part_k, (d_k, d_v))):
            for i, x in enumerate(xs):
                ref[i, :, cols] = ends(x)
        if rows > 2 * h:
            att_o[mid, cols] = out[mid].astype(BF16)
            d_x, _ = norm_back(d_q[mid], q_unit[mid], q_inv[mid], q_gain, scale)
            dq_o[mid, cols] = d_x.astype(BF16)
            d_x, _ = norm_back(d_k[mid], k_unit[mid], k_inv[mid], k_gain, scale)
            dk_o[mid, cols] = d_x.astype(BF16)
            dv_o[mid, cols] = (d_v[mid] * s_all[mid]).astype(BF16)
        return acc_q + column_sum(d_q * q_unit), acc_k + column_sum(d_k * k_unit)

    n_own = heads // own_hpc

    def own_step(c, acc):
        prepared = [own_prepare(c * own_hpc + j) for j in range(own_hpc)]
        results = attend([x for _, x in prepared], scale)
        for (ready, _), result in zip(prepared, results):
            acc = own_conclude(ready, result, acc)
        for i in range(min(n_own, len(dists))):
            @pl.when(c == i)
            def _():
                say_here(i + 1)
        return acc

    zero = jnp.zeros((1, hd), F32)
    acc = lax.fori_loop(0, n_own, own_step, (zero, zero))

    def edge_prepare(head):
        cols = columns_of(head)
        near_u, _ = unit(jnp.concatenate([near[0, 0, :, cols], near[1, 0, :, cols]], axis=0).astype(F32))
        near_k = (near_u * k_gain).astype(BF16)
        far_u, _ = unit(near[0, 2, :, cols].astype(F32))
        kn_hi[:, cols] = near_k[hh:]
        k = jnp.concatenate([(far_u * k_gain).astype(BF16), near_k[:hh], kn[:, cols], near_k[hh:]], axis=0)
        v = jnp.concatenate([near[0, 3, :, cols], near[0, 1, :, cols], vd[:, cols], near[1, 1, :, cols]], axis=0)
        q = jnp.concatenate([(far_u * q_gain).astype(BF16), qn[:, cols]], axis=0)
        g = jnp.concatenate([near[0, 3, :, cols], gv[:h, cols], gv[hi_all, cols]], axis=0)
        return (cols, near_u, far_u), (q, k, v, g, bias_edge[...])

    def edge_conclude(ready, result, acc):
        acc_q, acc_k = acc
        cols, near_u, far_u = ready
        own_rows = slice(h, h + 2 * h)
        for i, (x, inward, edge) in enumerate(((result[2], kv[lo_in, cols], qv[lo, cols]),
                                               (result[3], vd[lo_in, cols], gv[lo, cols]))):
            back[0, i, :, cols] = jnp.where(
                lo_is_long, jnp.where(lo_far, inward.astype(F32), x[hh:h]), edge.astype(F32)).astype(BF16)
            back[1, i, :, cols] = x[3 * h:].astype(BF16)
            part_k[i, :, cols] += x[own_rows]
            part_q[i, :, cols] += result[i][hh:]
        d_q, d_k = result[1], result[2]
        along_q, along_k = d_q[hh:] * unit_q[:, cols], d_k[own_rows] * unit_k[:, cols]
        for_lo = (column_sum(d_q[:hh] * far_u) + column_sum(along_q[:h]),
                  column_sum(d_k[:hh] * far_u) + column_sum(d_k[hh:h] * near_u[:hh]) + column_sum(along_k[:h]))
        for_hi = (column_sum(along_q[h:]), column_sum(along_k[h:]) + column_sum(d_k[3 * h:] * near_u[hh:]))
        return tuple(a + x + jnp.where(hi_is_counted, y, 0.0) for a, x, y in zip(acc, for_lo, for_hi))

    rounds_at = list(range(nc))[:max(len(dists) - n_own, 0)]

    def edge_step(c, acc):
        for side, there in sides:
            @pl.when(there)
            def _():
                arrival(near.at[side, 0:4 - 2 * side, :, columns(c)], send_sem.at[side], recv_sem.at[side, c],
                        side).wait_recv()
        prepared = [edge_prepare(c * hpc + j) for j in range(hpc)]
        results = attend([x for _, x in prepared], scale)
        for (ready, _), result in zip(prepared, results):
            acc = edge_conclude(ready, result, acc)
        for i, at in enumerate(rounds_at):
            @pl.when(c == at)
            def _():
                say_here(n_own + i + 1)
        return acc

    acc_q, acc_k = lax.fori_loop(0, nc, edge_step, acc)
    for i in range(min(n_own, len(dists)) + len(rounds_at), len(dists)):
        say_here(i + 1)
    pl.semaphore_wait(here_sem.at[len(dists)], n_dp - 1)

    stages = grouped(sizes)
    me = {a: i for a, i in zip(AXES, (dp, blk, inner))}
    total = jnp.concatenate([acc_q, acc_k], axis=0) * scale

    def devices(stage):
        axes, n = stages[stage]
        for to in range(n):
            device, rest = {}, to
            for axis in reversed(axes):
                device[axis], rest = rest % sizes[axis], rest // sizes[axis]
            yield to, device

    def spread(stage, offset, total, between=None):
        axes, n = stages[stage]
        index = 0
        for axis in axes:
            index = index * sizes[axis] + me[axis]
        gsrc[stage] = total
        gslot[offset + index] = total
        order = sorted(devices(stage), key=lambda x: [x[1].get(a, 0) for a in ("blk", "inner", "dp")])
        for i, (to, device) in enumerate(order):
            if between is not None and i == n // 2:
                between()

            @pl.when(index != to)
            def _():
                pltpu.make_async_remote_copy(
                    src_ref=gsrc.at[stage], dst_ref=gslot.at[offset + index],
                    send_sem=gsend.at[stage], recv_sem=grecv.at[stage],
                    device_id=device, device_id_type=MESH).start()

    def gathered(stage, offset):
        axes, n = stages[stage]
        everything = gslot.at[pl.ds(offset, n - 1)]
        pltpu.make_async_remote_copy(
            src_ref=everything, dst_ref=everything,
            send_sem=gsend.at[stage], recv_sem=grecv.at[stage],
            device_id={axis: 0 for axis in axes}, device_id_type=MESH).wait()
        total = gslot[offset]
        for i in range(1, n):
            total = total + gslot[offset + i]
        return total

    def send_back():
        for c in range(nc):
            for side, there in sides:
                @pl.when(there)
                def _():
                    back_copy(side, c).start()

    spread(0, 0, total, send_back)

    q_done, k_done = slice(0, h + hh), slice(hh, h)

    def finish_step(c, carry):
        for j in range(late_hpc):
            head = c * late_hpc + j
            cols = columns_of(head)
            out = part_q[0, q_done, cols].astype(BF16)
            d_q = norm_back(part_q[1, q_done, cols], unit_q[q_done, cols], inv_q[q_done, cols], q_gain, scale)[0]
            d_q = d_q.astype(BF16)
            att_o[:h, cols], att_o[hi_in, cols] = out[:h], out[h:]
            dq_o[:h, cols], dq_o[hi_in, cols] = d_q[:h], d_q[h:]
            d_k = norm_back(part_k[0, k_done, cols], unit_k[k_done, cols], inv_k[k_done, cols], k_gain, scale)[0]
            dk_o[lo_in, cols] = d_k.astype(BF16)
            dv_o[lo_in, cols] = (part_k[1, k_done, cols] * scale_of(head, lo_in)).astype(BF16)
        return carry

    lax.fori_loop(0, heads // late_hpc, finish_step, 0)

    q_late, k_lo, k_hi = slice(h + hh, 2 * h), slice(0, hh), slice(h, 2 * h)

    def late_prepare(head):
        cols = columns_of(head)
        s_ends = jnp.concatenate([scale_of(head, lo), scale_of(head, hi_all)], axis=0)
        far_u, _ = unit(take[1, 0, :, cols].astype(F32))
        far_1 = take[1, 1, :, cols].astype(F32)
        q_e = (jnp.where(hi_is_short, unit_q[q_late, cols], far_u) * q_gain).astype(BF16)
        g_e = jnp.where(hi_is_short, gv[hi, cols].astype(F32), far_1).astype(BF16)
        k_x = (jnp.where(hi_is_short, far_u, unit_k[h:h + hh, cols]) * k_gain).astype(BF16)
        v_x = jnp.where(hi_is_short, far_1, vd[h:h + hh, cols].astype(F32)).astype(BF16)
        k_e = jnp.concatenate([kn[q_late, cols], kn_hi[:, cols], k_x], axis=0)
        v_e = jnp.concatenate([vd[q_late, cols], near[1, 1, :, cols], v_x], axis=0)
        return (cols, s_ends), (q_e, k_e, v_e, g_e, bias_hi[...])

    def late_conclude(ready, result):
        cols, s_ends = ready
        out, d_q, d_k, d_v = result

        def to_keys(i, e):
            from_lo, from_hi = take[0, i, :, cols].astype(F32), take[1, i, :, cols].astype(F32)
            return jnp.concatenate(
                [part_k[i, lo, cols] + jnp.where(lo_adds, from_lo, 0.0),
                 part_k[i, h:h + hh, cols] + jnp.where(hi_is_short, 0.0, e[h:]),
                 part_k[i, q_late, cols] + jnp.where(hi_is_short, jnp.where(hi_adds, from_hi, 0.0), e[:hh])], axis=0)

        def both(ref):
            return jnp.concatenate([ref[k_lo, cols], ref[k_hi, cols]], axis=0)

        att_o[hi, cols] = (part_q[0, q_late, cols] + jnp.where(hi_is_short, out, 0.0)).astype(BF16)
        d_q = part_q[1, q_late, cols] + jnp.where(hi_is_short, d_q, 0.0)
        dq_o[hi, cols] = norm_back(d_q, unit_q[q_late, cols], inv_q[q_late, cols], q_gain, scale)[0].astype(BF16)
        d_x = norm_back(to_keys(0, d_k), both(unit_k), both(inv_k), k_gain, scale)[0].astype(BF16)
        dk_o[lo, cols], dk_o[hi_all, cols] = d_x[lo], d_x[hh:]
        d_v = (to_keys(1, d_v) * s_ends).astype(BF16)
        dv_o[lo, cols], dv_o[hi_all, cols] = d_v[lo], d_v[hh:]

    def late_step(c, carry):
        for i in range(late_hpc // hpc):
            chunk = c * (late_hpc // hpc) + i
            for side, there in sides:
                @pl.when(there)
                def _():
                    arrival(take.at[side, :, :, columns(chunk)], back_sem.at[side], take_sem.at[side, chunk],
                            side).wait_recv()
        prepared = [late_prepare(c * late_hpc + j) for j in range(late_hpc)]
        results = attend([x for _, x in prepared], scale)
        for (ready, _), result in zip(prepared, results):
            late_conclude(ready, result)
        return carry

    lax.fori_loop(0, heads // late_hpc, late_step, 0)

    @pl.when(has_left)
    def _():
        arrival(near.at[1, 0:2], send_sem.at[0], recv_sem.at[1, 0], 0).wait_send()

    @pl.when(has_right)
    def _():
        arrival(near.at[0], send_sem.at[1], recv_sem.at[0, 0], 1).wait_send()
    for side, there in sides:
        @pl.when(there)
        def _():
            arrival(take.at[side], back_sem.at[side], take_sem.at[side, 0], side).wait_send()

    offset = 0
    for stage, (_, n) in enumerate(stages):
        if stage > 0:
            spread(stage, offset, total)
        total = gathered(stage, offset)
        offset += n
    gq_o[...] = total[0:1]
    gk_o[...] = total[1:2]


def store(*refs):
    n = len(refs) // 2
    sem = refs[-1]
    copies = [pltpu.make_async_copy(refs[i], refs[n + i], sem.at[i]) for i in range(n)]
    for x in copies:
        x.start()
    for x in copies:
        x.wait()


def local(queries, keys, values, v_scale, d_out, q_gain, k_gain, segment_ids):
    _, rows, cols = queries.shape
    hd = q_gain.shape[0]
    heads = cols // hd
    sizes = {a: lax.axis_size(a) for a in AXES}
    h = rows * sizes["inner"] // 8
    hpc = 4 if heads % 4 == 0 else 1
    nc = heads // hpc
    late_hpc = hpc
    own_hpc = 6 if heads % 6 == 0 else 1
    flat = lambda x: x.reshape(rows, x.shape[2])
    vmem = pl.BlockSpec(memory_space=pltpu.VMEM)
    hbm = pl.BlockSpec(memory_space=pltpu.HBM)
    in_hbm = lambda x: pltpu.with_memory_space_constraint(x, pltpu.HBM)
    in_vmem = lambda x: pltpu.with_memory_space_constraint(x, pltpu.VMEM)
    big = jax.ShapeDtypeStruct((rows, cols), BF16)
    small = jax.ShapeDtypeStruct((1, hd), F32)
    stages = grouped(sizes)
    outs = pl.pallas_call(
        functools.partial(kernel, (sizes, rows, heads, hd, h, hpc, own_hpc, late_hpc)),
        out_shape=(big, big, big, big, small, small),
        in_specs=[hbm] * 8,
        out_specs=(vmem,) * 6,
        scratch_shapes=[
            pltpu.VMEM((rows, cols), BF16),
            pltpu.VMEM((rows, cols), BF16),
            pltpu.VMEM((rows, cols), BF16),
            pltpu.VMEM((rows, cols), BF16),
            pltpu.VMEM((heads, rows), BF16),
            pltpu.VMEM((1, hd), F32),
            pltpu.VMEM((1, hd), F32),
            pltpu.VMEM(segment_ids.shape, jnp.int32),
            pltpu.VMEM((rows, heads), BF16),
            pltpu.VMEM((2, 4, h // 2, cols), BF16),
            pltpu.VMEM((2, 4, h // 2, cols), BF16),
            pltpu.VMEM((2, 2, h // 2, cols), BF16),
            pltpu.VMEM((2, 2, h // 2, cols), BF16),
            pltpu.VMEM((2, 2 * h, cols), F32),
            pltpu.VMEM((2, 2 * h, cols), F32),
            pltpu.VMEM((2 * h, cols), F32),
            pltpu.VMEM((2 * h, cols), F32),
            pltpu.VMEM((2 * h, cols), F32),
            pltpu.VMEM((2 * h, cols), F32),
            pltpu.VMEM((2 * h, cols), BF16),
            pltpu.VMEM((2 * h, cols), BF16),
            pltpu.VMEM((2 * h, cols), BF16),
            pltpu.VMEM((h // 2, cols), BF16),
            pltpu.VMEM((rows, rows), F32),
            pltpu.VMEM((7 * h // 2, 5 * h // 2), F32),
            pltpu.VMEM((3 * h // 2, h // 2), F32),
            pltpu.VMEM((len(stages), 2, hd), F32),
            pltpu.VMEM((sum(n for _, n in stages), 2, hd), F32),
            pltpu.SemaphoreType.DMA((8,)),
            pltpu.SemaphoreType.DMA((2,)),
            pltpu.SemaphoreType.DMA((2, nc)),
            pltpu.SemaphoreType.DMA((2,)),
            pltpu.SemaphoreType.DMA((2, nc)),
            pltpu.SemaphoreType.REGULAR((len(rounds(sizes)) + 1,)),
            pltpu.SemaphoreType.DMA((len(stages),)),
            pltpu.SemaphoreType.DMA((len(stages),)),
        ],
        compiler_params=pltpu.CompilerParams(
            collective_id=0, has_side_effects=True, vmem_limit_bytes=32 << 20),
    )(*map(in_hbm, (flat(queries), flat(keys), flat(values), flat(v_scale).T, flat(d_out),
                    q_gain.reshape(1, hd), k_gain.reshape(1, hd), segment_ids)))
    outs = pl.pallas_call(
        store,
        out_shape=(big, big, big, big, small, small),
        in_specs=[vmem] * 6,
        out_specs=(hbm,) * 6,
        scratch_shapes=[pltpu.SemaphoreType.DMA((6,))],
    )(*map(in_vmem, outs))
    wide = tuple(x.reshape(1, rows, cols) for x in outs[:4])
    return wide + (outs[4].reshape(hd), outs[5].reshape(hd))


def solution(mesh):
    tokens = P("dp", ("blk", "inner"), None)
    return jax.shard_map(
        local,
        mesh=mesh,
        in_specs=(tokens,) * 5 + (P(), P(), P("dp", None)),
        out_specs=(tokens,) * 4 + (P(), P()),
        check_vma=False,
    )
```

```python
import functools
import math

import jax
import jax.numpy as jnp
from jax import lax
from jax.experimental import pallas as pl
from jax.experimental.pallas import tpu as pltpu
from jax.sharding import PartitionSpec as P

EPSILON = 1e-06
MESH = pl.DeviceIdType.MESH
AXES = ("dp", "blk", "inner")
F32 = jnp.float32
BF16 = jnp.bfloat16
NT = (((1,), (1,)), ((), ()))
NN = (((1,), (0,)), ((), ()))
TN = (((0,), (0,)), ((), ()))
OFF = -1e30
NO_QUERY = -9.0
NO_KEY = -7.0


def dot(a, b, dims):
    return lax.dot_general(a, b, dims, preferred_element_type=F32)


def unit(x):
    inverse = lax.rsqrt(jnp.mean(x * x, axis=-1, keepdims=True) + EPSILON)
    return x * inverse, inverse


def norm_back(d_norm, unit_rows, inverse, gain, scale):
    along = d_norm * unit_rows
    mean = jnp.mean(along * gain, axis=-1, keepdims=True)
    return (inverse * scale) * (d_norm * gain - unit_rows * mean), along


def attend(problems, scale):
    factor = scale * math.log2(math.e)
    scores = [dot(k_norm, q_norm, NT) for q_norm, k_norm, _, _, _ in problems]
    d_ws = [dot(v, g, NT) for _, _, v, g, _ in problems]
    es = [jnp.exp2(s * factor + p[4]) for s, p in zip(scores, problems)]
    totals = [jnp.sum(e, axis=0, keepdims=True) for e in es]
    ws = [e * (1.0 / jnp.where(t == 0.0, 1.0, t)) for e, t in zip(es, totals)]
    w_bs = [w.astype(BF16) for w in ws]
    outs = [dot(w_b, p[2], TN) for w_b, p in zip(w_bs, problems)]
    d_vs = [dot(w_b, p[3], NN) for w_b, p in zip(w_bs, problems)]
    dots = [jnp.sum(w * d_w, axis=0, keepdims=True) for w, d_w in zip(ws, d_ws)]
    d_ss = [(w * (d_w - o)).astype(BF16) for w, d_w, o in zip(ws, d_ws, dots)]
    d_qs = [dot(d_s, p[1], TN) for d_s, p in zip(d_ss, problems)]
    d_ks = [dot(d_s, p[0], NN) for d_s, p in zip(d_ss, problems)]
    return list(zip(outs, d_qs, d_ks, d_vs))


def to_column(row):
    n = row.shape[1]
    r = lax.broadcasted_iota(jnp.int32, (n, n), 0)
    c = lax.broadcasted_iota(jnp.int32, (n, n), 1)
    return jnp.sum(jnp.where(r == c, row, 0.0), axis=1, keepdims=True)


def transposed(x):
    n = x.shape[1]
    r = lax.broadcasted_iota(jnp.int32, (n, n), 0)
    c = lax.broadcasted_iota(jnp.int32, (n, n), 1)
    return dot((r == c).astype(F32).astype(BF16), x, NT)


def grouped(sizes):
    groups = []
    for axis in AXES:
        if groups and groups[-1][1] * sizes[axis] <= 32:
            groups[-1] = (groups[-1][0] + (axis,), groups[-1][1] * sizes[axis])
        else:
            groups.append(((axis,), sizes[axis]))
    return groups


def rounds(sizes):
    n, found, d = sizes["blk"] * sizes["inner"], [], 1
    while d < n:
        found.append(d)
        d *= 2
    return found


def kernel(cfg, q_hbm, k_hbm, v_hbm, s_hbm, g_hbm, qg_hbm, kg_hbm, seg_hbm,
           att_o, dq_o, dk_o, dv_o, gq_o, gk_o,
           qv, kv, vv, gv, s_ref, qg_ref, kg_ref, seg_ref, s_col, near, give, take, back,
           part_q, part_k, unit_q, unit_k, inv_q, inv_k, qn, kn, vd, kn_hi,
           bias_own, bias_edge, bias_hi, gsrc, gslot,
           load_sem, send_sem, recv_sem, back_sem, take_sem, here_sem, gsend, grecv):
    sizes, rows, heads, hd, h, hpc, own_hpc, late_hpc = cfg
    n_dp, n_blk, n_inner = (sizes[a] for a in AXES)
    nc = heads // hpc
    hh = h // 2
    width = hpc * hd
    scale = 1.0 / math.sqrt(hd)
    dp, blk, inner = (lax.axis_index(a) for a in AXES)
    p = blk * n_inner + inner
    n_line = n_blk * n_inner
    last = n_line - 1
    has_left, has_right = p > 0, p < last
    left, right = p - 1, p + 1
    first, final = inner == 0, inner == n_inner - 1
    ids = ({"blk": jnp.where(first, blk - 1, blk), "inner": jnp.where(first, n_inner - 1, inner - 1)},
           {"blk": jnp.where(final, blk + 1, blk), "inner": jnp.where(final, 0, inner + 1)})
    sides = ((0, has_left), (1, has_right))
    lo, hi = slice(0, hh), slice(rows - hh, rows)
    lo_in, hi_in = slice(hh, h), slice(rows - h, rows - hh)

    loads = [
        pltpu.make_async_copy(src, dst, load_sem.at[i])
        for i, (src, dst) in enumerate(((s_hbm, s_ref), (seg_hbm, seg_ref), (v_hbm, vv), (k_hbm, kv),
                                        (q_hbm, qv), (g_hbm, gv), (qg_hbm, qg_ref), (kg_hbm, kg_ref)))
    ]
    for c in loads:
        c.start()

    barrier = pltpu.get_barrier_semaphore()
    others = [jnp.where(dp + d >= n_dp, dp + d - n_dp, dp + d) for d in range(1, n_dp)]
    for side, there in sides:
        @pl.when(there)
        def _():
            pl.semaphore_signal(barrier, inc=1, device_id=ids[side], device_id_type=MESH)
    is_first = p == 0

    @pl.when(is_first)
    def _():
        for other in others:
            pl.semaphore_signal(barrier, inc=1, device_id={"dp": other}, device_id_type=MESH)

    dists = rounds(sizes)

    def say_here(i):
        if i > 0:
            d = dists[i - 1]
            pl.semaphore_wait(here_sem.at[i - 1], (p >= d).astype(jnp.int32) + (p + d <= last).astype(jnp.int32))
        if i < len(dists):
            for pos, there in ((p - dists[i], p >= dists[i]), (p + dists[i], p + dists[i] <= last)):
                @pl.when(there)
                def _():
                    pl.semaphore_signal(here_sem.at[i], inc=1, device_id_type=MESH,
                                        device_id={"blk": pos // n_inner, "inner": lax.rem(pos, n_inner)})
        else:
            @pl.when(is_first)
            def _():
                for other in others:
                    pl.semaphore_signal(here_sem.at[i], inc=1, device_id={"dp": other}, device_id_type=MESH)

    def say_all_here():
        @pl.when(is_first)
        def _():
            pl.semaphore_wait(here_sem.at[len(dists)], n_dp - 1)
            for pos in range(1, n_line):
                pl.semaphore_signal(here_sem.at[len(dists)], inc=1, device_id_type=MESH,
                                    device_id={"blk": pos // n_inner, "inner": pos % n_inner})

    loads[0].wait()
    s_f = transposed(s_ref[...])
    s_col[...] = s_f.astype(BF16)

    def seg_at(pos):
        start = pl.multiple_of(pos * rows, 128)
        return seg_ref[:, pl.ds(start, rows)].astype(F32)

    loads[1].wait()
    own = seg_at(p)
    prev = jnp.where(has_left, seg_at(jnp.maximum(left, 0)), -1.0)
    nxt = jnp.where(has_right, seg_at(jnp.minimum(right, last)), -2.0)

    def pick(row, index):
        return jnp.sum(row[:, index:index + 1], axis=1, keepdims=True)

    before, after = pick(prev, rows - 1), pick(nxt, 0)
    own_first, own_last = pick(own, 0), pick(own, rows - 1)
    long_lo = jnp.where(pick(own, hh) == before, 1.0, 0.0)
    long_hi = jnp.where(pick(own, rows - hh - 1) == after, 1.0, 0.0)
    short_lo = jnp.where(pick(prev, rows - hh - 1) == own_first, 1.0, 0.0)
    short_hi = jnp.where(pick(nxt, hh) == own_last, 1.0, 0.0)

    def over(x):
        return jnp.broadcast_to(x, (hh, hd)) > 0.5

    lo_is_long, hi_is_long = over(long_lo), over(long_hi)
    lo_is_short, hi_is_short = over(short_lo), over(short_hi)

    def columns(c):
        return pl.ds(pl.multiple_of(c * width, 128), width)

    def near_copy(side, c):
        cols = slice(c * width, (c + 1) * width)
        parts = slice(0, 2 + 2 * side)
        return pltpu.make_async_remote_copy(
            src_ref=give.at[side, parts, :, cols],
            dst_ref=near.at[1 - side, parts, :, cols],
            send_sem=send_sem.at[side],
            recv_sem=recv_sem.at[1 - side, c],
            device_id=ids[side],
            device_id_type=MESH,
        )

    def back_copy(side, c):
        return pltpu.make_async_remote_copy(
            src_ref=back.at[side, :, :, columns(c)],
            dst_ref=take.at[1 - side, :, :, columns(c)],
            send_sem=back_sem.at[side],
            recv_sem=take_sem.at[1 - side, c],
            device_id=ids[side],
            device_id_type=MESH,
        )

    def arrival(ref, send, recv, side):
        return pltpu.make_async_remote_copy(
            src_ref=ref, dst_ref=ref, send_sem=send, recv_sem=recv, device_id=ids[side], device_id_type=MESH)

    for c in loads[2:6]:
        c.wait()
    pl.semaphore_wait(barrier, has_left.astype(jnp.int32) + has_right.astype(jnp.int32)
                      + is_first.astype(jnp.int32) * (n_dp - 1))
    say_here(0)
    for c in range(nc):
        for head in range(c * hpc, (c + 1) * hpc):
            cols = slice(head * hd, (head + 1) * hd)
            for side, edge in ((0, lo), (1, hi)):
                give[side, 0, :, cols] = kv[edge, cols]
                give[side, 1, :, cols] = (vv[edge, cols].astype(F32) * s_f[edge, head:head + 1]).astype(BF16)
            give[1, 2, :, cols] = jnp.where(
                hi_is_long, kv[hi_in, cols].astype(F32), qv[hi, cols].astype(F32)).astype(BF16)
            give[1, 3, :, cols] = jnp.where(
                hi_is_long, vv[hi_in, cols].astype(F32) * s_f[hi_in, head:head + 1],
                gv[hi, cols].astype(F32)).astype(BF16)
        @pl.when(has_right)
        def _():
            near_copy(1, c).start()
    for c in range(nc):
        @pl.when(has_left)
        def _():
            near_copy(0, c).start()
    for side, there in sides:
        @pl.when(jnp.logical_not(there))
        def _():
            near[side] = jnp.zeros((4, hh, heads * hd), BF16)
            take[side] = jnp.zeros((2, hh, heads * hd), BF16)

    own_col, prev_col, nxt_col = to_column(own), to_column(prev), to_column(nxt)

    own_q = jnp.where((own == before) | (own == after), NO_QUERY, own)
    bias_own[...] = jnp.where(own_col == own_q, 0.0, OFF)

    split_lo, split_hi = own_first == before, own_last == after
    q_recv = jnp.where((prev[:, rows - hh:] == before) & split_lo & (short_lo < 0.5), prev[:, rows - hh:], NO_QUERY)
    q_lo = jnp.where(own[:, :h] == before, own[:, :h], NO_QUERY)
    q_hi = jnp.where((own[:, rows - h:] == after) & (short_hi < 0.5), own[:, rows - h:], NO_QUERY)
    k_far = jnp.where(short_lo > 0.5, prev_col[rows - h:rows - hh], NO_KEY)
    edge_q = jnp.concatenate([q_recv, q_lo, q_hi], axis=1)
    edge_k = jnp.concatenate(
        [k_far, prev_col[rows - hh:], own_col[:h], own_col[rows - h:], nxt_col[:hh]], axis=0)
    bias_edge[...] = jnp.where(edge_k == edge_q, 0.0, OFF)

    q_late = jnp.where(short_hi > 0.5, own[:, rows - hh:], nxt[:, :hh])
    q_late = jnp.where((q_late == after) & split_hi, q_late, NO_QUERY)
    k_late = jnp.where(short_hi > 0.5, nxt_col[hh:h], own_col[rows - h:rows - hh])
    hi_col = jnp.concatenate([own_col[rows - hh:], nxt_col[:hh], k_late], axis=0)
    bias_hi[...] = jnp.where(hi_col == q_late, 0.0, OFF)
    lo_far = jnp.broadcast_to(own_col[lo_in], (hh, hd)) == before
    lo_adds = over(jnp.where(own_col[:hh] == before, short_lo, 0.0))
    hi_adds = over(jnp.where(own_col[rows - hh:] == after, short_hi, 0.0))

    for c in loads[6:]:
        c.wait()
    q_gain, k_gain = qg_ref[...], kg_ref[...]
    which = lax.broadcasted_iota(jnp.int32, (heads, hd), 0)

    def scale_of(head, part):
        one = jnp.where(which == head, 1.0, 0.0).astype(BF16)
        return dot(s_col[part], one, NN)

    mid, hi_all = slice(h, rows - h), slice(rows - h, rows)
    hi_is_counted = jnp.broadcast_to(long_hi, (1, hd)) > 0.5

    def column_sum(x):
        return jnp.sum(x, axis=0, keepdims=True)

    def ends(x):
        return jnp.concatenate([x[:h], x[rows - h:]], axis=0)

    def columns_of(head):
        return pl.ds(pl.multiple_of(head * hd, 128), hd)

    def own_prepare(head):
        cols = columns_of(head)
        s_all = scale_of(head, slice(0, rows))
        v = (vv[:, cols].astype(F32) * s_all).astype(BF16)
        q_unit, q_inv = unit(qv[:, cols].astype(F32))
        k_unit, k_inv = unit(kv[:, cols].astype(F32))
        q_norm, k_norm = (q_unit * q_gain).astype(BF16), (k_unit * k_gain).astype(BF16)
        for ref, x in ((unit_q, q_unit), (unit_k, k_unit), (qn, q_norm), (kn, k_norm), (vd, v)):
            ref[:, cols] = ends(x)
        for ref, x in ((inv_q, q_inv), (inv_k, k_inv)):
            ref[:, cols] = jnp.broadcast_to(ends(x), (2 * h, hd))
        return (cols, s_all, q_unit, q_inv, k_unit, k_inv), (q_norm, k_norm, v, gv[:, cols], bias_own[...])

    def own_conclude(ready, result, acc):
        acc_q, acc_k = acc
        cols, s_all, q_unit, q_inv, k_unit, k_inv = ready
        out, d_q, d_k, d_v = result
        for ref, xs in ((part_q, (out, d_q)), (part_k, (d_k, d_v))):
            for i, x in enumerate(xs):
                ref[i, :, cols] = ends(x)
        if rows > 2 * h:
            att_o[mid, cols] = out[mid].astype(BF16)
            d_x, _ = norm_back(d_q[mid], q_unit[mid], q_inv[mid], q_gain, scale)
            dq_o[mid, cols] = d_x.astype(BF16)
            d_x, _ = norm_back(d_k[mid], k_unit[mid], k_inv[mid], k_gain, scale)
            dk_o[mid, cols] = d_x.astype(BF16)
            dv_o[mid, cols] = (d_v[mid] * s_all[mid]).astype(BF16)
        return acc_q + column_sum(d_q * q_unit), acc_k + column_sum(d_k * k_unit)

    n_own = heads // own_hpc

    def own_step(c, acc):
        prepared = [own_prepare(c * own_hpc + j) for j in range(own_hpc)]
        results = attend([x for _, x in prepared], scale)
        for (ready, _), result in zip(prepared, results):
            acc = own_conclude(ready, result, acc)
        for i in range(min(n_own, len(dists))):
            @pl.when(c == i)
            def _():
                say_here(i + 1)
        return acc

    zero = jnp.zeros((1, hd), F32)
    acc = lax.fori_loop(0, n_own, own_step, (zero, zero))

    def edge_prepare(head):
        cols = columns_of(head)
        near_u, _ = unit(jnp.concatenate([near[0, 0, :, cols], near[1, 0, :, cols]], axis=0).astype(F32))
        near_k = (near_u * k_gain).astype(BF16)
        far_u, _ = unit(near[0, 2, :, cols].astype(F32))
        kn_hi[:, cols] = near_k[hh:]
        k = jnp.concatenate([(far_u * k_gain).astype(BF16), near_k[:hh], kn[:, cols], near_k[hh:]], axis=0)
        v = jnp.concatenate([near[0, 3, :, cols], near[0, 1, :, cols], vd[:, cols], near[1, 1, :, cols]], axis=0)
        q = jnp.concatenate([(far_u * q_gain).astype(BF16), qn[:, cols]], axis=0)
        g = jnp.concatenate([near[0, 3, :, cols], gv[:h, cols], gv[hi_all, cols]], axis=0)
        return (cols, near_u, far_u), (q, k, v, g, bias_edge[...])

    def edge_conclude(ready, result, acc):
        acc_q, acc_k = acc
        cols, near_u, far_u = ready
        own_rows = slice(h, h + 2 * h)
        for i, (x, inward, edge) in enumerate(((result[2], kv[lo_in, cols], qv[lo, cols]),
                                               (result[3], vd[lo_in, cols], gv[lo, cols]))):
            back[0, i, :, cols] = jnp.where(
                lo_is_long, jnp.where(lo_far, inward.astype(F32), x[hh:h]), edge.astype(F32)).astype(BF16)
            back[1, i, :, cols] = x[3 * h:].astype(BF16)
            part_k[i, :, cols] += x[own_rows]
            part_q[i, :, cols] += result[i][hh:]
        d_q, d_k = result[1], result[2]
        along_q, along_k = d_q[hh:] * unit_q[:, cols], d_k[own_rows] * unit_k[:, cols]
        for_lo = (column_sum(d_q[:hh] * far_u) + column_sum(along_q[:h]),
                  column_sum(d_k[:hh] * far_u) + column_sum(d_k[hh:h] * near_u[:hh]) + column_sum(along_k[:h]))
        for_hi = (column_sum(along_q[h:]), column_sum(along_k[h:]) + column_sum(d_k[3 * h:] * near_u[hh:]))
        return tuple(a + x + jnp.where(hi_is_counted, y, 0.0) for a, x, y in zip(acc, for_lo, for_hi))

    rounds_at = list(range(nc))[:max(len(dists) - n_own, 0)]

    tell_at = len(rounds_at) if len(rounds_at) + n_own >= len(dists) and len(rounds_at) < nc else nc

    def edge_step(c, acc):
        for side, there in sides:
            @pl.when(there)
            def _():
                arrival(near.at[side, 0:4 - 2 * side, :, columns(c)], send_sem.at[side], recv_sem.at[side, c],
                        side).wait_recv()
        prepared = [edge_prepare(c * hpc + j) for j in range(hpc)]
        results = attend([x for _, x in prepared], scale)
        for (ready, _), result in zip(prepared, results):
            acc = edge_conclude(ready, result, acc)
        for i, at in enumerate(rounds_at):
            @pl.when(c == at)
            def _():
                say_here(n_own + i + 1)

        @pl.when(c == tell_at)
        def _():
            say_all_here()
        return acc

    acc_q, acc_k = lax.fori_loop(0, nc, edge_step, acc)
    for i in range(min(n_own, len(dists)) + len(rounds_at), len(dists)):
        say_here(i + 1)
    if tell_at == nc:
        say_all_here()

    @pl.when(jnp.logical_not(is_first))
    def _():
        pl.semaphore_wait(here_sem.at[len(dists)], 1)

    stages = grouped(sizes)
    me = {a: i for a, i in zip(AXES, (dp, blk, inner))}
    total = jnp.concatenate([acc_q, acc_k], axis=0) * scale

    def devices(stage):
        axes, n = stages[stage]
        for to in range(n):
            device, rest = {}, to
            for axis in reversed(axes):
                device[axis], rest = rest % sizes[axis], rest // sizes[axis]
            yield to, device

    def spread(stage, offset, total, between=None):
        axes, n = stages[stage]
        index = 0
        for axis in axes:
            index = index * sizes[axis] + me[axis]
        gsrc[stage] = total
        gslot[offset + index] = total
        order = sorted(devices(stage), key=lambda x: [x[1].get(a, 0) for a in ("blk", "inner", "dp")])
        for i, (to, device) in enumerate(order):
            if between is not None and i == n // 2:
                between()

            @pl.when(index != to)
            def _():
                pltpu.make_async_remote_copy(
                    src_ref=gsrc.at[stage], dst_ref=gslot.at[offset + index],
                    send_sem=gsend.at[stage], recv_sem=grecv.at[stage],
                    device_id=device, device_id_type=MESH).start()

    def gathered(stage, offset):
        axes, n = stages[stage]
        everything = gslot.at[pl.ds(offset, n - 1)]
        pltpu.make_async_remote_copy(
            src_ref=everything, dst_ref=everything,
            send_sem=gsend.at[stage], recv_sem=grecv.at[stage],
            device_id={axis: 0 for axis in axes}, device_id_type=MESH).wait()
        total = gslot[offset]
        for i in range(1, n):
            total = total + gslot[offset + i]
        return total

    def send_back():
        for c in range(nc):
            for side, there in sides:
                @pl.when(there)
                def _():
                    back_copy(side, c).start()

    spread(0, 0, total, send_back)

    q_done, k_done = slice(0, h + hh), slice(hh, h)

    def finish_step(c, carry):
        for j in range(late_hpc):
            head = c * late_hpc + j
            cols = columns_of(head)
            out = part_q[0, q_done, cols].astype(BF16)
            d_q = norm_back(part_q[1, q_done, cols], unit_q[q_done, cols], inv_q[q_done, cols], q_gain, scale)[0]
            d_q = d_q.astype(BF16)
            att_o[:h, cols], att_o[hi_in, cols] = out[:h], out[h:]
            dq_o[:h, cols], dq_o[hi_in, cols] = d_q[:h], d_q[h:]
            d_k = norm_back(part_k[0, k_done, cols], unit_k[k_done, cols], inv_k[k_done, cols], k_gain, scale)[0]
            dk_o[lo_in, cols] = d_k.astype(BF16)
            dv_o[lo_in, cols] = (part_k[1, k_done, cols] * scale_of(head, lo_in)).astype(BF16)
        return carry

    lax.fori_loop(0, heads // late_hpc, finish_step, 0)

    q_late, k_lo, k_hi = slice(h + hh, 2 * h), slice(0, hh), slice(h, 2 * h)

    def late_prepare(head):
        cols = columns_of(head)
        s_ends = jnp.concatenate([scale_of(head, lo), scale_of(head, hi_all)], axis=0)
        far_u, _ = unit(take[1, 0, :, cols].astype(F32))
        far_1 = take[1, 1, :, cols].astype(F32)
        q_e = (jnp.where(hi_is_short, unit_q[q_late, cols], far_u) * q_gain).astype(BF16)
        g_e = jnp.where(hi_is_short, gv[hi, cols].astype(F32), far_1).astype(BF16)
        k_x = (jnp.where(hi_is_short, far_u, unit_k[h:h + hh, cols]) * k_gain).astype(BF16)
        v_x = jnp.where(hi_is_short, far_1, vd[h:h + hh, cols].astype(F32)).astype(BF16)
        k_e = jnp.concatenate([kn[q_late, cols], kn_hi[:, cols], k_x], axis=0)
        v_e = jnp.concatenate([vd[q_late, cols], near[1, 1, :, cols], v_x], axis=0)
        return (cols, s_ends), (q_e, k_e, v_e, g_e, bias_hi[...])

    def late_conclude(ready, result):
        cols, s_ends = ready
        out, d_q, d_k, d_v = result

        def to_keys(i, e):
            from_lo, from_hi = take[0, i, :, cols].astype(F32), take[1, i, :, cols].astype(F32)
            return jnp.concatenate(
                [part_k[i, lo, cols] + jnp.where(lo_adds, from_lo, 0.0),
                 part_k[i, h:h + hh, cols] + jnp.where(hi_is_short, 0.0, e[h:]),
                 part_k[i, q_late, cols] + jnp.where(hi_is_short, jnp.where(hi_adds, from_hi, 0.0), e[:hh])], axis=0)

        def both(ref):
            return jnp.concatenate([ref[k_lo, cols], ref[k_hi, cols]], axis=0)

        att_o[hi, cols] = (part_q[0, q_late, cols] + jnp.where(hi_is_short, out, 0.0)).astype(BF16)
        d_q = part_q[1, q_late, cols] + jnp.where(hi_is_short, d_q, 0.0)
        dq_o[hi, cols] = norm_back(d_q, unit_q[q_late, cols], inv_q[q_late, cols], q_gain, scale)[0].astype(BF16)
        d_x = norm_back(to_keys(0, d_k), both(unit_k), both(inv_k), k_gain, scale)[0].astype(BF16)
        dk_o[lo, cols], dk_o[hi_all, cols] = d_x[lo], d_x[hh:]
        d_v = (to_keys(1, d_v) * s_ends).astype(BF16)
        dv_o[lo, cols], dv_o[hi_all, cols] = d_v[lo], d_v[hh:]

    def late_step(c, carry):
        for i in range(late_hpc // hpc):
            chunk = c * (late_hpc // hpc) + i
            for side, there in sides:
                @pl.when(there)
                def _():
                    arrival(take.at[side, :, :, columns(chunk)], back_sem.at[side], take_sem.at[side, chunk],
                            side).wait_recv()
        prepared = [late_prepare(c * late_hpc + j) for j in range(late_hpc)]
        results = attend([x for _, x in prepared], scale)
        for (ready, _), result in zip(prepared, results):
            late_conclude(ready, result)
        return carry

    lax.fori_loop(0, heads // late_hpc, late_step, 0)

    @pl.when(has_left)
    def _():
        arrival(near.at[1, 0:2], send_sem.at[0], recv_sem.at[1, 0], 0).wait_send()

    @pl.when(has_right)
    def _():
        arrival(near.at[0], send_sem.at[1], recv_sem.at[0, 0], 1).wait_send()
    for side, there in sides:
        @pl.when(there)
        def _():
            arrival(take.at[side], back_sem.at[side], take_sem.at[side, 0], side).wait_send()

    offset = 0
    for stage, (_, n) in enumerate(stages):
        if stage > 0:
            spread(stage, offset, total)
        total = gathered(stage, offset)
        offset += n
    gq_o[...] = total[0:1]
    gk_o[...] = total[1:2]


def store(*refs):
    n = len(refs) // 2
    sem = refs[-1]
    copies = [pltpu.make_async_copy(refs[i], refs[n + i], sem.at[i]) for i in range(n)]
    for x in copies:
        x.start()
    for x in copies:
        x.wait()


def local(queries, keys, values, v_scale, d_out, q_gain, k_gain, segment_ids):
    _, rows, cols = queries.shape
    hd = q_gain.shape[0]
    heads = cols // hd
    sizes = {a: lax.axis_size(a) for a in AXES}
    h = rows * sizes["inner"] // 8
    hpc = 4 if heads % 4 == 0 else 1
    nc = heads // hpc
    late_hpc = hpc
    own_hpc = 6 if heads % 6 == 0 else 1
    flat = lambda x: x.reshape(rows, x.shape[2])
    vmem = pl.BlockSpec(memory_space=pltpu.VMEM)
    hbm = pl.BlockSpec(memory_space=pltpu.HBM)
    in_hbm = lambda x: pltpu.with_memory_space_constraint(x, pltpu.HBM)
    in_vmem = lambda x: pltpu.with_memory_space_constraint(x, pltpu.VMEM)
    big = jax.ShapeDtypeStruct((rows, cols), BF16)
    small = jax.ShapeDtypeStruct((1, hd), F32)
    stages = grouped(sizes)
    outs = pl.pallas_call(
        functools.partial(kernel, (sizes, rows, heads, hd, h, hpc, own_hpc, late_hpc)),
        out_shape=(big, big, big, big, small, small),
        in_specs=[hbm] * 8,
        out_specs=(vmem,) * 6,
        scratch_shapes=[
            pltpu.VMEM((rows, cols), BF16),
            pltpu.VMEM((rows, cols), BF16),
            pltpu.VMEM((rows, cols), BF16),
            pltpu.VMEM((rows, cols), BF16),
            pltpu.VMEM((heads, rows), BF16),
            pltpu.VMEM((1, hd), F32),
            pltpu.VMEM((1, hd), F32),
            pltpu.VMEM(segment_ids.shape, jnp.int32),
            pltpu.VMEM((rows, heads), BF16),
            pltpu.VMEM((2, 4, h // 2, cols), BF16),
            pltpu.VMEM((2, 4, h // 2, cols), BF16),
            pltpu.VMEM((2, 2, h // 2, cols), BF16),
            pltpu.VMEM((2, 2, h // 2, cols), BF16),
            pltpu.VMEM((2, 2 * h, cols), F32),
            pltpu.VMEM((2, 2 * h, cols), F32),
            pltpu.VMEM((2 * h, cols), F32),
            pltpu.VMEM((2 * h, cols), F32),
            pltpu.VMEM((2 * h, cols), F32),
            pltpu.VMEM((2 * h, cols), F32),
            pltpu.VMEM((2 * h, cols), BF16),
            pltpu.VMEM((2 * h, cols), BF16),
            pltpu.VMEM((2 * h, cols), BF16),
            pltpu.VMEM((h // 2, cols), BF16),
            pltpu.VMEM((rows, rows), F32),
            pltpu.VMEM((7 * h // 2, 5 * h // 2), F32),
            pltpu.VMEM((3 * h // 2, h // 2), F32),
            pltpu.VMEM((len(stages), 2, hd), F32),
            pltpu.VMEM((sum(n for _, n in stages), 2, hd), F32),
            pltpu.SemaphoreType.DMA((8,)),
            pltpu.SemaphoreType.DMA((2,)),
            pltpu.SemaphoreType.DMA((2, nc)),
            pltpu.SemaphoreType.DMA((2,)),
            pltpu.SemaphoreType.DMA((2, nc)),
            pltpu.SemaphoreType.REGULAR((len(rounds(sizes)) + 1,)),
            pltpu.SemaphoreType.DMA((len(stages),)),
            pltpu.SemaphoreType.DMA((len(stages),)),
        ],
        compiler_params=pltpu.CompilerParams(
            collective_id=0, has_side_effects=True, vmem_limit_bytes=32 << 20),
    )(*map(in_hbm, (flat(queries), flat(keys), flat(values), flat(v_scale).T, flat(d_out),
                    q_gain.reshape(1, hd), k_gain.reshape(1, hd), segment_ids)))
    outs = pl.pallas_call(
        store,
        out_shape=(big, big, big, big, small, small),
        in_specs=[vmem] * 6,
        out_specs=(hbm,) * 6,
        scratch_shapes=[pltpu.SemaphoreType.DMA((6,))],
    )(*map(in_vmem, outs))
    wide = tuple(x.reshape(1, rows, cols) for x in outs[:4])
    return wide + (outs[4].reshape(hd), outs[5].reshape(hd))


def solution(mesh):
    tokens = P("dp", ("blk", "inner"), None)
    return jax.shard_map(
        local,
        mesh=mesh,
        in_specs=(tokens,) * 5 + (P(), P(), P("dp", None)),
        out_specs=(tokens,) * 4 + (P(), P()),
        check_vma=False,
    )
```

```python
import functools
import math

import jax
import jax.numpy as jnp
from jax import lax
from jax.experimental import pallas as pl
from jax.experimental.pallas import tpu as pltpu
from jax.sharding import PartitionSpec as P

EPSILON = 1e-06
MESH = pl.DeviceIdType.MESH
AXES = ("dp", "blk", "inner")
F32 = jnp.float32
BF16 = jnp.bfloat16
NT = (((1,), (1,)), ((), ()))
NN = (((1,), (0,)), ((), ()))
TN = (((0,), (0,)), ((), ()))
OFF = -1e30
NO_QUERY = -9.0
NO_KEY = -7.0


def dot(a, b, dims):
    return lax.dot_general(a, b, dims, preferred_element_type=F32)


def unit(x):
    inverse = lax.rsqrt(jnp.mean(x * x, axis=-1, keepdims=True) + EPSILON)
    return x * inverse, inverse


def norm_back(d_norm, unit_rows, inverse, gain, scale):
    along = d_norm * unit_rows
    mean = jnp.mean(along * gain, axis=-1, keepdims=True)
    return (inverse * scale) * (d_norm * gain - unit_rows * mean), along


def attend(problems, scale):
    factor = scale * math.log2(math.e)
    scores = [dot(k_norm, q_norm, NT) for q_norm, k_norm, _, _, _ in problems]
    d_ws = [dot(v, g, NT) for _, _, v, g, _ in problems]
    es = [jnp.exp2(s * factor + p[4]) for s, p in zip(scores, problems)]
    totals = [jnp.sum(e, axis=0, keepdims=True) for e in es]
    ws = [e * (1.0 / jnp.where(t == 0.0, 1.0, t)) for e, t in zip(es, totals)]
    w_bs = [w.astype(BF16) for w in ws]
    outs = [dot(w_b, p[2], TN) for w_b, p in zip(w_bs, problems)]
    d_vs = [dot(w_b, p[3], NN) for w_b, p in zip(w_bs, problems)]
    dots = [jnp.sum(w * d_w, axis=0, keepdims=True) for w, d_w in zip(ws, d_ws)]
    d_ss = [(w * (d_w - o)).astype(BF16) for w, d_w, o in zip(ws, d_ws, dots)]
    d_qs = [dot(d_s, p[1], TN) for d_s, p in zip(d_ss, problems)]
    d_ks = [dot(d_s, p[0], NN) for d_s, p in zip(d_ss, problems)]
    return list(zip(outs, d_qs, d_ks, d_vs))


def to_column(row):
    n = row.shape[1]
    r = lax.broadcasted_iota(jnp.int32, (n, n), 0)
    c = lax.broadcasted_iota(jnp.int32, (n, n), 1)
    return jnp.sum(jnp.where(r == c, row, 0.0), axis=1, keepdims=True)


def transposed(x):
    n = x.shape[1]
    r = lax.broadcasted_iota(jnp.int32, (n, n), 0)
    c = lax.broadcasted_iota(jnp.int32, (n, n), 1)
    return dot((r == c).astype(F32).astype(BF16), x, NT)


def grouped(sizes):
    groups = []
    for axis in AXES:
        if groups and groups[-1][1] * sizes[axis] <= 32:
            groups[-1] = (groups[-1][0] + (axis,), groups[-1][1] * sizes[axis])
        else:
            groups.append(((axis,), sizes[axis]))
    return groups


def rounds(sizes):
    n, found, d = sizes["blk"] * sizes["inner"], [], 1
    while d < n:
        found.append(d)
        d *= 2
    return found


def kernel(cfg, q_hbm, k_hbm, v_hbm, s_hbm, g_hbm, qg_hbm, kg_hbm, seg_hbm,
           att_o, dq_o, dk_o, dv_o, gq_o, gk_o,
           qv, kv, vv, gv, s_ref, qg_ref, kg_ref, seg_ref, s_col, near, give, take, back,
           part_q, part_k, unit_q, unit_k, inv_q, inv_k, qn, kn, vd, kn_hi,
           bias_own, bias_edge, bias_hi, gsrc, gslot,
           load_sem, send_sem, recv_sem, back_sem, take_sem, here_sem, gsend, grecv):
    sizes, rows, heads, hd, h, hpc, own_hpc, late_hpc = cfg
    n_dp, n_blk, n_inner = (sizes[a] for a in AXES)
    nc = heads // hpc
    hh = h // 2
    width = hpc * hd
    scale = 1.0 / math.sqrt(hd)
    dp, blk, inner = (lax.axis_index(a) for a in AXES)
    p = blk * n_inner + inner
    n_line = n_blk * n_inner
    last = n_line - 1
    has_left, has_right = p > 0, p < last
    left, right = p - 1, p + 1
    first, final = inner == 0, inner == n_inner - 1
    ids = ({"blk": jnp.where(first, blk - 1, blk), "inner": jnp.where(first, n_inner - 1, inner - 1)},
           {"blk": jnp.where(final, blk + 1, blk), "inner": jnp.where(final, 0, inner + 1)})
    sides = ((0, has_left), (1, has_right))
    lo, hi = slice(0, hh), slice(rows - hh, rows)
    lo_in, hi_in = slice(hh, h), slice(rows - h, rows - hh)

    loads = [
        pltpu.make_async_copy(src, dst, load_sem.at[i])
        for i, (src, dst) in enumerate(((s_hbm, s_ref), (seg_hbm, seg_ref), (v_hbm, vv), (k_hbm, kv),
                                        (q_hbm, qv), (g_hbm, gv), (qg_hbm, qg_ref), (kg_hbm, kg_ref)))
    ]
    barrier = pltpu.get_barrier_semaphore()
    others = [jnp.where(dp + d >= n_dp, dp + d - n_dp, dp + d) for d in range(1, n_dp)]
    for side, there in sides:
        @pl.when(there)
        def _():
            pl.semaphore_signal(barrier, inc=1, device_id=ids[side], device_id_type=MESH)
    for c in loads:
        c.start()
    for other in others:
        pl.semaphore_signal(barrier, inc=1, device_id={"dp": other}, device_id_type=MESH)

    dists = rounds(sizes)

    def say_here(i):
        if i > 0:
            d = dists[i - 1]
            pl.semaphore_wait(here_sem.at[i - 1], (p >= d).astype(jnp.int32) + (p + d <= last).astype(jnp.int32))
        if i < len(dists):
            for pos, there in ((p - dists[i], p >= dists[i]), (p + dists[i], p + dists[i] <= last)):
                @pl.when(there)
                def _():
                    pl.semaphore_signal(here_sem.at[i], inc=1, device_id_type=MESH,
                                        device_id={"blk": pos // n_inner, "inner": lax.rem(pos, n_inner)})
        else:
            for other in others:
                pl.semaphore_signal(here_sem.at[i], inc=1, device_id={"dp": other}, device_id_type=MESH)

    loads[0].wait()
    s_f = transposed(s_ref[...])
    s_col[...] = s_f.astype(BF16)

    def seg_at(pos):
        start = pl.multiple_of(pos * rows, 128)
        return seg_ref[:, pl.ds(start, rows)].astype(F32)

    loads[1].wait()
    own = seg_at(p)
    prev = jnp.where(has_left, seg_at(jnp.maximum(left, 0)), -1.0)
    nxt = jnp.where(has_right, seg_at(jnp.minimum(right, last)), -2.0)

    def pick(row, index):
        return jnp.sum(row[:, index:index + 1], axis=1, keepdims=True)

    before, after = pick(prev, rows - 1), pick(nxt, 0)
    own_first, own_last = pick(own, 0), pick(own, rows - 1)
    long_lo = jnp.where(pick(own, hh) == before, 1.0, 0.0)
    long_hi = jnp.where(pick(own, rows - hh - 1) == after, 1.0, 0.0)
    short_lo = jnp.where(pick(prev, rows - hh - 1) == own_first, 1.0, 0.0)
    short_hi = jnp.where(pick(nxt, hh) == own_last, 1.0, 0.0)

    def over(x):
        return jnp.broadcast_to(x, (hh, hd)) > 0.5

    lo_is_long, hi_is_long = over(long_lo), over(long_hi)
    lo_is_short, hi_is_short = over(short_lo), over(short_hi)

    def columns(c):
        return pl.ds(pl.multiple_of(c * width, 128), width)

    def near_copy(side, c):
        cols = slice(c * width, (c + 1) * width)
        parts = slice(0, 2 + 2 * side)
        return pltpu.make_async_remote_copy(
            src_ref=give.at[side, parts, :, cols],
            dst_ref=near.at[1 - side, parts, :, cols],
            send_sem=send_sem.at[side],
            recv_sem=recv_sem.at[1 - side, c],
            device_id=ids[side],
            device_id_type=MESH,
        )

    def back_copy(side, c):
        return pltpu.make_async_remote_copy(
            src_ref=back.at[side, :, :, columns(c)],
            dst_ref=take.at[1 - side, :, :, columns(c)],
            send_sem=back_sem.at[side],
            recv_sem=take_sem.at[1 - side, c],
            device_id=ids[side],
            device_id_type=MESH,
        )

    def arrival(ref, send, recv, side):
        return pltpu.make_async_remote_copy(
            src_ref=ref, dst_ref=ref, send_sem=send, recv_sem=recv, device_id=ids[side], device_id_type=MESH)

    for c in loads[2:6]:
        c.wait()
    pl.semaphore_wait(barrier, has_left.astype(jnp.int32) + has_right.astype(jnp.int32) + (n_dp - 1))
    say_here(0)
    for c in range(nc):
        for head in range(c * hpc, (c + 1) * hpc):
            cols = slice(head * hd, (head + 1) * hd)
            for side, edge in ((0, lo), (1, hi)):
                give[side, 0, :, cols] = kv[edge, cols]
                give[side, 1, :, cols] = (vv[edge, cols].astype(F32) * s_f[edge, head:head + 1]).astype(BF16)
            give[1, 2, :, cols] = jnp.where(
                hi_is_long, kv[hi_in, cols].astype(F32), qv[hi, cols].astype(F32)).astype(BF16)
            give[1, 3, :, cols] = jnp.where(
                hi_is_long, vv[hi_in, cols].astype(F32) * s_f[hi_in, head:head + 1],
                gv[hi, cols].astype(F32)).astype(BF16)
        for side, there in sides:
            @pl.when(there)
            def _():
                near_copy(side, c).start()
    for side, there in sides:
        @pl.when(jnp.logical_not(there))
        def _():
            near[side] = jnp.zeros((4, hh, heads * hd), BF16)
            take[side] = jnp.zeros((2, hh, heads * hd), BF16)

    own_col, prev_col, nxt_col = to_column(own), to_column(prev), to_column(nxt)

    own_q = jnp.where((own == before) | (own == after), NO_QUERY, own)
    bias_own[...] = jnp.where(own_col == own_q, 0.0, OFF)

    split_lo, split_hi = own_first == before, own_last == after
    q_recv = jnp.where((prev[:, rows - hh:] == before) & split_lo & (short_lo < 0.5), prev[:, rows - hh:], NO_QUERY)
    q_lo = jnp.where(own[:, :h] == before, own[:, :h], NO_QUERY)
    q_hi = jnp.where((own[:, rows - h:] == after) & (short_hi < 0.5), own[:, rows - h:], NO_QUERY)
    k_far = jnp.where(short_lo > 0.5, prev_col[rows - h:rows - hh], NO_KEY)
    edge_q = jnp.concatenate([q_recv, q_lo, q_hi], axis=1)
    edge_k = jnp.concatenate(
        [k_far, prev_col[rows - hh:], own_col[:h], own_col[rows - h:], nxt_col[:hh]], axis=0)
    bias_edge[...] = jnp.where(edge_k == edge_q, 0.0, OFF)

    q_late = jnp.where(short_hi > 0.5, own[:, rows - hh:], nxt[:, :hh])
    q_late = jnp.where((q_late == after) & split_hi, q_late, NO_QUERY)
    k_late = jnp.where(short_hi > 0.5, nxt_col[hh:h], own_col[rows - h:rows - hh])
    hi_col = jnp.concatenate([own_col[rows - hh:], nxt_col[:hh], k_late], axis=0)
    bias_hi[...] = jnp.where(hi_col == q_late, 0.0, OFF)
    lo_far = jnp.broadcast_to(own_col[lo_in], (hh, hd)) == before
    lo_adds = over(jnp.where(own_col[:hh] == before, short_lo, 0.0))
    hi_adds = over(jnp.where(own_col[rows - hh:] == after, short_hi, 0.0))

    for c in loads[6:]:
        c.wait()
    q_gain, k_gain = qg_ref[...], kg_ref[...]
    which = lax.broadcasted_iota(jnp.int32, (heads, hd), 0)

    def scale_of(head, part):
        one = jnp.where(which == head, 1.0, 0.0).astype(BF16)
        return dot(s_col[part], one, NN)

    mid, hi_all = slice(h, rows - h), slice(rows - h, rows)
    hi_is_counted = jnp.broadcast_to(long_hi, (1, hd)) > 0.5

    def column_sum(x):
        return jnp.sum(x, axis=0, keepdims=True)

    def ends(x):
        return jnp.concatenate([x[:h], x[rows - h:]], axis=0)

    def columns_of(head):
        return pl.ds(pl.multiple_of(head * hd, 128), hd)

    def own_prepare(head):
        cols = columns_of(head)
        s_all = scale_of(head, slice(0, rows))
        v = (vv[:, cols].astype(F32) * s_all).astype(BF16)
        q_unit, q_inv = unit(qv[:, cols].astype(F32))
        k_unit, k_inv = unit(kv[:, cols].astype(F32))
        q_norm, k_norm = (q_unit * q_gain).astype(BF16), (k_unit * k_gain).astype(BF16)
        for ref, x in ((unit_q, q_unit), (unit_k, k_unit), (qn, q_norm), (kn, k_norm), (vd, v)):
            ref[:, cols] = ends(x)
        for ref, x in ((inv_q, q_inv), (inv_k, k_inv)):
            ref[:, cols] = jnp.broadcast_to(ends(x), (2 * h, hd))
        return (cols, s_all, q_unit, q_inv, k_unit, k_inv), (q_norm, k_norm, v, gv[:, cols], bias_own[...])

    def own_conclude(ready, result, acc):
        acc_q, acc_k = acc
        cols, s_all, q_unit, q_inv, k_unit, k_inv = ready
        out, d_q, d_k, d_v = result
        for ref, xs in ((part_q, (out, d_q)), (part_k, (d_k, d_v))):
            for i, x in enumerate(xs):
                ref[i, :, cols] = ends(x)
        if rows > 2 * h:
            att_o[mid, cols] = out[mid].astype(BF16)
            d_x, _ = norm_back(d_q[mid], q_unit[mid], q_inv[mid], q_gain, scale)
            dq_o[mid, cols] = d_x.astype(BF16)
            d_x, _ = norm_back(d_k[mid], k_unit[mid], k_inv[mid], k_gain, scale)
            dk_o[mid, cols] = d_x.astype(BF16)
            dv_o[mid, cols] = (d_v[mid] * s_all[mid]).astype(BF16)
        return acc_q + column_sum(d_q * q_unit), acc_k + column_sum(d_k * k_unit)

    n_own = heads // own_hpc

    def own_step(c, acc):
        prepared = [own_prepare(c * own_hpc + j) for j in range(own_hpc)]
        results = attend([x for _, x in prepared], scale)
        for (ready, _), result in zip(prepared, results):
            acc = own_conclude(ready, result, acc)
        for i in range(min(n_own, len(dists))):
            @pl.when(c == i)
            def _():
                say_here(i + 1)
        return acc

    zero = jnp.zeros((1, hd), F32)
    acc = lax.fori_loop(0, n_own, own_step, (zero, zero))

    def edge_prepare(head):
        cols = columns_of(head)
        near_u, _ = unit(jnp.concatenate([near[0, 0, :, cols], near[1, 0, :, cols]], axis=0).astype(F32))
        near_k = (near_u * k_gain).astype(BF16)
        far_u, _ = unit(near[0, 2, :, cols].astype(F32))
        kn_hi[:, cols] = near_k[hh:]
        k = jnp.concatenate([(far_u * k_gain).astype(BF16), near_k[:hh], kn[:, cols], near_k[hh:]], axis=0)
        v = jnp.concatenate([near[0, 3, :, cols], near[0, 1, :, cols], vd[:, cols], near[1, 1, :, cols]], axis=0)
        q = jnp.concatenate([(far_u * q_gain).astype(BF16), qn[:, cols]], axis=0)
        g = jnp.concatenate([near[0, 3, :, cols], gv[:h, cols], gv[hi_all, cols]], axis=0)
        return (cols, near_u, far_u), (q, k, v, g, bias_edge[...])

    def edge_conclude(ready, result, acc):
        acc_q, acc_k = acc
        cols, near_u, far_u = ready
        own_rows = slice(h, h + 2 * h)
        for i, (x, inward, edge) in enumerate(((result[2], kv[lo_in, cols], qv[lo, cols]),
                                               (result[3], vd[lo_in, cols], gv[lo, cols]))):
            back[0, i, :, cols] = jnp.where(
                lo_is_long, jnp.where(lo_far, inward.astype(F32), x[hh:h]), edge.astype(F32)).astype(BF16)
            back[1, i, :, cols] = x[3 * h:].astype(BF16)
            part_k[i, :, cols] += x[own_rows]
            part_q[i, :, cols] += result[i][hh:]
        d_q, d_k = result[1], result[2]
        along_q, along_k = d_q[hh:] * unit_q[:, cols], d_k[own_rows] * unit_k[:, cols]
        for_lo = (column_sum(d_q[:hh] * far_u) + column_sum(along_q[:h]),
                  column_sum(d_k[:hh] * far_u) + column_sum(d_k[hh:h] * near_u[:hh]) + column_sum(along_k[:h]))
        for_hi = (column_sum(along_q[h:]), column_sum(along_k[h:]) + column_sum(d_k[3 * h:] * near_u[hh:]))
        return tuple(a + x + jnp.where(hi_is_counted, y, 0.0) for a, x, y in zip(acc, for_lo, for_hi))

    rounds_at = list(range(nc))[:max(len(dists) - n_own, 0)]

    def edge_step(c, acc):
        for side, there in sides:
            @pl.when(there)
            def _():
                arrival(near.at[side, 0:4 - 2 * side, :, columns(c)], send_sem.at[side], recv_sem.at[side, c],
                        side).wait_recv()
        prepared = [edge_prepare(c * hpc + j) for j in range(hpc)]
        results = attend([x for _, x in prepared], scale)
        for (ready, _), result in zip(prepared, results):
            acc = edge_conclude(ready, result, acc)
        for i, at in enumerate(rounds_at):
            @pl.when(c == at)
            def _():
                say_here(n_own + i + 1)
        return acc

    acc_q, acc_k = lax.fori_loop(0, nc, edge_step, acc)
    for i in range(min(n_own, len(dists)) + len(rounds_at), len(dists)):
        say_here(i + 1)
    pl.semaphore_wait(here_sem.at[len(dists)], n_dp - 1)

    stages = grouped(sizes)
    me = {a: i for a, i in zip(AXES, (dp, blk, inner))}
    total = jnp.concatenate([acc_q, acc_k], axis=0) * scale

    def devices(stage):
        axes, n = stages[stage]
        for to in range(n):
            device, rest = {}, to
            for axis in reversed(axes):
                device[axis], rest = rest % sizes[axis], rest // sizes[axis]
            yield to, device

    def spread(stage, offset, total, between=None):
        axes, n = stages[stage]
        index = 0
        for axis in axes:
            index = index * sizes[axis] + me[axis]
        gsrc[stage] = total
        gslot[offset + index] = total
        order = sorted(devices(stage), key=lambda x: [x[1].get(a, 0) for a in ("blk", "inner", "dp")])
        for i, (to, device) in enumerate(order):
            if between is not None and i == n // 2:
                between()

            @pl.when(index != to)
            def _():
                pltpu.make_async_remote_copy(
                    src_ref=gsrc.at[stage], dst_ref=gslot.at[offset + index],
                    send_sem=gsend.at[stage], recv_sem=grecv.at[stage],
                    device_id=device, device_id_type=MESH).start()

    def gathered(stage, offset):
        axes, n = stages[stage]
        everything = gslot.at[pl.ds(offset, n - 1)]
        pltpu.make_async_remote_copy(
            src_ref=everything, dst_ref=everything,
            send_sem=gsend.at[stage], recv_sem=grecv.at[stage],
            device_id={axis: 0 for axis in axes}, device_id_type=MESH).wait()
        total = gslot[offset]
        for i in range(1, n):
            total = total + gslot[offset + i]
        return total

    def send_back():
        for c in range(nc):
            for side, there in sides:
                @pl.when(there)
                def _():
                    back_copy(side, c).start()

    spread(0, 0, total, send_back)

    q_done, k_done = slice(0, h + hh), slice(hh, h)

    def finish_step(c, carry):
        for j in range(late_hpc):
            head = c * late_hpc + j
            cols = columns_of(head)
            out = part_q[0, q_done, cols].astype(BF16)
            d_q = norm_back(part_q[1, q_done, cols], unit_q[q_done, cols], inv_q[q_done, cols], q_gain, scale)[0]
            d_q = d_q.astype(BF16)
            att_o[:h, cols], att_o[hi_in, cols] = out[:h], out[h:]
            dq_o[:h, cols], dq_o[hi_in, cols] = d_q[:h], d_q[h:]
            d_k = norm_back(part_k[0, k_done, cols], unit_k[k_done, cols], inv_k[k_done, cols], k_gain, scale)[0]
            dk_o[lo_in, cols] = d_k.astype(BF16)
            dv_o[lo_in, cols] = (part_k[1, k_done, cols] * scale_of(head, lo_in)).astype(BF16)
        return carry

    lax.fori_loop(0, heads // late_hpc, finish_step, 0)

    q_late, k_lo, k_hi = slice(h + hh, 2 * h), slice(0, hh), slice(h, 2 * h)

    def late_prepare(head):
        cols = columns_of(head)
        s_ends = jnp.concatenate([scale_of(head, lo), scale_of(head, hi_all)], axis=0)
        far_u, _ = unit(take[1, 0, :, cols].astype(F32))
        far_1 = take[1, 1, :, cols].astype(F32)
        q_e = (jnp.where(hi_is_short, unit_q[q_late, cols], far_u) * q_gain).astype(BF16)
        g_e = jnp.where(hi_is_short, gv[hi, cols].astype(F32), far_1).astype(BF16)
        k_x = (jnp.where(hi_is_short, far_u, unit_k[h:h + hh, cols]) * k_gain).astype(BF16)
        v_x = jnp.where(hi_is_short, far_1, vd[h:h + hh, cols].astype(F32)).astype(BF16)
        k_e = jnp.concatenate([kn[q_late, cols], kn_hi[:, cols], k_x], axis=0)
        v_e = jnp.concatenate([vd[q_late, cols], near[1, 1, :, cols], v_x], axis=0)
        return (cols, s_ends), (q_e, k_e, v_e, g_e, bias_hi[...])

    def late_conclude(ready, result):
        cols, s_ends = ready
        out, d_q, d_k, d_v = result

        def to_keys(i, e):
            from_lo, from_hi = take[0, i, :, cols].astype(F32), take[1, i, :, cols].astype(F32)
            return jnp.concatenate(
                [part_k[i, lo, cols] + jnp.where(lo_adds, from_lo, 0.0),
                 part_k[i, h:h + hh, cols] + jnp.where(hi_is_short, 0.0, e[h:]),
                 part_k[i, q_late, cols] + jnp.where(hi_is_short, jnp.where(hi_adds, from_hi, 0.0), e[:hh])], axis=0)

        def both(ref):
            return jnp.concatenate([ref[k_lo, cols], ref[k_hi, cols]], axis=0)

        att_o[hi, cols] = (part_q[0, q_late, cols] + jnp.where(hi_is_short, out, 0.0)).astype(BF16)
        d_q = part_q[1, q_late, cols] + jnp.where(hi_is_short, d_q, 0.0)
        dq_o[hi, cols] = norm_back(d_q, unit_q[q_late, cols], inv_q[q_late, cols], q_gain, scale)[0].astype(BF16)
        d_x = norm_back(to_keys(0, d_k), both(unit_k), both(inv_k), k_gain, scale)[0].astype(BF16)
        dk_o[lo, cols], dk_o[hi_all, cols] = d_x[lo], d_x[hh:]
        d_v = (to_keys(1, d_v) * s_ends).astype(BF16)
        dv_o[lo, cols], dv_o[hi_all, cols] = d_v[lo], d_v[hh:]

    def late_step(c, carry):
        for i in range(late_hpc // hpc):
            chunk = c * (late_hpc // hpc) + i
            for side, there in sides:
                @pl.when(there)
                def _():
                    arrival(take.at[side, :, :, columns(chunk)], back_sem.at[side], take_sem.at[side, chunk],
                            side).wait_recv()
        prepared = [late_prepare(c * late_hpc + j) for j in range(late_hpc)]
        results = attend([x for _, x in prepared], scale)
        for (ready, _), result in zip(prepared, results):
            late_conclude(ready, result)
        return carry

    lax.fori_loop(0, heads // late_hpc, late_step, 0)

    @pl.when(has_left)
    def _():
        arrival(near.at[1, 0:2], send_sem.at[0], recv_sem.at[1, 0], 0).wait_send()

    @pl.when(has_right)
    def _():
        arrival(near.at[0], send_sem.at[1], recv_sem.at[0, 0], 1).wait_send()
    for side, there in sides:
        @pl.when(there)
        def _():
            arrival(take.at[side], back_sem.at[side], take_sem.at[side, 0], side).wait_send()

    offset = 0
    for stage, (_, n) in enumerate(stages):
        if stage > 0:
            spread(stage, offset, total)
        total = gathered(stage, offset)
        offset += n
    gq_o[...] = total[0:1]
    gk_o[...] = total[1:2]


def store(*refs):
    n = len(refs) // 2
    sem = refs[-1]
    copies = [pltpu.make_async_copy(refs[i], refs[n + i], sem.at[i]) for i in range(n)]
    for x in copies:
        x.start()
    for x in copies:
        x.wait()


def local(queries, keys, values, v_scale, d_out, q_gain, k_gain, segment_ids):
    _, rows, cols = queries.shape
    hd = q_gain.shape[0]
    heads = cols // hd
    sizes = {a: lax.axis_size(a) for a in AXES}
    h = rows * sizes["inner"] // 8
    hpc = 4 if heads % 4 == 0 else 1
    nc = heads // hpc
    late_hpc = hpc
    own_hpc = 6 if heads % 6 == 0 else 1
    flat = lambda x: x.reshape(rows, x.shape[2])
    vmem = pl.BlockSpec(memory_space=pltpu.VMEM)
    hbm = pl.BlockSpec(memory_space=pltpu.HBM)
    in_hbm = lambda x: pltpu.with_memory_space_constraint(x, pltpu.HBM)
    in_vmem = lambda x: pltpu.with_memory_space_constraint(x, pltpu.VMEM)
    big = jax.ShapeDtypeStruct((rows, cols), BF16)
    small = jax.ShapeDtypeStruct((1, hd), F32)
    stages = grouped(sizes)
    outs = pl.pallas_call(
        functools.partial(kernel, (sizes, rows, heads, hd, h, hpc, own_hpc, late_hpc)),
        out_shape=(big, big, big, big, small, small),
        in_specs=[hbm] * 8,
        out_specs=(vmem,) * 6,
        scratch_shapes=[
            pltpu.VMEM((rows, cols), BF16),
            pltpu.VMEM((rows, cols), BF16),
            pltpu.VMEM((rows, cols), BF16),
            pltpu.VMEM((rows, cols), BF16),
            pltpu.VMEM((heads, rows), BF16),
            pltpu.VMEM((1, hd), F32),
            pltpu.VMEM((1, hd), F32),
            pltpu.VMEM(segment_ids.shape, jnp.int32),
            pltpu.VMEM((rows, heads), BF16),
            pltpu.VMEM((2, 4, h // 2, cols), BF16),
            pltpu.VMEM((2, 4, h // 2, cols), BF16),
            pltpu.VMEM((2, 2, h // 2, cols), BF16),
            pltpu.VMEM((2, 2, h // 2, cols), BF16),
            pltpu.VMEM((2, 2 * h, cols), F32),
            pltpu.VMEM((2, 2 * h, cols), F32),
            pltpu.VMEM((2 * h, cols), F32),
            pltpu.VMEM((2 * h, cols), F32),
            pltpu.VMEM((2 * h, cols), F32),
            pltpu.VMEM((2 * h, cols), F32),
            pltpu.VMEM((2 * h, cols), BF16),
            pltpu.VMEM((2 * h, cols), BF16),
            pltpu.VMEM((2 * h, cols), BF16),
            pltpu.VMEM((h // 2, cols), BF16),
            pltpu.VMEM((rows, rows), F32),
            pltpu.VMEM((7 * h // 2, 5 * h // 2), F32),
            pltpu.VMEM((3 * h // 2, h // 2), F32),
            pltpu.VMEM((len(stages), 2, hd), F32),
            pltpu.VMEM((sum(n for _, n in stages), 2, hd), F32),
            pltpu.SemaphoreType.DMA((8,)),
            pltpu.SemaphoreType.DMA((2,)),
            pltpu.SemaphoreType.DMA((2, nc)),
            pltpu.SemaphoreType.DMA((2,)),
            pltpu.SemaphoreType.DMA((2, nc)),
            pltpu.SemaphoreType.REGULAR((len(rounds(sizes)) + 1,)),
            pltpu.SemaphoreType.DMA((len(stages),)),
            pltpu.SemaphoreType.DMA((len(stages),)),
        ],
        compiler_params=pltpu.CompilerParams(
            collective_id=0, has_side_effects=True, vmem_limit_bytes=32 << 20),
    )(*map(in_hbm, (flat(queries), flat(keys), flat(values), flat(v_scale).T, flat(d_out),
                    q_gain.reshape(1, hd), k_gain.reshape(1, hd), segment_ids)))
    outs = pl.pallas_call(
        store,
        out_shape=(big, big, big, big, small, small),
        in_specs=[vmem] * 6,
        out_specs=(hbm,) * 6,
        scratch_shapes=[pltpu.SemaphoreType.DMA((6,))],
    )(*map(in_vmem, outs))
    wide = tuple(x.reshape(1, rows, cols) for x in outs[:4])
    return wide + (outs[4].reshape(hd), outs[5].reshape(hd))


def solution(mesh):
    tokens = P("dp", ("blk", "inner"), None)
    return jax.shard_map(
        local,
        mesh=mesh,
        in_specs=(tokens,) * 5 + (P(), P(), P("dp", None)),
        out_specs=(tokens,) * 4 + (P(), P()),
        check_vma=False,
    )
```
